128 devices in a mesh: section: 4 (over x_hi, core), dp: 32 (over y, z, x_lo).
Axes of the slice: x: 4 (x_hi: 2, x_lo: 2; x = x_hi * 2 + x_lo), y: 4, z: 4, core: 2. Of those that a mesh axis runs over, the one named last changes fastest.
Arguments:
- inputs: bfloat16 [2, 32, 128, 1024], P(None, 'dp'), may hold values from -6 to 6
- cotangent: bfloat16 [2, 32, 128, 1024], P(None, 'dp'), may hold values from -6 to 6
- lengths: int32 [2, 32], P(None, 'dp'), may hold values from 32 to 128, as said below
- attn_gain: float32 [4096], P(('section', 'dp')), may hold values from 0.25 to 1.75
- w_query: float32 [4096, 1024], P(('section', 'dp')), may hold values from -0.1875 to 0.1875
- w_key: float32 [4096, 128], P(('section', 'dp')), may hold values from -0.1875 to 0.1875
- w_value: float32 [4096, 128], P(('section', 'dp')), may hold values from -0.1875 to 0.1875
- w_out: float32 [4096, 1024], P(('section', 'dp')), may hold values from -0.75 to 0.75
- ffn_gain: float32 [4096], P(('section', 'dp')), may hold values from 0.25 to 1.75
- w_up: float32 [4096, 4096], P(('section', 'dp')), may hold values from -0.1875 to 0.1875
- w_down: float32 [16384, 1024], P(('section', 'dp')), may hold values from -0.09375 to 0.09375
Outputs:
- final: bfloat16 [2, 32, 128, 1024], P(None, 'dp', 'section')
- input_grad: bfloat16 [2, 32, 128, 1024], P(None, 'dp', 'section')
- grad_attn_gain: float32 [4096], P(('section', 'dp'))
- grad_query: float32 [4096, 1024], P(('section', 'dp'))
- grad_key: float32 [4096, 128], P(('section', 'dp'))
- grad_value: float32 [4096, 128], P(('section', 'dp'))
- grad_out: float32 [4096, 1024], P(('section', 'dp'))
- grad_ffn_gain: float32 [4096], P(('section', 'dp'))
- grad_up: float32 [4096, 4096], P(('section', 'dp'))
- grad_down: float32 [16384, 1024], P(('section', 'dp'))
The draws below stay inside these ranges and needn't reach their ends.
Inputs may be any that keep to these rules, and one draw needn't show every extreme that they name: `lengths`: some sequence is exactly 128 tokens long.
All inputs are finite; a program needn't handle non-finite values.
Results may differ from the reference program's by a relative error of at most 0.035.
Values may be sent and summed in bfloat16 or wider, within the bound.
A program may use at most 832 MiB of HBM per device.

```python
import jax
import jax.numpy as jnp
from jax import lax

D = 1024
HD = 128
FF = 4096
SEQ = 128
MICRO = 2
LAYERS = 4
SEQS = 64
N_DP = 32


def draw_lengths(key, part):
    key_draw, key_pick = jax.random.split(key)
    count_all = SEQS
    flat_values = jax.random.randint(key_draw, (count_all,), SEQ // 4, SEQ + 1)
    longest = jax.random.randint(key_pick, (), 0, count_all)
    flat_values = jnp.where(jnp.arange(count_all) == longest, SEQ, flat_values)
    return flat_values.reshape(MICRO, count_all // MICRO).astype(jnp.int32)


def shard_levels(key, extent, cuts, least, high):
    def one(position, shards_of):
        steps = jax.random.uniform(jax.random.fold_in(jax.random.fold_in(key, 6), position), (shards_of,), jnp.float32, least / len(cuts), high / len(cuts))
        return jnp.repeat(jnp.exp(steps), extent[position] // shards_of).reshape((-1,) + (1,) * (len(extent) - position - 1))

    gain = one(*cuts[0])
    for cut in cuts[1:]:
        gain = gain * one(*cut)
    return gain


def scatter_about(key, extent, spread, most, cuts=(), held_as=jnp.bfloat16):
    entries = jax.random.normal(key, extent, jnp.float32) * spread
    if len(cuts) > 0:
        entries = shard_levels(key, extent, cuts, -0.22, 0.18) * entries
    return jnp.clip(entries, min=-most, max=most).astype(held_as)


def setup_inputs(seed: int = 0) -> dict:
    splits = jax.random.split(jax.random.key(seed), 12)
    return {
        "inputs": scatter_about(splits[0], (MICRO, N_DP, SEQ, D), 1.0, 6.0, ((1, 32),)),
        "cotangent": scatter_about(splits[1], (MICRO, N_DP, SEQ, D), 1.0, 6.0, ((1, 32),)),
        "lengths": draw_lengths(jax.random.fold_in(splits[11], 71), 0),
        "attn_gain": jnp.clip(1.0 + 0.15 * jax.random.normal(splits[3], (LAYERS * D,), jnp.float32), 0.25, 1.75),
        "w_query": scatter_about(splits[4], (LAYERS * D, D), D ** -0.5, 0.1875, ((0, 128),), jnp.float32),
        "w_key": scatter_about(splits[5], (LAYERS * D, HD), D ** -0.5, 0.1875, ((0, 128),), jnp.float32),
        "w_value": scatter_about(splits[6], (LAYERS * D, HD), D ** -0.5, 0.1875, ((0, 128),), jnp.float32),
        "w_out": scatter_about(splits[7], (LAYERS * D, D), (D // 16) ** -0.5, 0.75, ((0, 128),), jnp.float32),
        "ffn_gain": jnp.clip(1.0 + 0.15 * jax.random.normal(splits[8], (LAYERS * D,), jnp.float32), 0.25, 1.75),
        "w_up": scatter_about(splits[9], (LAYERS * D, FF), D ** -0.5, 0.1875, ((0, 128),), jnp.float32),
        "w_down": scatter_about(splits[10], (LAYERS * FF, D), FF ** -0.5, 0.09375, ((0, 128),), jnp.float32),
    }


NORM_EPS = 1e-06
NEG_FILL = -1000000000.0
HIGHEST_PREC = lax.Precision.HIGHEST

@jax.custom_vjp
def low(v):
    return lax.optimization_barrier(v.astype(jnp.bfloat16)).astype(jnp.float32)

@jax.custom_vjp
def low_back(v):
    return v

def low_keep(v):
    return (low(v), None)

def low_pass(kept, grad):
    return (grad,)

def back_keep(v):
    return (v, None)

def back_low(kept, grad):
    return (low(grad),)
low.defvjp(low_keep, low_pass)
low_back.defvjp(back_keep, back_low)

def matmul_high(left_side, right_side):
    return jnp.einsum('btk,kn->btn', left_side, right_side, precision=HIGHEST_PREC)

def rms_scale(values):
    return values * lax.rsqrt(lax.optimization_barrier(jnp.mean(values * values, axis=-1, keepdims=True)) + NORM_EPS)

def decoder_layer(hidden, lengths_now, params):
    attn_gain, w_query, w_key, w_value, w_out, ffn_gain, w_up, w_down = params
    hidden = low_back(hidden)
    seq_len = hidden.shape[1]
    positions = jnp.arange(seq_len)
    pad_mask = (positions[None, :] < lengths_now[:, None]).astype(jnp.float32)[:, :, None]
    attn_in = low(rms_scale(hidden) * attn_gain)
    queries = low_back(low(matmul_high(attn_in, w_query)))
    keys_all = low_back(low(matmul_high(attn_in, w_key)))
    values_all = low_back(low(matmul_high(attn_in, w_value)))
    head_count = w_query.shape[1] // HD
    query_heads = queries.reshape(queries.shape[0], seq_len, head_count, HD)
    scores = jnp.einsum('bthd,bsd->bhts', query_heads, keys_all, precision=HIGHEST_PREC) * HD ** (-0.5)
    scores = low_back(scores)
    causal = positions[None, :] <= positions[:, None]
    allowed = causal[None, None, :, :] & (positions[None, None, None, :] < lengths_now[:, None, None, None])
    scores = jnp.where(allowed, scores, NEG_FILL)
    row_max = lax.optimization_barrier(jnp.max(scores, axis=-1, keepdims=True))
    exp_scores = jnp.exp(scores - row_max)
    attn_probs = exp_scores / lax.optimization_barrier(jnp.sum(exp_scores, axis=-1, keepdims=True))
    mixed_heads = jnp.einsum('bhts,bsd->bthd', low(attn_probs), values_all, precision=HIGHEST_PREC)
    mixed_heads = low_back(low(mixed_heads.reshape(hidden.shape)))
    attn_out = low_back(matmul_high(mixed_heads, w_out))
    after_attn = hidden + pad_mask * attn_out
    ffn_in = low(rms_scale(after_attn) * ffn_gain)
    pre_act = low_back(matmul_high(ffn_in, w_up))
    act_out = low(jax.nn.silu(pre_act))
    ffn_out = low_back(matmul_high(act_out, w_down))
    return low(after_attn + pad_mask * ffn_out)

def reference(inputs, cotangent, lengths, attn_gain, w_query, w_key, w_value, w_out, ffn_gain, w_up, w_down):
    masters = (attn_gain, w_query, w_key, w_value, w_out, ffn_gain, w_up, w_down)

    def forward(params, start_rows, lengths_now):
        used = [low(master) for master in params]
        layered = (used[0].reshape(LAYERS, D), used[1].reshape(LAYERS, D, D), used[2].reshape(LAYERS, D, HD), used[3].reshape(LAYERS, D, HD), used[4].reshape(LAYERS, D, D), used[5].reshape(LAYERS, D), used[6].reshape(LAYERS, D, FF), used[7].reshape(LAYERS, FF, D))
        hidden = start_rows
        for layer_idx in range(LAYERS):
            hidden = decoder_layer(hidden, lengths_now, tuple((member[layer_idx] for member in layered)))
        return hidden

    def one_micro(totals, micro_batch):
        start_rows, grad_rows, lengths_now = micro_batch

        def apply_net(params, first_rows):
            return forward(params, first_rows, lengths_now)
        result, pullback = jax.vjp(apply_net, masters, start_rows.astype(jnp.float32))
        param_grads, start_grad = pullback(grad_rows.astype(jnp.float32))
        totals = tuple((total + term for total, term in zip(totals, param_grads)))
        return (totals, (result.astype(jnp.bfloat16), start_grad.astype(jnp.bfloat16)))
    zero_grads = tuple((jnp.zeros(master.shape, jnp.float32) for master in masters))
    totals, outputs = lax.scan(one_micro, zero_grads, (inputs, cotangent, lengths))
    final, input_grad = outputs
    return (final, input_grad, totals[0], totals[1], totals[2], totals[3], totals[4], totals[5], totals[6], totals[7])
```

```python
import functools

import jax
import jax.numpy as jnp
from jax import lax
from jax.experimental import pallas as pl
from jax.experimental.pallas import tpu as pltpu
from jax.sharding import PartitionSpec as P

D = 1024
HEADS = 8
HD = 128
FF = 4096
LAYERS = 4
SEQ = 128
MICRO = 2
NORM_EPS = 1e-06
NEG_FILL = -1000000000.0
W1 = D + 2 * HD + HD + D
BF = jnp.bfloat16
F32 = jnp.float32
MESH = pl.DeviceIdType.MESH


class Role:
    def __init__(self):
        section = lax.axis_index("section")
        dp = lax.axis_index("dp")
        self.c = section % 2
        self.x_lo = dp % 2
        self.x = (section // 2) * 2 + self.x_lo
        self.z = (dp // 2) % 4
        self.y = dp // 8
        self.native = self.c == self.x_lo

    def dev(self, x, y, z, c):
        return ((x // 2) * 2 + c, (y * 4 + z) * 2 + x % 2)

    def along(self, axis, step):
        if axis == 0:
            return self.dev(self.x, (self.y + step + 4) % 4, self.z, self.c)
        return self.dev(self.x, self.y, (self.z + step + 4) % 4, self.c)

    def partner(self):
        return self.dev(self.x, self.y, self.z, 1 - self.c)

    def swap(self):
        return self.dev(self.x + 1 - 2 * self.x_lo, self.y, self.z, 1 - self.c)


def remote(src, dst, sems, device):
    return pltpu.make_async_remote_copy(
        src_ref=src, dst_ref=dst, send_sem=sems[0], recv_sem=sems[1], device_id=device, device_id_type=MESH
    )


def greet(devices):
    barrier = pltpu.get_barrier_semaphore()
    for device in devices:
        pl.semaphore_signal(barrier, inc=1, device_id=device, device_id_type=MESH)
    pl.semaphore_wait(barrier, len(devices))


N_GATHER = 12


def gather_chunks(shards, fulls):
    chunks = []
    for which, cuts in ((0, 1), (1, 2), (2, 2)):
        wide = shards[which].shape[-1] // cuts
        for cut in range(cuts):
            chunks.append((shards[which], fulls[which], cut * wide, wide))
    return chunks


def gather_kernel(s1, s2, s3, act, f1, f2, f3, act_out, send, recv, swap_send, swap_recv, local):
    role = Role()
    y, z, c = role.y, role.z, role.c
    place = (y, z)
    greet([role.along(0, 1), role.along(0, -1), role.along(1, 1), role.along(1, -1), role.partner(), role.swap()])
    chunks = gather_chunks((s1, s2, s3), (f1, f2, f3))
    count = len(chunks)

    def moved(step):
        shard, full, start, wide = chunks[step]
        return shard.at[:, :, pl.ds(start, wide)], full

    def own_copies(step, owner):
        src, full = moved(step)
        start, wide = chunks[step][2:]
        return (
            remote(src, full.at[y, z, owner, :, :, pl.ds(start, wide)], (swap_send.at[step], swap_recv.at[step]), role.swap()),
            pltpu.make_async_copy(src, full.at[y, z, owner, :, :, pl.ds(start, wide)], local.at[step]),
        )

    act_far = remote(act, act_out, (swap_send.at[count], swap_recv.at[count]), role.swap())
    act_near = pltpu.make_async_copy(act, act_out, local.at[count])

    @pl.when(role.native)
    def _():
        for step in range(count):
            own_copies(step, c)[1].start()
        act_near.start()

    @pl.when(jnp.logical_not(role.native))
    def _():
        for step in range(count):
            own_copies(step, 1 - c)[0].start()
        act_far.start()

    def piece(step, half, first, second, cols=None):
        full, start, wide = chunks[step][1:]
        if cols is not None:
            near = (wide // HD + 1) // 2 * HD
            start, wide = (start, near) if cols[0] == 0 else (start + near, wide - near)
        index = (first, second) if half == 0 else (second, first)
        return full.at[index[0], index[1], c, half, :, pl.ds(start, wide)]

    def hop(step, half, number, view, device):
        at = (step * 2 + half) * N_GATHER + number
        return remote(view, view, (send.at[at], recv.at[at]), device)

    def copies(step, half):
        one, two = half, 1 - half
        p, s = place[one], place[two]
        nxt, prv, opp = (p + 1) % 4, (p + 3) % 4, (p + 2) % 4
        snx, spv, sop = (s + 1) % 4, (s + 3) % 4, (s + 2) % 4
        up1, down1 = role.along(one, 1), role.along(one, -1)
        up2, down2 = role.along(two, 1), role.along(two, -1)
        every = slice(None)
        low, high = pl.ds(0, 2), pl.ds(2, 2)
        sends = [
            hop(step, half, 0, piece(step, half, p, s), up1),
            hop(step, half, 1, piece(step, half, p, s), down1),
            hop(step, half, 2, piece(step, half, prv, s, (0,)), up1),
            hop(step, half, 3, piece(step, half, nxt, s, (1,)), down1),
            hop(step, half, 4, piece(step, half, every, s), up2),
            hop(step, half, 5, piece(step, half, every, s), down2),
            hop(step, half, 6, piece(step, half, low, spv), up2),
            hop(step, half, 7, piece(step, half, high, snx), down2),
            hop(step, half, 8, piece(step, half, every, s), role.partner()),
            hop(step, half, 9, piece(step, half, every, spv), role.partner()),
            hop(step, half, 10, piece(step, half, every, snx), role.partner()),
            hop(step, half, 11, piece(step, half, every, sop), role.partner()),
        ]
        return sends

    def start(step, half, numbers):
        made = copies(step, half)
        for number in numbers:
            made[number].start()

    def landed(step, half, numbers):
        made = copies(step, half)
        for number in numbers:
            made[number].wait_recv()

    def stage(step, level):
        if level == 0:
            @pl.when(role.native)
            def _():
                own_copies(step, c)[1].wait()

            @pl.when(jnp.logical_not(role.native))
            def _():
                own_copies(step, 1 - c)[0].wait()

            for half in (0, 1):
                start(step, half, (0, 1))
        elif level == 1:
            for half in (0, 1):
                landed(step, half, (0, 1))
                start(step, half, (2, 3))
        elif level == 2:
            for half in (0, 1):
                landed(step, half, (2, 3))
                start(step, half, (4, 5, 8))
        elif level == 3:
            for half in (0, 1):
                landed(step, half, (4, 5))
                start(step, half, (6, 7, 9, 10))
        elif level == 4:
            for half in (0, 1):
                landed(step, half, (6, 7))
                start(step, half, (11,))

    for tick in range(count + 4):
        for level in range(5):
            step = tick - level
            if 0 <= step < count:
                stage(step, level)
    for step in range(count):
        for half in (0, 1):
            made = copies(step, half)
            for number in (8, 9, 10, 11):
                made[number].wait_recv()
            for number in range(N_GATHER):
                made[number].wait_send()

    @pl.when(role.native)
    def _():
        act_near.wait()

    @pl.when(jnp.logical_not(role.native))
    def _():
        act_far.wait()


def gather(s1, s2, s3, act):
    steps = 5
    hops = steps * 2 * N_GATHER
    hbm = pl.BlockSpec(memory_space=pl.ANY)
    return pl.pallas_call(
        gather_kernel,
        out_shape=[
            jax.ShapeDtypeStruct((4, 4, 2) + s1.shape, BF),
            jax.ShapeDtypeStruct((4, 4, 2) + s2.shape, BF),
            jax.ShapeDtypeStruct((4, 4, 2) + s3.shape, BF),
            jax.ShapeDtypeStruct(act.shape, BF),
        ],
        in_specs=[hbm] * 4,
        out_specs=[hbm] * 4,
        scratch_shapes=[
            pltpu.SemaphoreType.DMA((hops,)),
            pltpu.SemaphoreType.DMA((hops,)),
            pltpu.SemaphoreType.DMA((steps + 1,)),
            pltpu.SemaphoreType.DMA((steps + 1,)),
            pltpu.SemaphoreType.DMA((steps + 1,)),
        ],
        compiler_params=pltpu.CompilerParams(collective_id=0, has_side_effects=True),
        name="gather_weights",
    )(s1, s2, s3, act)


N_SCATTER = 9


def scatter_kernel(
    g1, g2, g3, fin, ing,
    o1, o2, o3, fin_out, ing_out,
    l1, l2, l3, r1, r2, r3, a1, a2, a3, b1, b2, b3, c1, c2, c3, d1, d2, d3, w1, w2, w3,
    send, recv, swap_send, swap_recv, local, row_send, row_recv, row_local,
):
    role = Role()
    x, y, z, c = role.x, role.y, role.z, role.c
    place = (y, z)
    row = []
    for away in range(4):
        for other in range(2):
            if (away, other) != (0, 0):
                row.append(role.dev((x + away) % 4, y, z, (c + other) % 2))
    greet([role.along(0, 1), role.along(0, -1), role.along(1, 1), role.along(1, -1)] + row)

    rows = SEQ // LAYERS
    home = (fin, ing)
    away_out = (fin_out, ing_out)
    source_x = (3, 0)

    def row_copies(which):
        made = []
        for section in range(LAYERS):
            target_x, target_c = 2 * (section // 2) + c, section % 2
            src = home[which].at[:, pl.ds(section * rows, rows)]
            at = which * LAYERS + section
            self_here = jnp.logical_and(target_x == source_x[which], target_c == c)
            far = remote(src, away_out[which], (row_send.at[at], row_recv.at[which]), role.dev(target_x, y, z, target_c))
            near = pltpu.make_async_copy(src, away_out[which], row_local.at[which])
            made.append((self_here, far, near))
        return made

    def row_start(which):
        @pl.when(x == source_x[which])
        def _():
            for self_here, far, near in row_copies(which):
                @pl.when(self_here)
                def _():
                    near.start()

                @pl.when(jnp.logical_not(self_here))
                def _():
                    far.start()

    def row_finish(which):
        kept = jnp.logical_and(x == source_x[which], role.x_lo == c)
        kept = jnp.logical_and(kept, (x // 2) * 2 + c == x)

        @pl.when(x == source_x[which])
        def _():
            for self_here, far, near in row_copies(which):
                @pl.when(self_here)
                def _():
                    near.wait()

                @pl.when(jnp.logical_not(self_here))
                def _():
                    far.wait_send()

        @pl.when(jnp.logical_not(kept))
        def _():
            row_copies(which)[0][1].wait_recv()

    row_start(0)
    row_start(1)

    grads, outs = (g1, g2, g3), (o1, o2, o3)
    mine, theirs = (l1, l2, l3), (r1, r2, r3)
    bufs_a, bufs_b, bufs_c, bufs_d, bufs_w = (a1, a2, a3), (b1, b2, b3), (c1, c2, c3), (d1, d2, d3), (w1, w2, w3)
    chunks = []
    for which, cuts in ((2, 2), (1, 2), (0, 1)):
        wide = grads[which].shape[-1] // cuts
        for cut in range(cuts):
            chunks.append((which, cut * wide, wide))
    count = len(chunks)

    def core_copies(step):
        which, start, wide = chunks[step]
        cols = pl.ds(start, wide)
        at = step * 2 * N_SCATTER
        return (
            remote(grads[which].at[:, :, 1 - c, :, :, cols], theirs[which].at[:, :, :, :, cols], (send.at[at], recv.at[at]), role.partner()),
            pltpu.make_async_copy(grads[which].at[:, :, c, :, :, cols], mine[which].at[:, :, :, :, cols], local.at[step]),
        )

    for step in range(count):
        for copy in core_copies(step):
            copy.start()

    def near_far(step, part):
        start, wide = chunks[step][1:]
        near = (wide // HD + 1) // 2 * HD
        return pl.ds(start, near) if part == 0 else pl.ds(start + near, wide - near)

    def piece(step, half, first, second, part=None):
        which, start, wide = chunks[step]
        index = (first, second) if half == 0 else (second, first)
        cols = pl.ds(start, wide) if part is None else near_far(step, part)
        return mine[which].at[index[0], index[1], half, :, cols]

    def copies(step, half):
        which, start, wide = chunks[step]
        cols = pl.ds(start, wide)
        one, two = half, 1 - half
        p, s = place[one], place[two]
        nxt, prv, opp = (p + 1) % 4, (p + 3) % 4, (p + 2) % 4
        snx, spv, sop = (s + 1) % 4, (s + 3) % 4, (s + 2) % 4
        up1, down1 = role.along(one, 1), role.along(one, -1)
        up2, down2 = role.along(two, 1), role.along(two, -1)
        every, low, high = slice(None), pl.ds(0, 2), pl.ds(2, 2)
        a, b, cc, d = bufs_a[which], bufs_b[which], bufs_c[which], bufs_d[which]

        def hop(number, src, dst, device):
            at = (step * 2 + half) * N_SCATTER + 1 + number
            return remote(src, dst, (send.at[at], recv.at[at]), device)

        return [
            hop(0, piece(step, half, opp, low), a.at[half, 0, :, :, cols], up1),
            hop(1, piece(step, half, opp, high), a.at[half, 1, :, :, cols], down1),
            hop(2, piece(step, half, nxt, every), b.at[half, 0, :, :, cols], up1),
            hop(3, piece(step, half, prv, every), b.at[half, 1, :, :, cols], down1),
            hop(4, piece(step, half, p, sop, 0), cc.at[half, 0, :, near_far(step, 0)], up2),
            hop(5, piece(step, half, p, sop, 1), cc.at[half, 1, :, near_far(step, 1)], down2),
            hop(6, piece(step, half, p, snx), d.at[half, 0, :, cols], up2),
            hop(7, piece(step, half, p, spv), d.at[half, 1, :, cols], down2),
        ]

    def stage(step, level):
        which, start, wide = chunks[step]
        cols = pl.ds(start, wide)
        a, b, cc, d = bufs_a[which], bufs_b[which], bufs_c[which], bufs_d[which]
        if level == 0:
            far, near = core_copies(step)
            far.wait_recv()
            near.wait()
            mine_view, theirs_view = mine[which], theirs[which]

            @pl.loop(0, 16)
            def _(at):
                index = (at // 4, at % 4, slice(None), slice(None), cols)
                mine_view[index] = mine_view[index] + theirs_view[index]

        for half in (0, 1):
            made = copies(step, half)
            one, two = half, 1 - half
            p, s = place[one], place[two]
            nxt, prv = (p + 1) % 4, (p + 3) % 4
            snx, spv = (s + 1) % 4, (s + 3) % 4
            if level == 0:
                made[0].start()
                made[1].start()
            elif level == 1:
                made[0].wait_recv()
                made[1].wait_recv()
                for i in range(2):
                    up = piece(step, half, nxt, i)
                    up[...] = up[...] + a[half, 0, i, :, cols]
                    down = piece(step, half, prv, 2 + i)
                    down[...] = down[...] + a[half, 1, i, :, cols]
                made[2].start()
                made[3].start()
            elif level == 2:
                made[2].wait_recv()
                made[3].wait_recv()
                for i in range(4):
                    here = piece(step, half, p, i)
                    total = here[...].astype(F32) + b[half, 0, i, :, cols].astype(F32) + b[half, 1, i, :, cols].astype(F32)
                    here[...] = total.astype(BF)
                made[4].start()
                made[5].start()
            elif level == 3:
                made[4].wait_recv()
                made[5].wait_recv()
                up = piece(step, half, p, snx, 0)
                up[...] = up[...] + cc[half, 0, :, near_far(step, 0)]
                down = piece(step, half, p, spv, 1)
                down[...] = down[...] + cc[half, 1, :, near_far(step, 1)]
                made[6].start()
                made[7].start()
            elif level == 4:
                made[6].wait_recv()
                made[7].wait_recv()
                total = (
                    piece(step, half, p, s)[...].astype(F32)
                    + d[half, 0, :, cols].astype(F32)
                    + d[half, 1, :, cols].astype(F32)
                )

                @pl.when(role.native)
                def _():
                    outs[which][half, :, cols] = total

                @pl.when(jnp.logical_not(role.native))
                def _():
                    piece(step, half, p, s)[...] = total.astype(BF)
                    swapped(step, half).start()

    def swapped(step, half):
        which, start, wide = chunks[step]
        return remote(
            piece(step, half, y if half == 0 else z, z if half == 0 else y),
            bufs_w[which].at[half, :, pl.ds(start, wide)],
            (swap_send.at[step * 2 + half], swap_recv.at[step * 2 + half]),
            role.swap(),
        )

    for tick in range(count + 4):
        for level in range(4, -1, -1):
            step = tick - level
            if 0 <= step < count:
                stage(step, level)

    @pl.when(jnp.logical_not(role.native))
    def _():
        for step in range(count):
            which, start, wide = chunks[step]
            for half in (0, 1):
                swapped(step, half).wait()
                outs[which][half, :, pl.ds(start, wide)] = bufs_w[which][half, :, pl.ds(start, wide)].astype(F32)

    for step in range(count):
        core_copies(step)[0].wait_send()
        for half in (0, 1):
            for copy in copies(step, half):
                copy.wait_send()
    row_finish(0)
    row_finish(1)


def scatter(g1, g2, g3, fin, ing):
    steps = 5
    hops = steps * 2 * N_SCATTER
    hbm = pl.BlockSpec(memory_space=pl.ANY)
    vmem = pl.BlockSpec(memory_space=pltpu.VMEM)
    tails = [g.shape[4:] for g in (g1, g2, g3)]
    heads = ((4, 4, 2), (4, 4, 2), (2, 2, 2), (2, 2, 4), (2, 2), (2, 2), (2,))
    scratch = [pltpu.VMEM(head + tail, BF) for head in heads for tail in tails]
    rows = SEQ // LAYERS
    return pl.pallas_call(
        scatter_kernel,
        out_shape=[jax.ShapeDtypeStruct((2,) + tail, F32) for tail in tails]
        + [jax.ShapeDtypeStruct((MICRO, rows, D), BF)] * 2,
        in_specs=[hbm] * 5,
        out_specs=[vmem] * 3 + [hbm] * 2,
        scratch_shapes=scratch
        + [
            pltpu.SemaphoreType.DMA((hops,)),
            pltpu.SemaphoreType.DMA((hops,)),
            pltpu.SemaphoreType.DMA((steps * 2,)),
            pltpu.SemaphoreType.DMA((steps * 2,)),
            pltpu.SemaphoreType.DMA((steps,)),
            pltpu.SemaphoreType.DMA((2 * LAYERS,)),
            pltpu.SemaphoreType.DMA((2,)),
            pltpu.SemaphoreType.DMA((2,)),
        ],
        compiler_params=pltpu.CompilerParams(collective_id=1, has_side_effects=True, vmem_limit_bytes=60 << 20),
        name="scatter_gradients",
    )(g1, g2, g3, fin, ing)


def plain_dot(left, right):
    return jnp.dot(left, right, preferred_element_type=F32)


def contract_rows(left, right):
    return lax.dot_general(left, right, (((0,), (0,)), ((), ())), preferred_element_type=F32)


def times_transpose(left, right):
    return lax.dot_general(left, right, (((1,), (1,)), ((), ())), preferred_element_type=F32)


def rms_parts(values):
    factor = lax.rsqrt(jnp.mean(values * values, axis=-1, keepdims=True) + NORM_EPS)
    return values * factor, factor


def norm_back(grad_normed, normed, factor):
    return factor * (grad_normed - normed * jnp.mean(grad_normed * normed, axis=-1, keepdims=True))


def split_weights(fulls):
    first, second, third = fulls
    first = first.reshape(D, W1)
    gains = first[:, D + 2 * HD : D + 2 * HD + 2].astype(F32)
    return (
        gains[:, 0],
        first[:, :D],
        first[:, D : D + HD],
        first[:, D + HD : D + 2 * HD],
        first[:, W1 - D :],
        gains[:, 1],
        second.reshape(D, FF),
        third.reshape(FF, D),
    )


def attention_scores(queries, keys_all, lengths):
    positions = jnp.arange(SEQ)
    allowed = (positions[None, None, :] <= positions[None, :, None]) & (positions[None, None, :] < lengths[:, None, None])
    scores = jnp.einsum("bthd,bsd->bhts", queries, keys_all, preferred_element_type=F32) * HD ** (-0.5)
    scores = jnp.where(allowed[:, None], scores, NEG_FILL)
    shifted = jnp.exp(scores - jnp.max(scores, axis=-1, keepdims=True))
    return shifted / jnp.sum(shifted, axis=-1, keepdims=True)


def layer_forward(hidden_in, lengths, params):
    attn_gain, w_query, w_key, w_value, w_out, ffn_gain, w_up, w_down = params
    tokens = MICRO * SEQ
    hidden = hidden_in.astype(F32)
    pad_mask = (jnp.arange(SEQ)[None, :] < lengths[:, None]).astype(F32).reshape(tokens, 1)
    normed_a, _ = rms_parts(hidden)
    attn_in = (normed_a * attn_gain).astype(BF)
    queries = plain_dot(attn_in, w_query).astype(BF)
    keys_all = plain_dot(attn_in, w_key).astype(BF)
    values_all = plain_dot(attn_in, w_value).astype(BF)
    probs = attention_scores(
        queries.reshape(MICRO, SEQ, HEADS, HD), keys_all.reshape(MICRO, SEQ, HD), lengths
    )
    mixed = jnp.einsum("bhts,bsd->bthd", probs.astype(BF), values_all.reshape(MICRO, SEQ, HD), preferred_element_type=F32)
    mixed = mixed.reshape(tokens, D).astype(BF)
    after = hidden + pad_mask * plain_dot(mixed, w_out)
    normed_f, _ = rms_parts(after)
    ffn_in = (normed_f * ffn_gain).astype(BF)
    pre_act = plain_dot(ffn_in, w_up)
    act_out = jax.nn.silu(pre_act).astype(BF)
    result = (after + pad_mask * plain_dot(act_out, w_down)).astype(BF)
    return result, (hidden_in, attn_in, queries, keys_all, values_all, probs, mixed, after, ffn_in, pre_act, act_out)


def layer_backward(kept, grad_in, lengths, params):
    attn_gain, w_query, w_key, w_value, w_out, ffn_gain, w_up, w_down = params
    hidden_in, attn_in, queries, keys_all, values_all, probs, mixed, after, ffn_in, pre_act, act_out = kept
    tokens = MICRO * SEQ
    scale = HD ** (-0.5)
    pad_mask = (jnp.arange(SEQ)[None, :] < lengths[:, None]).astype(F32).reshape(tokens, 1)
    normed_a, factor_a = rms_parts(hidden_in.astype(F32))
    normed_f, factor_f = rms_parts(after)
    grad_out = grad_in.astype(F32)
    grad_ffn = (grad_out * pad_mask).astype(BF)
    g_down = contract_rows(act_out, grad_ffn)
    grad_act = times_transpose(grad_ffn, w_down)
    sigmoid = jax.nn.sigmoid(pre_act)
    grad_pre = (grad_act * sigmoid * (1.0 + pre_act * (1.0 - sigmoid))).astype(BF)
    g_up = contract_rows(ffn_in, grad_pre)
    grad_ffn_in = times_transpose(grad_pre, w_up)
    g_ffn_gain = jnp.sum(grad_ffn_in * normed_f, axis=0)
    grad_after = grad_out + norm_back(grad_ffn_in * ffn_gain, normed_f, factor_f)
    grad_attn = (grad_after * pad_mask).astype(BF)
    g_out = contract_rows(mixed, grad_attn)
    grad_mixed = times_transpose(grad_attn, w_out).astype(BF).reshape(MICRO, SEQ, HEADS, HD)
    keys_b, values_b = keys_all.reshape(MICRO, SEQ, HD), values_all.reshape(MICRO, SEQ, HD)
    queries_b = queries.reshape(MICRO, SEQ, HEADS, HD)
    grad_probs = jnp.einsum("bthd,bsd->bhts", grad_mixed, values_b, preferred_element_type=F32)
    grad_values = jnp.einsum("bhts,bthd->bsd", probs.astype(BF), grad_mixed, preferred_element_type=F32).astype(BF)
    grad_scores = (probs * (grad_probs - jnp.sum(probs * grad_probs, axis=-1, keepdims=True))).astype(BF)
    grad_queries = (jnp.einsum("bhts,bsd->bthd", grad_scores, keys_b, preferred_element_type=F32) * scale).astype(BF)
    grad_keys = (jnp.einsum("bhts,bthd->bsd", grad_scores, queries_b, preferred_element_type=F32) * scale).astype(BF)
    grad_queries = grad_queries.reshape(tokens, D)
    grad_keys, grad_values = grad_keys.reshape(tokens, HD), grad_values.reshape(tokens, HD)
    g_query = contract_rows(attn_in, grad_queries)
    g_key = contract_rows(attn_in, grad_keys)
    g_value = contract_rows(attn_in, grad_values)
    grad_attn_in = (
        times_transpose(grad_queries, w_query)
        + times_transpose(grad_keys, w_key)
        + times_transpose(grad_values, w_value)
    )
    g_attn_gain = jnp.sum(grad_attn_in * normed_a, axis=0)
    grad_hidden = grad_after + norm_back(grad_attn_in * attn_gain, normed_a, factor_a)
    gains = jnp.pad(jnp.stack([g_attn_gain, g_ffn_gain], axis=1), ((0, 0), (0, HD - 2)))
    first = jnp.concatenate([g_query, g_key, g_value, gains, g_out], axis=1).astype(BF)
    shaped = (
        first.reshape(4, 4, 2, 2, 16, W1),
        g_up.astype(BF).reshape(4, 4, 2, 2, 16, FF),
        g_down.astype(BF).reshape(4, 4, 2, 2, 64, D),
    )
    return grad_hidden.astype(BF), shaped


def relay(value, distance):
    route = []
    for x in range(4):
        for yz in range(16):
            for c in range(2):
                if 0 <= x + distance < 4:
                    there = x + distance
                    route.append((((x // 2) * 2 + c) * 32 + yz * 2 + x % 2, ((there // 2) * 2 + c) * 32 + yz * 2 + there % 2))
    return lax.ppermute(value, ("section", "dp"), route)


def body(
    inputs, cotangent, lengths, attn_gain, w_query, w_key, w_value, w_out, ffn_gain, w_up, w_down
):
    role = Role()
    tokens = MICRO * SEQ
    gains = jnp.pad(jnp.stack([attn_gain, ffn_gain], axis=1), ((0, 0), (0, HD - 2)))
    first = jnp.concatenate([w_query, w_key, w_value, gains, w_out], axis=1).astype(BF).reshape(2, 16, W1)
    second = w_up.astype(BF).reshape(2, 16, FF)
    third = w_down.astype(BF).reshape(2, 64, D)
    rows = jnp.where(role.x < 2, inputs[:, 0], cotangent[:, 0])
    lengths_rows = jnp.broadcast_to(lengths.astype(BF)[:, :, None], (MICRO, 16, D))
    act = jnp.concatenate([rows, lengths_rows], axis=1)
    f1, f2, f3, act = gather(first, second, third, act)
    start_rows = act[:, :SEQ].reshape(tokens, D)
    lengths_here = act[:, SEQ, 0].astype(jnp.int32)
    params = split_weights((f1, f2, f3))

    hidden = start_rows
    kept = None
    for tick in range(LAYERS):
        def run(operands):
            return layer_forward(operands, lengths_here, params)

        shapes = jax.eval_shape(run, hidden)
        if kept is None:
            kept = jax.tree.map(lambda a: jnp.zeros(a.shape, a.dtype), shapes[1])
        hidden_out, kept = lax.cond(
            role.x == tick, lambda ops: layer_forward(ops[0], lengths_here, params), lambda ops: ops, (hidden, kept)
        )
        hidden = relay(hidden_out, 1) if tick < LAYERS - 1 else hidden_out
    final_full = hidden

    grad = start_rows
    shaped = None
    for tick in range(LAYERS - 1, -1, -1):
        if shaped is None:
            shaped = (
                jnp.zeros((4, 4, 2, 2, 16, W1), BF),
                jnp.zeros((4, 4, 2, 2, 16, FF), BF),
                jnp.zeros((4, 4, 2, 2, 64, D), BF),
            )
        grad, shaped = lax.cond(
            role.x == tick,
            lambda ops: layer_backward(kept, ops[0], lengths_here, params),
            lambda ops: ops,
            (grad, shaped),
        )
        if tick > 0:
            grad = relay(grad, -1)
    o1, o2, o3, final_rows, input_rows = scatter(
        *shaped, final_full.reshape(MICRO, SEQ, D), grad.reshape(MICRO, SEQ, D)
    )
    o1 = o1.reshape(32, W1)
    return (
        final_rows[:, None],
        input_rows[:, None],
        o1[:, D + 2 * HD],
        o1[:, :D],
        o1[:, D : D + HD],
        o1[:, D + HD : D + 2 * HD],
        o1[:, W1 - D :],
        o1[:, D + 2 * HD + 1],
        o2.reshape(32, FF),
        o3.reshape(128, D),
    )


def solution(mesh):
    both = P(("section", "dp"))
    both_rows = P(("section", "dp"), None)
    acts = P(None, "dp", None, None)
    outs = P(None, "dp", "section", None)
    weights = (both, both_rows, both_rows, both_rows, both_rows, both, both_rows, both_rows)
    return jax.shard_map(
        body,
        mesh=mesh,
        in_specs=(acts, acts, P(None, "dp")) + weights,
        out_specs=(outs, outs) + weights,
        check_vma=False,
    )
```

```python
import functools

import jax
import jax.numpy as jnp
from jax import lax
from jax.experimental import pallas as pl
from jax.experimental.pallas import tpu as pltpu
from jax.sharding import PartitionSpec as P

D = 1024
HEADS = 8
HD = 128
FF = 4096
LAYERS = 4
SEQ = 128
MICRO = 2
NORM_EPS = 1e-06
NEG_FILL = -1000000000.0
W1 = D + 2 * HD + HD + D
BF = jnp.bfloat16
F32 = jnp.float32
MESH = pl.DeviceIdType.MESH


class Role:
    def __init__(self):
        section = lax.axis_index("section")
        dp = lax.axis_index("dp")
        self.c = section % 2
        self.x_lo = dp % 2
        self.x = (section // 2) * 2 + self.x_lo
        self.z = (dp // 2) % 4
        self.y = dp // 8
        self.native = self.c == self.x_lo

    def dev(self, x, y, z, c):
        return ((x // 2) * 2 + c, (y * 4 + z) * 2 + x % 2)

    def along(self, axis, step):
        if axis == 0:
            return self.dev(self.x, (self.y + step + 4) % 4, self.z, self.c)
        return self.dev(self.x, self.y, (self.z + step + 4) % 4, self.c)

    def partner(self):
        return self.dev(self.x, self.y, self.z, 1 - self.c)

    def swap(self):
        return self.dev(self.x + 1 - 2 * self.x_lo, self.y, self.z, 1 - self.c)


def remote(src, dst, sems, device):
    return pltpu.make_async_remote_copy(
        src_ref=src, dst_ref=dst, send_sem=sems[0], recv_sem=sems[1], device_id=device, device_id_type=MESH
    )


def greet(devices):
    barrier = pltpu.get_barrier_semaphore()
    for device in devices:
        pl.semaphore_signal(barrier, inc=1, device_id=device, device_id_type=MESH)
    pl.semaphore_wait(barrier, len(devices))


class Bufs:
    pass


SCRATCH = (
    ("w1", (4, 4, 2, 2, 16, W1), BF),
    ("w2", (4, 4, 2, 2, 16, FF), BF),
    ("w3", (4, 4, 2, 2, 64, D), BF),
    ("g1", (4, 4, 2, 2, 16, W1), BF),
    ("g2", (4, 4, 2, 2, 16, FF), BF),
    ("g3", (4, 4, 2, 2, 64, D), BF),
    ("act", (MICRO, SEQ + 16, D), BF),
    ("hb", (MICRO, SEQ, D), BF),
    ("gb", (MICRO, SEQ, D), BF),
    ("ho", (MICRO, SEQ, D), BF),
    ("xa", (MICRO, SEQ, D), BF),
    ("qkv", (MICRO, SEQ, D + 2 * HD), BF),
    ("probs", (MICRO, HEADS * SEQ, SEQ), F32),
    ("mixed", (MICRO, SEQ, D), BF),
    ("after", (MICRO, SEQ, D), F32),
    ("xf", (MICRO, SEQ, D), BF),
    ("u", (MICRO, SEQ, FF), BF),
    ("dp", (MICRO, SEQ, FF), BF),
    ("gf", (MICRO, SEQ, D), BF),
    ("dx", (SEQ, D), F32),
    ("dr", (SEQ, D), F32),
    ("ga", (MICRO, SEQ, D), BF),
    ("do", (SEQ, D), BF),
    ("dqkv", (MICRO, SEQ, D + 2 * HD), BF),
    ("gains", (8, D), F32),
    ("gain_sums", (2, MICRO, 8, D), F32),
)


def dot(left, right):
    return jnp.dot(left, right, preferred_element_type=F32)


def dot_nt(left, right):
    return lax.dot_general(left, right, (((1,), (1,)), ((), ())), preferred_element_type=F32)


def dot_tn(left, right):
    return lax.dot_general(left, right, (((0,), (0,)), ((), ())), preferred_element_type=F32)


def rms_factor(values):
    return lax.rsqrt(jnp.mean(values * values, axis=-1, keepdims=True) + NORM_EPS)


def norm_back(grad_normed, normed, factor):
    return factor * (grad_normed - normed * jnp.mean(grad_normed * normed, axis=-1, keepdims=True))


def tile(at, wide):
    return pl.ds(pl.multiple_of(at * wide, wide), wide)


def heads_down(value):
    return jnp.concatenate([value[:, h * HD : (h + 1) * HD] for h in range(HEADS)], axis=0)


def heads_across(value):
    return jnp.concatenate([value[h * SEQ : (h + 1) * SEQ] for h in range(HEADS)], axis=1)


def pad_column(act, m):
    length = act[m, SEQ : SEQ + 1, 0:1].astype(F32)
    positions = lax.broadcasted_iota(jnp.int32, (SEQ, 1), 0).astype(F32)
    return jnp.where(positions < length, 1.0, 0.0)


def read_gains(b):
    for start in range(4):
        block = b.w1[start, :, :, :, :, D + 2 * HD : D + 3 * HD].reshape(D // 4, HD).astype(F32)
        b.gains[:, start * 256 : (start + 1) * 256] = jnp.transpose(block)[0:8]


def forward_layer(b, m):
    pad = pad_column(b.act, m)
    hidden = b.hb[m].astype(F32)
    b.xa[m] = (hidden * rms_factor(hidden) * b.gains[0:1, :]).astype(BF)

    @pl.loop(0, (D + 2 * HD) // 256)
    def _(n):
        b.qkv[m, :, tile(n, 256)] = dot(b.xa[m], b.w1[:, :, :, :, :, tile(n, 256)].reshape(D, 256)).astype(BF)

    length = b.act[m, SEQ : SEQ + 1, 0:1].astype(F32)
    rows = lax.broadcasted_iota(jnp.int32, (SEQ, SEQ), 0)
    columns = lax.broadcasted_iota(jnp.int32, (SEQ, SEQ), 1)
    allowed = jnp.logical_and(columns <= rows, columns.astype(F32) < length)
    keys_all = b.qkv[m, :, D : D + HD]
    values_all = b.qkv[m, :, D + HD : D + 2 * HD]
    scores = dot_nt(heads_down(b.qkv[m, :, 0:D]), keys_all) * HD ** (-0.5)
    scores = jnp.where(allowed[None], scores.reshape(HEADS, SEQ, SEQ), NEG_FILL)
    raised = jnp.exp(scores - jnp.max(scores, axis=-1, keepdims=True))
    probs = (raised / jnp.sum(raised, axis=-1, keepdims=True)).reshape(HEADS * SEQ, SEQ)
    b.probs[m] = probs
    b.mixed[m] = heads_across(dot(probs.astype(BF), values_all)).astype(BF)

    @pl.loop(0, D // 256)
    def _(n):
        w = b.w1[:, :, :, :, :, pl.ds(pl.multiple_of(W1 - D + n * 256, HD), 256)].reshape(D, 256)
        b.after[m, :, tile(n, 256)] = b.hb[m, :, tile(n, 256)].astype(F32) + pad * dot(b.mixed[m], w)

    after = b.after[m]
    b.xf[m] = (after * rms_factor(after) * b.gains[1:2, :]).astype(BF)

    @pl.loop(0, FF // 512)
    def _(n):
        a = dot(b.xf[m], b.w2[:, :, :, :, :, tile(n, 512)].reshape(D, 512))
        sigmoid = 1.0 / (1.0 + jnp.exp(-a))
        b.u[m, :, tile(n, 512)] = (a * sigmoid).astype(BF)
        b.dp[m, :, tile(n, 512)] = (sigmoid * (1.0 + a * (1.0 - sigmoid))).astype(BF)

    @pl.loop(0, D // 256)
    def _(n):
        w = b.w3[:, :, :, :, :, tile(n, 256)].reshape(FF, 256)
        b.ho[m, :, tile(n, 256)] = (b.after[m, :, tile(n, 256)] + pad * dot(b.u[m], w)).astype(BF)


def backward_ffn(b, m):
    pad = pad_column(b.act, m)
    b.gf[m] = (b.gb[m].astype(F32) * pad).astype(BF)

    @pl.loop(0, 16)
    def _(n):
        w = b.w3[n // 4, n % 4].reshape(256, D)
        b.dp[m, :, tile(n, 256)] = (dot_nt(b.gf[m], w) * b.dp[m, :, tile(n, 256)].astype(F32)).astype(BF)

    @pl.loop(0, 4)
    def _(n):
        b.dx[:, tile(n, 256)] = dot_nt(b.dp[m], b.w2[n].reshape(256, FF))

    after = b.after[m]
    factor = rms_factor(after)
    normed = after * factor
    d_xf = b.dx[...]
    b.gain_sums[1, m] = jnp.sum((d_xf * normed).reshape(SEQ // 8, 8, D), axis=0)
    d_r = b.gb[m].astype(F32) + norm_back(d_xf * b.gains[1:2, :], normed, factor)
    b.dr[...] = d_r
    b.ga[m] = (d_r * pad).astype(BF)


def backward_attention(b, m):
    scale = HD ** (-0.5)

    @pl.loop(0, 4)
    def _(n):
        b.do[:, tile(n, 256)] = dot_nt(b.ga[m], b.w1[n, :, :, :, :, W1 - D :].reshape(256, D)).astype(BF)

    d_mixed = heads_down(b.do[...])
    keys_all = b.qkv[m, :, D : D + HD]
    values_all = b.qkv[m, :, D + HD : D + 2 * HD]
    probs = b.probs[m]
    d_p = dot_nt(d_mixed, values_all)
    b.dqkv[m, :, D + HD : D + 2 * HD] = dot_tn(probs.astype(BF), d_mixed).astype(BF)
    d_s = (probs * (d_p - jnp.sum(probs * d_p, axis=-1, keepdims=True))).astype(BF)
    b.dqkv[m, :, 0:D] = heads_across(dot(d_s, keys_all) * scale).astype(BF)
    b.dqkv[m, :, D : D + HD] = (dot_tn(d_s, heads_down(b.qkv[m, :, 0:D])) * scale).astype(BF)

    @pl.loop(0, 4)
    def _(n):
        w = b.w1[n, :, :, :, :, 0 : D + 2 * HD].reshape(256, D + 2 * HD)
        b.dx[:, tile(n, 256)] = dot_nt(b.dqkv[m], w)

    hidden = b.hb[m].astype(F32)
    factor = rms_factor(hidden)
    normed = hidden * factor
    d_xa = b.dx[...]
    b.gain_sums[0, m] = jnp.sum((d_xa * normed).reshape(SEQ // 8, 8, D), axis=0)
    b.ho[m] = (b.dr[...] + norm_back(d_xa * b.gains[0:1, :], normed, factor)).astype(BF)


def both(ref, cols):
    return ref[:, :, cols].reshape(MICRO * SEQ, -1)


def grads_down(b):
    @pl.loop(0, 16)
    def _(n):
        left = b.u[:, :, tile(n, 256)].reshape(MICRO * SEQ, 256)
        b.g3[n // 4, n % 4] = dot_tn(left, b.gf[...].reshape(MICRO * SEQ, D)).astype(BF).reshape(2, 2, 64, D)


def grads_up(b):
    @pl.loop(0, 16)
    def _(n):
        left = b.xf[:, :, tile(n // 4, 256)].reshape(MICRO * SEQ, 256)
        right = b.dp[:, :, tile(n % 4, D)].reshape(MICRO * SEQ, D)
        b.g2[n // 4, :, :, :, :, tile(n % 4, D)] = dot_tn(left, right).astype(BF).reshape(4, 2, 2, 16, D)


def grads_first(b):
    wide = D + 2 * HD

    @pl.loop(0, 4)
    def _(n):
        left = b.xa[:, :, tile(n, 256)].reshape(MICRO * SEQ, 256)
        b.g1[n, :, :, :, :, 0:wide] = dot_tn(left, b.dqkv[...].reshape(MICRO * SEQ, wide)).astype(BF).reshape(4, 2, 2, 16, wide)
        left = b.mixed[:, :, tile(n, 256)].reshape(MICRO * SEQ, 256)
        b.g1[n, :, :, :, :, W1 - D :] = dot_tn(left, b.ga[...].reshape(MICRO * SEQ, D)).astype(BF).reshape(4, 2, 2, 16, D)

    lines = [jnp.sum(b.gain_sums[k, 0] + b.gain_sums[k, 1], axis=0, keepdims=True) for k in range(2)]
    sums = jnp.concatenate(lines + [jnp.zeros((HD - 2, D), F32)], axis=0)
    for n in range(4):
        block = jnp.transpose(sums[:, n * 256 : (n + 1) * 256]).astype(BF)
        b.g1[n, :, :, :, :, D + 2 * HD : D + 3 * HD] = block.reshape(4, 2, 2, 16, HD)


N_GATHER = 12
N_SCATTER = 9
GATHER_CUTS = ((0, 1), (1, 2), (2, 2))
SCATTER_CUTS = ((2, 2), (1, 2), (0, 1))
STEPS = 5
WIDTHS = (W1, FF, D)
SEMAPHORES = (
    ("ag_send", STEPS * 2 * N_GATHER),
    ("ag_recv", STEPS * 2 * N_GATHER),
    ("ag_swap_send", STEPS + 1),
    ("ag_swap_recv", STEPS + 1),
    ("ag_local", STEPS + 1),
    ("rs_send", STEPS * 2 * N_SCATTER),
    ("rs_recv", STEPS * 2 * N_SCATTER),
    ("rs_swap_send", STEPS * 2),
    ("rs_swap_recv", STEPS * 2),
    ("relay_send", 2 * MICRO),
    ("relay_recv", 2 * MICRO),
    ("row_send", 2 * MICRO * LAYERS),
    ("row_recv", 2 * MICRO),
    ("row_local", 2 * MICRO),
)


def cut(cuts):
    made = []
    for which, count in cuts:
        wide = WIDTHS[which] // count
        for at in range(count):
            made.append((which, at * wide, wide))
    return made


def near_far(chunk, part):
    which, start, wide = chunk
    near = (wide // HD + 1) // 2 * HD
    return pl.ds(start, near) if part == 0 else pl.ds(start + near, wide - near)


def gather_weights(role, shards, fulls, act_in, b, sem):
    y, z, c = role.y, role.z, role.c
    place = (y, z)
    chunks = cut(GATHER_CUTS)
    count = len(chunks)

    def own_copies(step, owner):
        which, start, wide = chunks[step]
        src = shards[which].at[:, :, pl.ds(start, wide)]
        dst = fulls[which].at[y, z, owner, :, :, pl.ds(start, wide)]
        return (
            remote(src, dst, (sem.ag_swap_send.at[step], sem.ag_swap_recv.at[step]), role.swap()),
            pltpu.make_async_copy(src, dst, sem.ag_local.at[step]),
        )

    act_far = remote(act_in, b.act, (sem.ag_swap_send.at[count], sem.ag_swap_recv.at[count]), role.swap())
    act_near = pltpu.make_async_copy(act_in, b.act, sem.ag_local.at[count])

    @pl.when(role.native)
    def _():
        for step in range(count):
            own_copies(step, c)[1].start()
        act_near.start()

    @pl.when(jnp.logical_not(role.native))
    def _():
        for step in range(count):
            own_copies(step, 1 - c)[0].start()
        act_far.start()

    def piece(step, half, first, second, part=None):
        which, start, wide = chunks[step]
        cols = pl.ds(start, wide) if part is None else near_far(chunks[step], part)
        index = (first, second) if half == 0 else (second, first)
        return fulls[which].at[index[0], index[1], c, half, :, cols]

    def hop(step, half, number):
        one, two = half, 1 - half
        p, s = place[one], place[two]
        nxt, prv = (p + 1) % 4, (p + 3) % 4
        snx, spv, sop = (s + 1) % 4, (s + 3) % 4, (s + 2) % 4
        every, low, high = slice(None), pl.ds(0, 2), pl.ds(2, 2)
        first, second, part, device = (
            (p, s, None, role.along(one, 1)),
            (p, s, None, role.along(one, -1)),
            (prv, s, 0, role.along(one, 1)),
            (nxt, s, 1, role.along(one, -1)),
            (every, s, None, role.along(two, 1)),
            (every, s, None, role.along(two, -1)),
            (low, spv, None, role.along(two, 1)),
            (high, snx, None, role.along(two, -1)),
            (every, s, None, role.partner()),
            (every, spv, None, role.partner()),
            (every, snx, None, role.partner()),
            (every, sop, None, role.partner()),
        )[number]
        view = piece(step, half, first, second, part)
        at = (step * 2 + half) * N_GATHER + number
        return remote(view, view, (sem.ag_send.at[at], sem.ag_recv.at[at]), device)

    arrive = ((), (0, 1), (2, 3), (4, 5), (6, 7))
    leave = ((0, 1), (2, 3), (4, 5, 8), (6, 7, 9, 10), (11,))
    for tick in range(count + 4):
        for level in range(5):
            step = tick - level
            if not 0 <= step < count:
                continue
            if level == 0:

                @pl.when(role.native)
                def _():
                    own_copies(step, c)[1].wait()

                @pl.when(jnp.logical_not(role.native))
                def _():
                    own_copies(step, 1 - c)[0].wait()

            for half in (0, 1):
                for number in arrive[level]:
                    hop(step, half, number).wait_recv()
                for number in leave[level]:
                    hop(step, half, number).start()
    for step in range(count):
        for half in (0, 1):
            for number in (8, 9, 10, 11):
                hop(step, half, number).wait_recv()
            for number in range(N_GATHER):
                hop(step, half, number).wait_send()

    @pl.when(role.native)
    def _():
        act_near.wait()

    @pl.when(jnp.logical_not(role.native))
    def _():
        act_far.wait()


class Scatter:
    def __init__(self, role, grads, works, swaps, outs, sem, free):
        self.role, self.grads, self.works, self.swaps, self.outs = role, grads, works, swaps, outs
        self.sem, self.free = sem, free
        self.chunks = cut(SCATTER_CUTS)
        self.peers = [role.along(0, 1), role.along(0, -1), role.along(1, 1), role.along(1, -1), role.partner()]

    def say_free(self, which):
        for device in self.peers:
            pl.semaphore_signal(self.free.at[which], inc=1, device_id=device, device_id_type=MESH)

    def wait_free(self, which):
        pl.semaphore_wait(self.free.at[which], len(self.peers))

    def cols(self, step):
        which, start, wide = self.chunks[step]
        return pl.ds(start, wide)

    def core_copy(self, step):
        which = self.chunks[step][0]
        at = step * 2 * N_SCATTER
        return remote(
            self.grads[which].at[:, :, 1 - self.role.c, :, :, self.cols(step)],
            self.works[which].at[:, :, 0, :, :, self.cols(step)],
            (self.sem.rs_send.at[at], self.sem.rs_recv.at[at]),
            self.role.partner(),
        )

    def piece(self, step, half, first, second, part=None):
        index = (first, second) if half == 0 else (second, first)
        cols = self.cols(step) if part is None else near_far(self.chunks[step], part)
        return self.grads[self.chunks[step][0]].at[index[0], index[1], self.role.c, half, :, cols]

    def spot(self, step, half, first, second, part=None):
        cols = self.cols(step) if part is None else near_far(self.chunks[step], part)
        return self.works[self.chunks[step][0]].at[first, second, 1, half, :, cols]

    def hop(self, step, half, number):
        role = self.role
        place = (role.y, role.z)
        one, two = half, 1 - half
        p, s = place[one], place[two]
        nxt, prv, opp = (p + 1) % 4, (p + 3) % 4, (p + 2) % 4
        snx, spv, sop = (s + 1) % 4, (s + 3) % 4, (s + 2) % 4
        every, low, high = slice(None), pl.ds(0, 2), pl.ds(2, 2)
        src, dst = (
            ((opp, low, None), (2, low, None)),
            ((opp, high, None), (2, high, None)),
            ((nxt, every, None), (0, every, None)),
            ((prv, every, None), (1, every, None)),
            ((p, sop, 0), (3, 0, 0)),
            ((p, sop, 1), (3, 1, 1)),
            ((p, snx, None), (3, 2, None)),
            ((p, spv, None), (3, 3, None)),
        )[number]
        axis = one if number < 4 else two
        at = (step * 2 + half) * N_SCATTER + 1 + number
        return remote(
            self.piece(step, half, *src),
            self.spot(step, half, *dst),
            (self.sem.rs_send.at[at], self.sem.rs_recv.at[at]),
            role.along(axis, 1 if number % 2 == 0 else -1),
        )

    def swapped(self, step, half):
        which = self.chunks[step][0]
        at = step * 2 + half
        return remote(
            self.grads[which].at[self.role.y, self.role.z, self.role.c, half, :, self.cols(step)],
            self.swaps[which].at[half, :, self.cols(step)],
            (self.sem.rs_swap_send.at[at], self.sem.rs_swap_recv.at[at]),
            self.role.swap(),
        )

    def add_core(self, step):
        self.core_copy(step).wait_recv()
        which = self.chunks[step][0]
        cols, c = self.cols(step), self.role.c
        grad, work = self.grads[which], self.works[which]

        @pl.loop(0, 16)
        def _(at):
            y, z = at // 4, at % 4
            grad[y, z, c, :, :, cols] = grad[y, z, c, :, :, cols] + work[y, z, 0, :, :, cols]

    def level(self, step, half, number):
        role = self.role
        place = (role.y, role.z)
        one, two = half, 1 - half
        p, s = place[one], place[two]
        nxt, prv = (p + 1) % 4, (p + 3) % 4
        snx, spv = (s + 1) % 4, (s + 3) % 4
        which = self.chunks[step][0]
        if number > 0:
            self.hop(step, half, 2 * number - 2).wait_recv()
            self.hop(step, half, 2 * number - 1).wait_recv()

        def add(there, *spots):
            total = there[...].astype(F32)
            for spot in spots:
                total = total + spot[...].astype(F32)
            there[...] = total.astype(BF)

        if number == 1:
            for i in range(2):
                add(self.piece(step, half, nxt, i), self.spot(step, half, 2, i))
                add(self.piece(step, half, prv, 2 + i), self.spot(step, half, 2, 2 + i))
        elif number == 2:
            for i in range(4):
                add(self.piece(step, half, p, i), self.spot(step, half, 0, i), self.spot(step, half, 1, i))
        elif number == 3:
            add(self.piece(step, half, p, snx, 0), self.spot(step, half, 3, 0, 0))
            add(self.piece(step, half, p, spv, 1), self.spot(step, half, 3, 1, 1))
        elif number == 4:
            here = self.piece(step, half, p, s)
            total = here[...].astype(F32)
            for i in (2, 3):
                total = total + self.spot(step, half, 3, i)[...].astype(F32)

            @pl.when(role.native)
            def _():
                self.outs[which][half, :, self.cols(step)] = total

            @pl.when(jnp.logical_not(role.native))
            def _():
                here[...] = total.astype(BF)
                self.swapped(step, half).start()

        if number < 4:
            self.hop(step, half, 2 * number).start()
            self.hop(step, half, 2 * number + 1).start()

    def run(self):
        count = len(self.chunks)
        for step in range(count):
            which = self.chunks[step][0]
            if step == 0 or self.chunks[step - 1][0] != which:
                self.wait_free(which)
            self.core_copy(step).start()
        for tick in range(count + 4):
            for number in range(4, -1, -1):
                step = tick - number
                if 0 <= step < count:
                    if number == 0:
                        self.add_core(step)
                    for half in (0, 1):
                        self.level(step, half, number)

    def finish(self):
        role = self.role

        @pl.when(jnp.logical_not(role.native))
        def _():
            for step in range(len(self.chunks)):
                which = self.chunks[step][0]
                for half in (0, 1):
                    self.swapped(step, half).wait()
                    self.outs[which][half, :, self.cols(step)] = self.swaps[which][half, :, self.cols(step)].astype(F32)

        for step in range(len(self.chunks)):
            self.core_copy(step).wait_send()
            for half in (0, 1):
                for number in range(8):
                    self.hop(step, half, number).wait_send()


class Rows:
    def __init__(self, role, which, source, out, sem):
        self.role, self.which, self.source, self.out, self.sem = role, which, source, out, sem
        self.source_x = (3, 0)[which]
        self.holds = role.x == self.source_x

    def copies(self, m):
        role, rows = self.role, SEQ // LAYERS
        made = []
        for section in range(LAYERS):
            target_x, target_c = 2 * (section // 2) + role.c, section % 2
            src = self.source.at[m, pl.ds(section * rows, rows)]
            at = (self.which * MICRO + m) * LAYERS + section
            arrival = self.which * MICRO + m
            here = jnp.logical_and(target_x == self.source_x, target_c == role.c)
            far = remote(
                src, self.out.at[m], (self.sem.row_send.at[at], self.sem.row_recv.at[arrival]), role.dev(target_x, role.y, role.z, target_c)
            )
            near = pltpu.make_async_copy(src, self.out.at[m], self.sem.row_local.at[arrival])
            made.append((here, far, near))
        return made

    def start(self, m):
        @pl.when(self.holds)
        def _():
            for here, far, near in self.copies(m):
                pl.when(here)(near.start)
                pl.when(jnp.logical_not(here))(far.start)

    def sent(self, m):
        @pl.when(self.holds)
        def _():
            for here, far, near in self.copies(m):
                pl.when(here)(near.wait)
                pl.when(jnp.logical_not(here))(far.wait_send)

    def arrived(self, m):
        kept = jnp.logical_and(self.holds, (self.role.x // 2) * 2 + self.role.c == self.role.x)
        kept = jnp.logical_and(kept, self.role.x_lo == self.role.c)

        @pl.when(jnp.logical_not(kept))
        def _():
            self.copies(m)[0][1].wait_recv()


def decoder_kernel(*refs):
    names = [name for name, _, _ in SCRATCH]
    s1, s2, s3, act_in, o1, o2, o3, final_out, start_out = refs[:9]
    b, sem = Bufs(), Bufs()
    rest = list(refs[9:])
    for name in names:
        setattr(b, name, rest.pop(0))
    swaps = [rest.pop(0) for _ in range(3)]
    for name, _ in SEMAPHORES:
        setattr(sem, name, rest.pop(0))
    free = rest.pop(0)

    role = Role()
    x, y, z, c = role.x, role.y, role.z, role.c
    peers = [role.along(0, 1), role.along(0, -1), role.along(1, 1), role.along(1, -1)]
    for away in range(4):
        for other in range(2):
            if (away, other) != (0, 0):
                peers.append(role.dev((x + away) % 4, y, z, (c + other) % 2))
    greet(peers)

    gather_weights(role, (s1, s2, s3), (b.w1, b.w2, b.w3), act_in, b, sem)
    read_gains(b)
    first, last = x == 0, x == LAYERS - 1

    @pl.when(first)
    def _():
        b.hb[...] = b.act[:, 0:SEQ]

    @pl.when(last)
    def _():
        b.gb[...] = b.act[:, 0:SEQ]

    def relay(which, m):
        dst, there = ((b.hb, (x + 1) % 4), (b.gb, (x + 3) % 4))[which]
        at = which * MICRO + m
        return remote(b.ho.at[m], dst.at[m], (sem.relay_send.at[at], sem.relay_recv.at[at]), role.dev(there, y, z, c))

    final_rows = Rows(role, 0, b.ho, final_out, sem)
    start_rows = Rows(role, 1, b.ho, start_out, sem)

    @pl.loop(0, MICRO)
    def _(m):
        pl.when(jnp.logical_not(first))(lambda: relay(0, m).wait_recv())
        forward_layer(b, m)
        pl.when(jnp.logical_not(last))(lambda: relay(0, m).start())
        final_rows.start(m)

    scatter = Scatter(role, (b.g1, b.g2, b.g3), (b.w1, b.w2, b.w3), swaps, (o1, o2, o3), sem, free)

    @pl.loop(0, MICRO)
    def _(m):
        pl.when(jnp.logical_not(last))(lambda: relay(1, m).wait_recv())
        backward_ffn(b, m)
        pl.when(jnp.logical_not(last))(lambda: relay(0, m).wait_send())
        final_rows.sent(m)
        backward_attention(b, m)
        pl.when(jnp.logical_not(first))(lambda: relay(1, m).start())
        start_rows.start(m)

    for which in (2, 1, 0):
        scatter.say_free(which)
    grads_down(b)
    grads_up(b)
    grads_first(b)
    scatter.run()
    scatter.finish()
    for m in range(MICRO):
        pl.when(jnp.logical_not(first))(lambda: relay(1, m).wait_send())
        start_rows.sent(m)
        final_rows.arrived(m)
        start_rows.arrived(m)


def decoder(s1, s2, s3, act):
    hbm = pl.BlockSpec(memory_space=pl.ANY)
    vmem = pl.BlockSpec(memory_space=pltpu.VMEM)
    shapes = [s.shape for s in (s1, s2, s3)]
    rows = SEQ // LAYERS
    return pl.pallas_call(
        decoder_kernel,
        out_shape=[jax.ShapeDtypeStruct(shape, F32) for shape in shapes]
        + [jax.ShapeDtypeStruct((MICRO, rows, D), BF)] * 2,
        in_specs=[hbm] * 4,
        out_specs=[vmem] * 3 + [hbm] * 2,
        scratch_shapes=[pltpu.VMEM(shape, dtype) for _, shape, dtype in SCRATCH]
        + [pltpu.VMEM(shape, BF) for shape in shapes]
        + [pltpu.SemaphoreType.DMA((count,)) for _, count in SEMAPHORES]
        + [pltpu.SemaphoreType.REGULAR((3,))],
        compiler_params=pltpu.CompilerParams(collective_id=0, has_side_effects=True, vmem_limit_bytes=63 << 20),
        name="decoder_step",
    )(s1, s2, s3, act)


def body(
    inputs, cotangent, lengths, attn_gain, w_query, w_key, w_value, w_out, ffn_gain, w_up, w_down
):
    role = Role()
    gains = jnp.pad(jnp.stack([attn_gain, ffn_gain], axis=1), ((0, 0), (0, HD - 2)))
    first = jnp.concatenate([w_query, w_key, w_value, gains, w_out], axis=1).astype(BF).reshape(2, 16, W1)
    second = w_up.astype(BF).reshape(2, 16, FF)
    third = w_down.astype(BF).reshape(2, 64, D)
    rows = jnp.where(role.x < 2, inputs[:, 0], cotangent[:, 0])
    lengths_rows = jnp.broadcast_to(lengths.astype(BF)[:, :, None], (MICRO, 16, D))
    act = jnp.concatenate([rows, lengths_rows], axis=1)
    o1, o2, o3, final_rows, input_rows = decoder(first, second, third, act)
    o1 = o1.reshape(32, W1)
    return (
        final_rows[:, None],
        input_rows[:, None],
        o1[:, D + 2 * HD],
        o1[:, :D],
        o1[:, D : D + HD],
        o1[:, D + HD : D + 2 * HD],
        o1[:, W1 - D :],
        o1[:, D + 2 * HD + 1],
        o2.reshape(32, FF),
        o3.reshape(128, D),
    )


def solution(mesh):
    both_axes = P(("section", "dp"))
    both_rows = P(("section", "dp"), None)
    acts = P(None, "dp", None, None)
    outs = P(None, "dp", "section", None)
    weights = (both_axes, both_rows, both_rows, both_rows, both_rows, both_axes, both_rows, both_rows)
    return jax.shard_map(
        body,
        mesh=mesh,
        in_specs=(acts, acts, P(None, "dp")) + weights,
        out_specs=(outs, outs) + weights,
        check_vma=False,
    )
```

```python
import functools

import jax
import jax.numpy as jnp
from jax import lax
from jax.experimental import pallas as pl
from jax.experimental.pallas import tpu as pltpu
from jax.sharding import PartitionSpec as P

D = 1024
HEADS = 8
HD = 128
FF = 4096
LAYERS = 4
SEQ = 128
MICRO = 2
NORM_EPS = 1e-06
NEG_FILL = -1000000000.0
W1 = D + 2 * HD + HD + D
BF = jnp.bfloat16
F32 = jnp.float32
MESH = pl.DeviceIdType.MESH


class Role:
    def __init__(self):
        section = lax.axis_index("section")
        dp = lax.axis_index("dp")
        self.c = section % 2
        self.x_lo = dp % 2
        self.x = (section // 2) * 2 + self.x_lo
        self.z = (dp // 2) % 4
        self.y = dp // 8
        self.native = self.c == self.x_lo

    def dev(self, x, y, z, c):
        return ((x // 2) * 2 + c, (y * 4 + z) * 2 + x % 2)

    def along(self, axis, step):
        if axis == 0:
            return self.dev(self.x, (self.y + step + 4) % 4, self.z, self.c)
        return self.dev(self.x, self.y, (self.z + step + 4) % 4, self.c)

    def partner(self):
        return self.dev(self.x, self.y, self.z, 1 - self.c)

    def swap(self):
        return self.dev(self.x + 1 - 2 * self.x_lo, self.y, self.z, 1 - self.c)


def remote(src, dst, sems, device):
    return pltpu.make_async_remote_copy(
        src_ref=src, dst_ref=dst, send_sem=sems[0], recv_sem=sems[1], device_id=device, device_id_type=MESH
    )


def greet(devices):
    barrier = pltpu.get_barrier_semaphore()
    for device in devices:
        pl.semaphore_signal(barrier, inc=1, device_id=device, device_id_type=MESH)
    pl.semaphore_wait(barrier, len(devices))


class Bufs:
    pass


SCRATCH = (
    ("w1", (4, 4, 2, 2, 16, W1), BF),
    ("w2", (4, 4, 2, 2, 16, FF), BF),
    ("w3", (4, 4, 2, 2, 64, D), BF),
    ("g1", (4, 4, 2, 2, 16, W1), BF),
    ("g2", (4, 4, 2, 2, 16, FF), BF),
    ("g3", (4, 4, 2, 2, 64, D), BF),
    ("act", (MICRO, SEQ + 16, D), BF),
    ("hb", (MICRO, SEQ, D), BF),
    ("gb", (MICRO, SEQ, D), BF),
    ("ho", (MICRO, SEQ, D), BF),
    ("xa", (MICRO, SEQ, D), BF),
    ("qkv", (MICRO, SEQ, D + 2 * HD), BF),
    ("probs", (MICRO, HEADS * SEQ, SEQ), F32),
    ("mixed", (MICRO, SEQ, D), BF),
    ("after", (MICRO, SEQ, D), F32),
    ("xf", (MICRO, SEQ, D), BF),
    ("u", (MICRO, SEQ, FF), BF),
    ("dp", (MICRO, SEQ, FF), BF),
    ("gf", (MICRO, SEQ, D), BF),
    ("dx", (SEQ, D), F32),
    ("dr", (SEQ, D), F32),
    ("ga", (MICRO, SEQ, D), BF),
    ("do", (SEQ, D), BF),
    ("dqkv", (MICRO, SEQ, D + 2 * HD), BF),
    ("gains", (8, D), F32),
    ("gain_sums", (2, MICRO, 8, D), F32),
)


def dot(left, right):
    return jnp.dot(left, right, preferred_element_type=F32)


def dot_nt(left, right):
    return lax.dot_general(left, right, (((1,), (1,)), ((), ())), preferred_element_type=F32)


def dot_tn(left, right):
    return lax.dot_general(left, right, (((0,), (0,)), ((), ())), preferred_element_type=F32)


def dot_w(weight, value):
    return jnp.transpose(dot(weight, jnp.transpose(value)))


def rms_factor(values):
    return lax.rsqrt(jnp.mean(values * values, axis=-1, keepdims=True) + NORM_EPS)


def norm_back(grad_normed, normed, factor):
    return factor * (grad_normed - normed * jnp.mean(grad_normed * normed, axis=-1, keepdims=True))


def tile(at, wide):
    return pl.ds(pl.multiple_of(at * wide, wide), wide)


def heads_down(value):
    return jnp.concatenate([value[:, h * HD : (h + 1) * HD] for h in range(HEADS)], axis=0)


def heads_across(value):
    return jnp.concatenate([value[h * SEQ : (h + 1) * SEQ] for h in range(HEADS)], axis=1)


def pad_column(act, m):
    length = act[m, SEQ : SEQ + 1, 0:1].astype(F32)
    positions = lax.broadcasted_iota(jnp.int32, (SEQ, 1), 0).astype(F32)
    return jnp.where(positions < length, 1.0, 0.0)


def read_gains(b):
    for start in range(4):
        block = b.w1[start, :, :, :, :, D + 2 * HD : D + 3 * HD].reshape(D // 4, HD).astype(F32)
        b.gains[:, start * 256 : (start + 1) * 256] = jnp.transpose(block)[0:8]


def transpose_down(b):
    @pl.loop(0, 4)
    def _(n):
        b.g2[:, :, :, :, :, tile(n, D)] = jnp.transpose(b.w3[n].reshape(D, D)).reshape(4, 4, 2, 2, 16, D)


def transpose_up(b):
    @pl.loop(0, 4)
    def _(n):
        b.g3[n] = jnp.transpose(b.w2[:, :, :, :, :, tile(n, D)].reshape(D, D)).reshape(4, 2, 2, 64, D)


def forward_qkv(b, m):
    hidden = b.hb[m].astype(F32)
    b.xa[m] = (hidden * rms_factor(hidden) * b.gains[0:1, :]).astype(BF)

    wide = D + 2 * HD
    b.qkv[m] = dot(b.xa[m], b.w1[:, :, :, :, :, 0:wide].reshape(D, wide)).astype(BF)


def forward_attention(b, m):
    length = b.act[m, SEQ : SEQ + 1, 0:1].astype(F32)
    rows = lax.broadcasted_iota(jnp.int32, (SEQ, SEQ), 0)
    columns = lax.broadcasted_iota(jnp.int32, (SEQ, SEQ), 1)
    allowed = jnp.logical_and(columns <= rows, columns.astype(F32) < length)
    keys_all = b.qkv[m, :, D : D + HD]
    values_all = b.qkv[m, :, D + HD : D + 2 * HD]
    scores = dot_nt(heads_down(b.qkv[m, :, 0:D]), keys_all) * HD ** (-0.5)
    scores = jnp.where(allowed[None], scores.reshape(HEADS, SEQ, SEQ), NEG_FILL)
    raised = jnp.exp(scores - jnp.max(scores, axis=-1, keepdims=True))
    probs = (raised / jnp.sum(raised, axis=-1, keepdims=True)).reshape(HEADS * SEQ, SEQ)
    b.probs[m] = probs
    b.mixed[m] = heads_across(dot(probs.astype(BF), values_all)).astype(BF)


def forward_out(b, m):
    pad = pad_column(b.act, m)

    w = b.w1[:, :, :, :, :, W1 - D :].reshape(D, D)
    b.after[m] = b.hb[m].astype(F32) + pad * dot(b.mixed[m], w)

    after = b.after[m]
    b.xf[m] = (after * rms_factor(after) * b.gains[1:2, :]).astype(BF)


def forward_up(b, m):
    a = dot(b.xf[m], b.w2[...].reshape(D, FF))
    sigmoid = 1.0 / (1.0 + jnp.exp(-a))
    b.u[m] = (a * sigmoid).astype(BF)
    b.dp[m] = (sigmoid * (1.0 + a * (1.0 - sigmoid))).astype(BF)


def forward_down(b, m):
    pad = pad_column(b.act, m)

    b.ho[m] = (b.after[m] + pad * dot(b.u[m], b.w3[...].reshape(FF, D))).astype(BF)


def backward_act(b, m):
    pad = pad_column(b.act, m)
    b.gf[m] = (b.gb[m].astype(F32) * pad).astype(BF)

    b.dp[m] = (dot(b.gf[m], b.g2[...].reshape(D, FF)) * b.dp[m].astype(F32)).astype(BF)


def backward_up(b, m):
    b.dx[...] = dot(b.dp[m], b.g3[...].reshape(FF, D))


def backward_ffn_norm(b, m):
    pad = pad_column(b.act, m)
    after = b.after[m]
    factor = rms_factor(after)
    normed = after * factor
    d_xf = b.dx[...]
    b.gain_sums[1, m] = jnp.sum((d_xf * normed).reshape(SEQ // 8, 8, D), axis=0)
    d_r = b.gb[m].astype(F32) + norm_back(d_xf * b.gains[1:2, :], normed, factor)
    b.dr[...] = d_r
    b.ga[m] = (d_r * pad).astype(BF)


def backward_out(b, m):
    b.do[...] = dot_w(b.w1[:, :, :, :, :, W1 - D :].reshape(D, D), b.ga[m]).astype(BF)


def backward_attention(b, m):
    scale = HD ** (-0.5)
    d_mixed = heads_down(b.do[...])
    keys_all = b.qkv[m, :, D : D + HD]
    values_all = b.qkv[m, :, D + HD : D + 2 * HD]
    probs = b.probs[m]
    d_p = dot_nt(d_mixed, values_all)
    b.dqkv[m, :, D + HD : D + 2 * HD] = dot_tn(probs.astype(BF), d_mixed).astype(BF)
    d_s = (probs * (d_p - jnp.sum(probs * d_p, axis=-1, keepdims=True))).astype(BF)
    b.dqkv[m, :, 0:D] = heads_across(dot(d_s, keys_all) * scale).astype(BF)
    b.dqkv[m, :, D : D + HD] = (dot_tn(d_s, heads_down(b.qkv[m, :, 0:D])) * scale).astype(BF)


def backward_qkv(b, m):
    wide = D + 2 * HD
    b.dx[...] = dot_w(b.w1[:, :, :, :, :, 0:wide].reshape(D, wide), b.dqkv[m])


def backward_in(b, m):
    hidden = b.hb[m].astype(F32)
    factor = rms_factor(hidden)
    normed = hidden * factor
    d_xa = b.dx[...]
    b.gain_sums[0, m] = jnp.sum((d_xa * normed).reshape(SEQ // 8, 8, D), axis=0)
    b.ho[m] = (b.dr[...] + norm_back(d_xa * b.gains[0:1, :], normed, factor)).astype(BF)


def both(ref, cols):
    return ref[:, :, cols].reshape(MICRO * SEQ, -1)


def grads_down(b):
    left = b.u[...].reshape(MICRO * SEQ, FF)
    b.g3[...] = dot_tn(left, b.gf[...].reshape(MICRO * SEQ, D)).astype(BF).reshape(4, 4, 2, 2, 64, D)


def grads_up(b):
    right = b.dp[...].reshape(MICRO * SEQ, FF)
    b.g2[...] = dot_tn(b.xf[...].reshape(MICRO * SEQ, D), right).astype(BF).reshape(4, 4, 2, 2, 16, FF)


def grads_first(b):
    wide = D + 2 * HD

    left = b.xa[...].reshape(MICRO * SEQ, D)
    b.g1[:, :, :, :, :, 0:wide] = dot_tn(left, b.dqkv[...].reshape(MICRO * SEQ, wide)).astype(BF).reshape(4, 4, 2, 2, 16, wide)
    left = b.mixed[...].reshape(MICRO * SEQ, D)
    b.g1[:, :, :, :, :, W1 - D :] = dot_tn(left, b.ga[...].reshape(MICRO * SEQ, D)).astype(BF).reshape(4, 4, 2, 2, 16, D)

    lines = [jnp.sum(b.gain_sums[k, 0] + b.gain_sums[k, 1], axis=0, keepdims=True) for k in range(2)]
    sums = jnp.concatenate(lines + [jnp.zeros((HD - 2, D), F32)], axis=0)
    for n in range(4):
        block = jnp.transpose(sums[:, n * 256 : (n + 1) * 256]).astype(BF)
        b.g1[n, :, :, :, :, D + 2 * HD : D + 3 * HD] = block.reshape(4, 2, 2, 16, HD)


FORWARD = (forward_qkv, forward_attention, forward_out, forward_up, forward_down)
BACKWARD = (
    backward_act,
    backward_up,
    backward_ffn_norm,
    backward_out,
    backward_attention,
    backward_qkv,
    backward_in,
)


N_GATHER = 12
N_SCATTER = 9
GATHER_CUTS = ((0, 1), (1, 2), (2, 2))
SCATTER_CUTS = ((2, 2), (1, 2), (0, 1))
STEPS = 5
WIDTHS = (W1, FF, D)
SEMAPHORES = (
    ("ag_send", STEPS * 2 * N_GATHER),
    ("ag_recv", STEPS * 2 * N_GATHER),
    ("ag_swap_send", STEPS + 1),
    ("ag_swap_recv", STEPS + 1),
    ("ag_local", STEPS + 1),
    ("rs_send", STEPS * 2 * N_SCATTER),
    ("rs_recv", STEPS * 2 * N_SCATTER),
    ("rs_swap_send", STEPS * 2),
    ("rs_swap_recv", STEPS * 2),
    ("relay_send", 2 * MICRO),
    ("relay_recv", 2 * MICRO),
    ("row_send", 2 * MICRO * LAYERS),
    ("row_recv", 2 * MICRO),
    ("row_local", 2 * MICRO),
)


def cut(cuts):
    made = []
    for which, count in cuts:
        wide = WIDTHS[which] // count
        for at in range(count):
            made.append((which, at * wide, wide))
    return made


def near_far(chunk, part):
    which, start, wide = chunk
    near = (wide // HD + 1) // 2 * HD
    return pl.ds(start, near) if part == 0 else pl.ds(start + near, wide - near)


def gather_weights(role, shards, fulls, act_in, b, sem):
    y, z, c = role.y, role.z, role.c
    place = (y, z)
    chunks = cut(GATHER_CUTS)
    count = len(chunks)

    def own_copies(step, owner):
        which, start, wide = chunks[step]
        src = shards[which].at[:, :, pl.ds(start, wide)]
        dst = fulls[which].at[y, z, owner, :, :, pl.ds(start, wide)]
        return (
            remote(src, dst, (sem.ag_swap_send.at[step], sem.ag_swap_recv.at[step]), role.swap()),
            pltpu.make_async_copy(src, dst, sem.ag_local.at[step]),
        )

    act_far = remote(act_in, b.act, (sem.ag_swap_send.at[count], sem.ag_swap_recv.at[count]), role.swap())
    act_near = pltpu.make_async_copy(act_in, b.act, sem.ag_local.at[count])

    @pl.when(role.native)
    def _():
        for step in range(count):
            own_copies(step, c)[1].start()
        act_near.start()

    @pl.when(jnp.logical_not(role.native))
    def _():
        for step in range(count):
            own_copies(step, 1 - c)[0].start()
        act_far.start()

    def piece(step, half, first, second, part=None):
        which, start, wide = chunks[step]
        cols = pl.ds(start, wide) if part is None else near_far(chunks[step], part)
        index = (first, second) if half == 0 else (second, first)
        return fulls[which].at[index[0], index[1], c, half, :, cols]

    def hop(step, half, number):
        one, two = half, 1 - half
        p, s = place[one], place[two]
        nxt, prv = (p + 1) % 4, (p + 3) % 4
        snx, spv, sop = (s + 1) % 4, (s + 3) % 4, (s + 2) % 4
        every, low, high = slice(None), pl.ds(0, 2), pl.ds(2, 2)
        first, second, part, device = (
            (p, s, None, role.along(one, 1)),
            (p, s, None, role.along(one, -1)),
            (prv, s, 0, role.along(one, 1)),
            (nxt, s, 1, role.along(one, -1)),
            (every, s, None, role.along(two, 1)),
            (every, s, None, role.along(two, -1)),
            (low, spv, None, role.along(two, 1)),
            (high, snx, None, role.along(two, -1)),
            (every, s, None, role.partner()),
            (every, spv, None, role.partner()),
            (every, snx, None, role.partner()),
            (every, sop, None, role.partner()),
        )[number]
        view = piece(step, half, first, second, part)
        at = (step * 2 + half) * N_GATHER + number
        return remote(view, view, (sem.ag_send.at[at], sem.ag_recv.at[at]), device)

    arrive = ((), (0, 1), (2, 3), (4, 5), (6, 7))
    leave = ((0, 1), (2, 3), (4, 5, 8), (6, 7, 9, 10), (11,))
    for tick in range(count + 4):
        for level in range(5):
            step = tick - level
            if not 0 <= step < count:
                continue
            if level == 0:

                @pl.when(role.native)
                def _():
                    own_copies(step, c)[1].wait()

                @pl.when(jnp.logical_not(role.native))
                def _():
                    own_copies(step, 1 - c)[0].wait()

            for half in (0, 1):
                for number in arrive[level]:
                    hop(step, half, number).wait_recv()
                for number in leave[level]:
                    hop(step, half, number).start()
    for step in range(count):
        for half in (0, 1):
            for number in (8, 9, 10, 11):
                hop(step, half, number).wait_recv()
            for number in range(N_GATHER):
                hop(step, half, number).wait_send()

    @pl.when(role.native)
    def _():
        act_near.wait()

    @pl.when(jnp.logical_not(role.native))
    def _():
        act_far.wait()


class Scatter:
    def __init__(self, role, grads, works, swaps, outs, sem, free):
        self.role, self.grads, self.works, self.swaps, self.outs = role, grads, works, swaps, outs
        self.sem, self.free = sem, free
        self.chunks = cut(SCATTER_CUTS)
        self.peers = [role.along(0, 1), role.along(0, -1), role.along(1, 1), role.along(1, -1), role.partner()]

    def say_free(self, which):
        for device in self.peers:
            pl.semaphore_signal(self.free.at[which], inc=1, device_id=device, device_id_type=MESH)

    def wait_free(self, which):
        pl.semaphore_wait(self.free.at[which], len(self.peers))

    def cols(self, step):
        which, start, wide = self.chunks[step]
        return pl.ds(start, wide)

    def core_copy(self, step):
        which = self.chunks[step][0]
        at = step * 2 * N_SCATTER
        return remote(
            self.grads[which].at[:, :, 1 - self.role.c, :, :, self.cols(step)],
            self.works[which].at[:, :, 0, :, :, self.cols(step)],
            (self.sem.rs_send.at[at], self.sem.rs_recv.at[at]),
            self.role.partner(),
        )

    def piece(self, step, half, first, second, part=None):
        index = (first, second) if half == 0 else (second, first)
        cols = self.cols(step) if part is None else near_far(self.chunks[step], part)
        return self.grads[self.chunks[step][0]].at[index[0], index[1], self.role.c, half, :, cols]

    def spot(self, step, half, first, second, part=None):
        cols = self.cols(step) if part is None else near_far(self.chunks[step], part)
        return self.works[self.chunks[step][0]].at[first, second, 1, half, :, cols]

    def hop(self, step, half, number):
        role = self.role
        place = (role.y, role.z)
        one, two = half, 1 - half
        p, s = place[one], place[two]
        nxt, prv, opp = (p + 1) % 4, (p + 3) % 4, (p + 2) % 4
        snx, spv, sop = (s + 1) % 4, (s + 3) % 4, (s + 2) % 4
        every, low, high = slice(None), pl.ds(0, 2), pl.ds(2, 2)
        src, dst = (
            ((opp, low, None), (2, low, None)),
            ((opp, high, None), (2, high, None)),
            ((nxt, every, None), (0, every, None)),
            ((prv, every, None), (1, every, None)),
            ((p, sop, 0), (3, 0, 0)),
            ((p, sop, 1), (3, 1, 1)),
            ((p, snx, None), (3, 2, None)),
            ((p, spv, None), (3, 3, None)),
        )[number]
        axis = one if number < 4 else two
        at = (step * 2 + half) * N_SCATTER + 1 + number
        return remote(
            self.piece(step, half, *src),
            self.spot(step, half, *dst),
            (self.sem.rs_send.at[at], self.sem.rs_recv.at[at]),
            role.along(axis, 1 if number % 2 == 0 else -1),
        )

    def swapped(self, step, half):
        which = self.chunks[step][0]
        at = step * 2 + half
        return remote(
            self.grads[which].at[self.role.y, self.role.z, self.role.c, half, :, self.cols(step)],
            self.swaps[which].at[half, :, self.cols(step)],
            (self.sem.rs_swap_send.at[at], self.sem.rs_swap_recv.at[at]),
            self.role.swap(),
        )

    def add_core(self, step):
        self.core_copy(step).wait_recv()
        which = self.chunks[step][0]
        cols, c = self.cols(step), self.role.c
        grad, work = self.grads[which], self.works[which]

        @pl.loop(0, 16)
        def _(at):
            y, z = at // 4, at % 4
            grad[y, z, c, :, :, cols] = grad[y, z, c, :, :, cols] + work[y, z, 0, :, :, cols]

    def level(self, step, half, number):
        role = self.role
        place = (role.y, role.z)
        one, two = half, 1 - half
        p, s = place[one], place[two]
        nxt, prv = (p + 1) % 4, (p + 3) % 4
        snx, spv = (s + 1) % 4, (s + 3) % 4
        which = self.chunks[step][0]
        if number > 0:
            self.hop(step, half, 2 * number - 2).wait_recv()
            self.hop(step, half, 2 * number - 1).wait_recv()

        def add(there, *spots):
            total = there[...].astype(F32)
            for spot in spots:
                total = total + spot[...].astype(F32)
            there[...] = total.astype(BF)

        if number == 1:
            for i in range(2):
                add(self.piece(step, half, nxt, i), self.spot(step, half, 2, i))
                add(self.piece(step, half, prv, 2 + i), self.spot(step, half, 2, 2 + i))
        elif number == 2:
            for i in range(4):
                add(self.piece(step, half, p, i), self.spot(step, half, 0, i), self.spot(step, half, 1, i))
        elif number == 3:
            add(self.piece(step, half, p, snx, 0), self.spot(step, half, 3, 0, 0))
            add(self.piece(step, half, p, spv, 1), self.spot(step, half, 3, 1, 1))
        elif number == 4:
            here = self.piece(step, half, p, s)
            total = here[...].astype(F32)
            for i in (2, 3):
                total = total + self.spot(step, half, 3, i)[...].astype(F32)

            @pl.when(role.native)
            def _():
                self.outs[which][half, :, self.cols(step)] = total

            @pl.when(jnp.logical_not(role.native))
            def _():
                here[...] = total.astype(BF)
                self.swapped(step, half).start()

        if number < 4:
            self.hop(step, half, 2 * number).start()
            self.hop(step, half, 2 * number + 1).start()

    def run(self):
        count = len(self.chunks)
        for step in range(count):
            which = self.chunks[step][0]
            if step == 0 or self.chunks[step - 1][0] != which:
                self.wait_free(which)
            self.core_copy(step).start()
        for tick in range(count + 4):
            for number in range(4, -1, -1):
                step = tick - number
                if 0 <= step < count:
                    if number == 0:
                        self.add_core(step)
                    for half in (0, 1):
                        self.level(step, half, number)

    def finish(self):
        role = self.role

        @pl.when(jnp.logical_not(role.native))
        def _():
            for step in range(len(self.chunks)):
                which = self.chunks[step][0]
                for half in (0, 1):
                    self.swapped(step, half).wait()
                    self.outs[which][half, :, self.cols(step)] = self.swaps[which][half, :, self.cols(step)].astype(F32)

        for step in range(len(self.chunks)):
            self.core_copy(step).wait_send()
            for half in (0, 1):
                for number in range(8):
                    self.hop(step, half, number).wait_send()


class Rows:
    def __init__(self, role, which, source, out, sem):
        self.role, self.which, self.source, self.out, self.sem = role, which, source, out, sem
        self.source_x = (3, 0)[which]
        self.holds = role.x == self.source_x

    def copies(self, m):
        role, rows = self.role, SEQ // LAYERS
        made = []
        for section in range(LAYERS):
            target_x, target_c = 2 * (section // 2) + role.c, section % 2
            src = self.source.at[m, pl.ds(section * rows, rows)]
            at = (self.which * MICRO + m) * LAYERS + section
            arrival = self.which * MICRO + m
            here = jnp.logical_and(target_x == self.source_x, target_c == role.c)
            far = remote(
                src, self.out.at[m], (self.sem.row_send.at[at], self.sem.row_recv.at[arrival]), role.dev(target_x, role.y, role.z, target_c)
            )
            near = pltpu.make_async_copy(src, self.out.at[m], self.sem.row_local.at[arrival])
            made.append((here, far, near))
        return made

    def start(self, m):
        @pl.when(self.holds)
        def _():
            for here, far, near in self.copies(m):
                pl.when(here)(near.start)
                pl.when(jnp.logical_not(here))(far.start)

    def sent(self, m):
        @pl.when(self.holds)
        def _():
            for here, far, near in self.copies(m):
                pl.when(here)(near.wait)
                pl.when(jnp.logical_not(here))(far.wait_send)

    def arrived(self, m):
        kept = jnp.logical_and(self.holds, (self.role.x // 2) * 2 + self.role.c == self.role.x)
        kept = jnp.logical_and(kept, self.role.x_lo == self.role.c)

        @pl.when(jnp.logical_not(kept))
        def _():
            self.copies(m)[0][1].wait_recv()


def decoder_kernel(*refs):
    names = [name for name, _, _ in SCRATCH]
    s1, s2, s3, act_in, o1, o2, o3, final_out, start_out = refs[:9]
    b, sem = Bufs(), Bufs()
    rest = list(refs[9:])
    for name in names:
        setattr(b, name, rest.pop(0))
    swaps = [rest.pop(0) for _ in range(3)]
    for name, _ in SEMAPHORES:
        setattr(sem, name, rest.pop(0))
    free = rest.pop(0)

    role = Role()
    x, y, z, c = role.x, role.y, role.z, role.c
    peers = [role.along(0, 1), role.along(0, -1), role.along(1, 1), role.along(1, -1)]
    for away in range(4):
        for other in range(2):
            if (away, other) != (0, 0):
                peers.append(role.dev((x + away) % 4, y, z, (c + other) % 2))
    greet(peers)

    gather_weights(role, (s1, s2, s3), (b.w1, b.w2, b.w3), act_in, b, sem)
    read_gains(b)
    first, last = x == 0, x == LAYERS - 1

    @pl.when(first)
    def _():
        b.hb[...] = b.act[:, 0:SEQ]

    @pl.when(last)
    def _():
        b.gb[...] = b.act[:, 0:SEQ]

    def relay(which, m):
        dst, there = ((b.hb, (x + 1) % 4), (b.gb, (x + 3) % 4))[which]
        at = which * MICRO + m
        return remote(b.ho.at[m], dst.at[m], (sem.relay_send.at[at], sem.relay_recv.at[at]), role.dev(there, y, z, c))

    early = jnp.logical_or(jnp.logical_not(first), c == 1)

    @pl.when(early)
    def _():
        transpose_down(b)

    @pl.when(jnp.logical_not(first))
    def _():
        transpose_up(b)

    final_rows = Rows(role, 0, b.ho, final_out, sem)
    start_rows = Rows(role, 1, b.ho, start_out, sem)

    @pl.loop(0, MICRO)
    def _(m):
        pl.when(jnp.logical_not(first))(lambda: relay(0, m).wait_recv())
        for phase in FORWARD:
            phase(b, m)
        pl.when(jnp.logical_not(last))(lambda: relay(0, m).start())
        final_rows.start(m)

    @pl.when(jnp.logical_not(early))
    def _():
        transpose_down(b)

    @pl.when(first)
    def _():
        transpose_up(b)

    scatter = Scatter(role, (b.g1, b.g2, b.g3), (b.w1, b.w2, b.w3), swaps, (o1, o2, o3), sem, free)

    @pl.loop(0, MICRO)
    def _(m):
        pl.when(jnp.logical_not(last))(lambda: relay(1, m).wait_recv())
        for phase in BACKWARD[:-1]:
            phase(b, m)
        pl.when(jnp.logical_not(last))(lambda: relay(0, m).wait_send())
        final_rows.sent(m)
        BACKWARD[-1](b, m)
        pl.when(jnp.logical_not(first))(lambda: relay(1, m).start())
        start_rows.start(m)

    for which in (2, 1, 0):
        scatter.say_free(which)
    grads_down(b)
    grads_up(b)
    grads_first(b)
    scatter.run()
    scatter.finish()
    for m in range(MICRO):
        pl.when(jnp.logical_not(first))(lambda: relay(1, m).wait_send())
        start_rows.sent(m)
        final_rows.arrived(m)
        start_rows.arrived(m)


def decoder(s1, s2, s3, act):
    hbm = pl.BlockSpec(memory_space=pl.ANY)
    vmem = pl.BlockSpec(memory_space=pltpu.VMEM)
    shapes = [s.shape for s in (s1, s2, s3)]
    rows = SEQ // LAYERS
    return pl.pallas_call(
        decoder_kernel,
        out_shape=[jax.ShapeDtypeStruct(shape, F32) for shape in shapes]
        + [jax.ShapeDtypeStruct((MICRO, rows, D), BF)] * 2,
        in_specs=[hbm] * 4,
        out_specs=[vmem] * 3 + [hbm] * 2,
        scratch_shapes=[pltpu.VMEM(shape, dtype) for _, shape, dtype in SCRATCH]
        + [pltpu.VMEM(shape, BF) for shape in shapes]
        + [pltpu.SemaphoreType.DMA((count,)) for _, count in SEMAPHORES]
        + [pltpu.SemaphoreType.REGULAR((3,))],
        compiler_params=pltpu.CompilerParams(collective_id=0, has_side_effects=True, vmem_limit_bytes=63 << 20),
        name="decoder_step",
    )(s1, s2, s3, act)


def body(
    inputs, cotangent, lengths, attn_gain, w_query, w_key, w_value, w_out, ffn_gain, w_up, w_down
):
    role = Role()
    gains = jnp.pad(jnp.stack([attn_gain, ffn_gain], axis=1), ((0, 0), (0, HD - 2)))
    first = jnp.concatenate([w_query, w_key, w_value, gains, w_out], axis=1).astype(BF).reshape(2, 16, W1)
    second = w_up.astype(BF).reshape(2, 16, FF)
    third = w_down.astype(BF).reshape(2, 64, D)
    rows = jnp.where(role.x < 2, inputs[:, 0], cotangent[:, 0])
    lengths_rows = jnp.broadcast_to(lengths.astype(BF)[:, :, None], (MICRO, 16, D))
    act = jnp.concatenate([rows, lengths_rows], axis=1)
    o1, o2, o3, final_rows, input_rows = decoder(first, second, third, act)
    o1 = o1.reshape(32, W1)
    return (
        final_rows[:, None],
        input_rows[:, None],
        o1[:, D + 2 * HD],
        o1[:, :D],
        o1[:, D : D + HD],
        o1[:, D + HD : D + 2 * HD],
        o1[:, W1 - D :],
        o1[:, D + 2 * HD + 1],
        o2.reshape(32, FF),
        o3.reshape(128, D),
    )


def solution(mesh):
    both_axes = P(("section", "dp"))
    both_rows = P(("section", "dp"), None)
    acts = P(None, "dp", None, None)
    outs = P(None, "dp", "section", None)
    weights = (both_axes, both_rows, both_rows, both_rows, both_rows, both_axes, both_rows, both_rows)
    return jax.shard_map(
        body,
        mesh=mesh,
        in_specs=(acts, acts, P(None, "dp")) + weights,
        out_specs=(outs, outs) + weights,
        check_vma=False,
    )
```

```python
import functools

import jax
import jax.numpy as jnp
from jax import lax
from jax.experimental import pallas as pl
from jax.experimental.pallas import tpu as pltpu
from jax.sharding import PartitionSpec as P

D = 1024
HEADS = 8
HD = 128
FF = 4096
LAYERS = 4
SEQ = 128
MICRO = 2
NORM_EPS = 1e-06
NEG_FILL = -1000000000.0
W1 = D + 2 * HD + HD + D
BF = jnp.bfloat16
F32 = jnp.float32
MESH = pl.DeviceIdType.MESH


class Role:
    def __init__(self):
        section = lax.axis_index("section")
        dp = lax.axis_index("dp")
        self.c = section % 2
        self.x_lo = dp % 2
        self.x = (section // 2) * 2 + self.x_lo
        self.z = (dp // 2) % 4
        self.y = dp // 8
        self.native = self.c == self.x_lo

    def dev(self, x, y, z, c):
        return ((x // 2) * 2 + c, (y * 4 + z) * 2 + x % 2)

    def along(self, axis, step):
        if axis == 0:
            return self.dev(self.x, (self.y + step + 4) % 4, self.z, self.c)
        return self.dev(self.x, self.y, (self.z + step + 4) % 4, self.c)

    def partner(self):
        return self.dev(self.x, self.y, self.z, 1 - self.c)

    def swap(self):
        return self.dev(self.x + 1 - 2 * self.x_lo, self.y, self.z, 1 - self.c)


def remote(src, dst, sems, device):
    return pltpu.make_async_remote_copy(
        src_ref=src, dst_ref=dst, send_sem=sems[0], recv_sem=sems[1], device_id=device, device_id_type=MESH
    )


def greet(devices):
    for device in devices:
        pl.semaphore_signal(pltpu.get_barrier_semaphore(), inc=1, device_id=device, device_id_type=MESH)


class Bufs:
    pass


SCRATCH = (
    ("w1", (4, 4, 2, 2, 16, W1), BF),
    ("w2", (4, 4, 2, 2, 16, FF), BF),
    ("w3", (4, 4, 2, 2, 64, D), BF),
    ("g1", (4, 4, 2, 2, 16, W1), BF),
    ("g2", (4, 4, 2, 2, 16, FF), BF),
    ("g3", (4, 4, 2, 2, 64, D), BF),
    ("act", (MICRO, SEQ, D), BF),
    ("lens", (MICRO, 16, HD), BF),
    ("lens_own", (MICRO, 16, HD), BF),
    ("hb", (MICRO, SEQ, D), BF),
    ("gb", (MICRO, SEQ, D), BF),
    ("ho", (MICRO, SEQ, D), BF),
    ("xa", (MICRO, SEQ, D), BF),
    ("qkv", (MICRO, SEQ, D + 2 * HD), BF),
    ("probs", (MICRO, HEADS * SEQ, SEQ), F32),
    ("mixed", (MICRO, SEQ, D), BF),
    ("after", (MICRO, SEQ, D), F32),
    ("xf", (MICRO, SEQ, D), BF),
    ("u", (MICRO, SEQ, FF), BF),
    ("dp", (MICRO, SEQ, FF), BF),
    ("gf", (MICRO, SEQ, D), BF),
    ("dx", (SEQ, D), F32),
    ("dr", (SEQ, D), F32),
    ("ga", (MICRO, SEQ, D), BF),
    ("do", (SEQ, D), BF),
    ("dqkv", (MICRO, SEQ, D + 2 * HD), BF),
    ("gains", (8, D), F32),
    ("gain_sums", (2, MICRO, 8, D), F32),
)


def dot(left, right):
    return jnp.dot(left, right, preferred_element_type=F32)


def dot_nt(left, right):
    return lax.dot_general(left, right, (((1,), (1,)), ((), ())), preferred_element_type=F32)


def dot_tn(left, right):
    return lax.dot_general(left, right, (((0,), (0,)), ((), ())), preferred_element_type=F32)


def dot_w(weight, value):
    return jnp.transpose(dot(weight, jnp.transpose(value)))


def rms_factor(values):
    return lax.rsqrt(jnp.mean(values * values, axis=-1, keepdims=True) + NORM_EPS)


def norm_back(grad_normed, normed, factor):
    return factor * (grad_normed - normed * jnp.mean(grad_normed * normed, axis=-1, keepdims=True))


def tile(at, wide):
    return pl.ds(pl.multiple_of(at * wide, wide), wide)


def heads_down(value):
    return jnp.concatenate([value[:, h * HD : (h + 1) * HD] for h in range(HEADS)], axis=0)


def heads_across(value):
    return jnp.concatenate([value[h * SEQ : (h + 1) * SEQ] for h in range(HEADS)], axis=1)


def pad_column(lens, m):
    length = lens[m, 0:1, 0:1].astype(F32)
    positions = lax.broadcasted_iota(jnp.int32, (SEQ, 1), 0).astype(F32)
    return jnp.where(positions < length, 1.0, 0.0)


def read_gains(b):
    for start in range(4):
        block = b.w1[start, :, :, :, :, D + 2 * HD : D + 3 * HD].reshape(D // 4, HD).astype(F32)
        b.gains[:, start * 256 : (start + 1) * 256] = jnp.transpose(block)[0:8]


def transpose_down(b):
    @pl.loop(0, 4)
    def _(n):
        b.g2[:, :, :, :, :, tile(n, D)] = jnp.transpose(b.w3[n].reshape(D, D)).reshape(4, 4, 2, 2, 16, D)


def transpose_up(b):
    @pl.loop(0, 4)
    def _(n):
        b.g3[n] = jnp.transpose(b.w2[:, :, :, :, :, tile(n, D)].reshape(D, D)).reshape(4, 2, 2, 64, D)


def forward_qkv(b, m):
    hidden = b.hb[m].astype(F32)
    b.xa[m] = (hidden * rms_factor(hidden) * b.gains[0:1, :]).astype(BF)

    wide = D + 2 * HD
    b.qkv[m] = dot(b.xa[m], b.w1[:, :, :, :, :, 0:wide].reshape(D, wide)).astype(BF)


def forward_attention(b, m):
    length = b.lens[m, 0:1, 0:1].astype(F32)
    rows = lax.broadcasted_iota(jnp.int32, (SEQ, SEQ), 0)
    columns = lax.broadcasted_iota(jnp.int32, (SEQ, SEQ), 1)
    allowed = jnp.logical_and(columns <= rows, columns.astype(F32) < length)
    keys_all = b.qkv[m, :, D : D + HD]
    values_all = b.qkv[m, :, D + HD : D + 2 * HD]
    scores = dot_nt(heads_down(b.qkv[m, :, 0:D]), keys_all) * HD ** (-0.5)
    scores = jnp.where(allowed[None], scores.reshape(HEADS, SEQ, SEQ), NEG_FILL)
    raised = jnp.exp(scores - jnp.max(scores, axis=-1, keepdims=True))
    probs = (raised / jnp.sum(raised, axis=-1, keepdims=True)).reshape(HEADS * SEQ, SEQ)
    b.probs[m] = probs
    b.mixed[m] = heads_across(dot(probs.astype(BF), values_all)).astype(BF)


def forward_out(b, m):
    pad = pad_column(b.lens, m)

    w = b.w1[:, :, :, :, :, W1 - D :].reshape(D, D)
    b.after[m] = b.hb[m].astype(F32) + pad * dot(b.mixed[m], w)

    after = b.after[m]
    b.xf[m] = (after * rms_factor(after) * b.gains[1:2, :]).astype(BF)


def forward_up(b, m):
    a = dot(b.xf[m], b.w2[...].reshape(D, FF))
    sigmoid = 1.0 / (1.0 + jnp.exp(-a))
    b.u[m] = (a * sigmoid).astype(BF)
    b.dp[m] = (sigmoid * (1.0 + a * (1.0 - sigmoid))).astype(BF)


def forward_down(b, m):
    pad = pad_column(b.lens, m)

    b.ho[m] = (b.after[m] + pad * dot(b.u[m], b.w3[...].reshape(FF, D))).astype(BF)


def backward_act(b, m):
    pad = pad_column(b.lens, m)
    b.gf[m] = (b.gb[m].astype(F32) * pad).astype(BF)

    b.dp[m] = (dot(b.gf[m], b.g2[...].reshape(D, FF)) * b.dp[m].astype(F32)).astype(BF)


def backward_up(b, m):
    b.dx[...] = dot(b.dp[m], b.g3[...].reshape(FF, D))


def backward_ffn_norm(b, m):
    pad = pad_column(b.lens, m)
    after = b.after[m]
    factor = rms_factor(after)
    normed = after * factor
    d_xf = b.dx[...]
    b.gain_sums[1, m] = jnp.sum((d_xf * normed).reshape(SEQ // 8, 8, D), axis=0)
    d_r = b.gb[m].astype(F32) + norm_back(d_xf * b.gains[1:2, :], normed, factor)
    b.dr[...] = d_r
    b.ga[m] = (d_r * pad).astype(BF)


def backward_out(b, m):
    b.do[...] = dot_w(b.w1[:, :, :, :, :, W1 - D :].reshape(D, D), b.ga[m]).astype(BF)


def backward_attention(b, m):
    scale = HD ** (-0.5)
    d_mixed = heads_down(b.do[...])
    keys_all = b.qkv[m, :, D : D + HD]
    values_all = b.qkv[m, :, D + HD : D + 2 * HD]
    probs = b.probs[m]
    d_p = dot_nt(d_mixed, values_all)
    b.dqkv[m, :, D + HD : D + 2 * HD] = dot_tn(probs.astype(BF), d_mixed).astype(BF)
    d_s = (probs * (d_p - jnp.sum(probs * d_p, axis=-1, keepdims=True))).astype(BF)
    b.dqkv[m, :, 0:D] = heads_across(dot(d_s, keys_all) * scale).astype(BF)
    b.dqkv[m, :, D : D + HD] = (dot_tn(d_s, heads_down(b.qkv[m, :, 0:D])) * scale).astype(BF)


def backward_qkv(b, m):
    wide = D + 2 * HD
    b.dx[...] = dot_w(b.w1[:, :, :, :, :, 0:wide].reshape(D, wide), b.dqkv[m])


def backward_in(b, m):
    hidden = b.hb[m].astype(F32)
    factor = rms_factor(hidden)
    normed = hidden * factor
    d_xa = b.dx[...]
    b.gain_sums[0, m] = jnp.sum((d_xa * normed).reshape(SEQ // 8, 8, D), axis=0)
    b.ho[m] = (b.dr[...] + norm_back(d_xa * b.gains[0:1, :], normed, factor)).astype(BF)


def both(ref, cols):
    return ref[:, :, cols].reshape(MICRO * SEQ, -1)


def grads_down(b):
    left = b.u[...].reshape(MICRO * SEQ, FF)
    b.g3[...] = dot_tn(left, b.gf[...].reshape(MICRO * SEQ, D)).astype(BF).reshape(4, 4, 2, 2, 64, D)


def grads_up(b):
    right = b.dp[...].reshape(MICRO * SEQ, FF)
    b.g2[...] = dot_tn(b.xf[...].reshape(MICRO * SEQ, D), right).astype(BF).reshape(4, 4, 2, 2, 16, FF)


def grads_first(b):
    wide = D + 2 * HD

    left = b.xa[...].reshape(MICRO * SEQ, D)
    b.g1[:, :, :, :, :, 0:wide] = dot_tn(left, b.dqkv[...].reshape(MICRO * SEQ, wide)).astype(BF).reshape(4, 4, 2, 2, 16, wide)
    left = b.mixed[...].reshape(MICRO * SEQ, D)
    b.g1[:, :, :, :, :, W1 - D :] = dot_tn(left, b.ga[...].reshape(MICRO * SEQ, D)).astype(BF).reshape(4, 4, 2, 2, 16, D)

    lines = [jnp.sum(b.gain_sums[k, 0] + b.gain_sums[k, 1], axis=0, keepdims=True) for k in range(2)]
    sums = jnp.concatenate(lines + [jnp.zeros((HD - 2, D), F32)], axis=0)
    for n in range(4):
        block = jnp.transpose(sums[:, n * 256 : (n + 1) * 256]).astype(BF)
        b.g1[n, :, :, :, :, D + 2 * HD : D + 3 * HD] = block.reshape(4, 2, 2, 16, HD)


FORWARD = (forward_qkv, forward_attention, forward_out, forward_up, forward_down)
BACKWARD = (
    backward_act,
    backward_up,
    backward_ffn_norm,
    backward_out,
    backward_attention,
    backward_qkv,
    backward_in,
)


N_GATHER = 12
N_SCATTER = 9
GATHER_CHUNKS = ((0, 0, 1280), (0, 1280, 1152), (1, 0, 2048), (1, 2048, 2048), (2, 0, 512), (2, 512, 512))
SCATTER_CHUNKS = ((1, 0, 2048), (1, 2048, 2048), (2, 0, 512), (2, 512, 512), (0, 0, 1280), (0, 1280, 1152))
RING = 3
SEMAPHORES = (
    ("send", RING * 2 * N_GATHER),
    ("recv", 6 * 2 * N_GATHER),
    ("swap_send", 12),
    ("swap_recv", 12),
    ("local", 9),
    ("relay_send", 2 * MICRO),
    ("relay_recv", 2 * MICRO),
    ("row_send", 2 * MICRO * LAYERS),
    ("row_recv", 2 * MICRO),
    ("row_local", 2 * MICRO),
)


def near_far(chunk, part):
    which, start, wide = chunk
    near = (wide // HD + 1) // 2 * HD
    return pl.ds(start, near) if part == 0 else pl.ds(start + near, wide - near)


class Gather:
    ARRIVE = ((), (0, 1), (2, 3), (4, 5), (6, 7), (8, 9, 10, 11))
    LEAVE = ((0, 1), (2, 3), (4, 5, 8), (6, 7, 9, 10), (11,), ())

    def __init__(self, role, shards, fulls, acts, act, lens_own, lens, sem):
        self.role, self.shards, self.fulls, self.sem = role, shards, fulls, sem
        self.acts, self.act, self.lens_own, self.lens = acts, act, lens_own, lens
        self.chunks = GATHER_CHUNKS

    def own_copies(self, step, owner):
        role = self.role
        which, start, wide = self.chunks[step]
        src = self.shards[which].at[:, :, pl.ds(start, wide)]
        dst = self.fulls[which].at[role.y, role.z, owner, :, :, pl.ds(start, wide)]
        return (
            remote(src, dst, (self.sem.swap_send.at[step], self.sem.swap_recv.at[step]), role.swap()),
            pltpu.make_async_copy(src, dst, self.sem.local.at[step]),
        )

    def extra_copies(self):
        made = []
        for at, (src, dst) in enumerate(((self.acts[0], self.act), (self.acts[1], self.act), (self.lens_own, self.lens))):
            at = len(self.chunks) + (0 if at < 2 else 1)
            made.append(
                (
                    remote(src, dst, (self.sem.swap_send.at[at], self.sem.swap_recv.at[at]), self.role.swap()),
                    pltpu.make_async_copy(src, dst, self.sem.local.at[at]),
                )
            )
        return made

    def open(self):
        role = self.role

        def each(kind, act):
            for step in range(len(self.chunks)):
                getattr(self.own_copies(step, role.c if kind else 1 - role.c)[kind], act)()
            extra = self.extra_copies()
            pl.when(role.x < 2)(lambda: getattr(extra[0][kind], act)())
            pl.when(role.x >= 2)(lambda: getattr(extra[1][kind], act)())
            getattr(extra[2][kind], act)()

        pl.when(role.native)(lambda: each(1, "start"))
        pl.when(jnp.logical_not(role.native))(lambda: each(0, "start"))

    def close_extra(self):
        role = self.role
        extra = self.extra_copies()
        for kind, native in ((1, role.native), (0, jnp.logical_not(role.native))):

            @pl.when(native)
            def _():
                extra[0][kind].wait()
                extra[2][kind].wait()

    def hop(self, step, half, number):
        role = self.role
        which, start, wide = self.chunks[step]
        place = (role.y, role.z)
        one, two = half, 1 - half
        p, s = place[one], place[two]
        nxt, prv = (p + 1) % 4, (p + 3) % 4
        snx, spv, sop = (s + 1) % 4, (s + 3) % 4, (s + 2) % 4
        every, low, high = slice(None), pl.ds(0, 2), pl.ds(2, 2)
        first, second, part, axis = (
            (p, s, None, one),
            (p, s, None, one),
            (prv, s, 0, one),
            (nxt, s, 1, one),
            (every, s, None, two),
            (every, s, None, two),
            (low, spv, None, two),
            (high, snx, None, two),
            (every, s, None, None),
            (every, spv, None, None),
            (every, snx, None, None),
            (every, sop, None, None),
        )[number]
        device = role.partner() if axis is None else role.along(axis, 1 if number % 2 == 0 else -1)
        cols = pl.ds(start, wide) if part is None else near_far(self.chunks[step], part)
        index = (first, second) if half == 0 else (second, first)
        view = self.fulls[which].at[index[0], index[1], role.c, half, :, cols]
        at = (step % RING * 2 + half) * N_GATHER + number
        to = (step * 2 + half) * N_GATHER + number
        return remote(view, view, (self.sem.send.at[at], self.sem.recv.at[to]), device)

    def level(self, step, number):
        role = self.role
        if number == 0:
            pl.when(role.native)(lambda: self.own_copies(step, role.c)[1].wait())
            pl.when(jnp.logical_not(role.native))(lambda: self.own_copies(step, 1 - role.c)[0].wait())
        for half in (0, 1):
            for hop in self.ARRIVE[number]:
                self.hop(step, half, hop).wait_recv()
            for hop in self.LEAVE[number]:
                if step >= RING:
                    self.hop(step - RING, half, hop).wait_send()
                self.hop(step, half, hop).start()

    def run(self, hooks):
        count = len(self.chunks)
        for tick in range(count + 5):
            for number in range(6):
                step = tick - number
                if 0 <= step < count:
                    self.level(step, number)
            if tick - 5 in hooks:
                hooks[tick - 5]()

    def finish(self):
        for step in range(len(self.chunks) - RING, len(self.chunks)):
            for half in (0, 1):
                for number in range(N_GATHER):
                    self.hop(step, half, number).wait_send()


class Scatter:
    def __init__(self, role, grads, works, swaps, outs, sem, free):
        self.role, self.grads, self.works, self.swaps, self.outs = role, grads, works, swaps, outs
        self.sem, self.free = sem, free
        self.chunks = SCATTER_CHUNKS
        self.peers = [role.along(0, 1), role.along(0, -1), role.along(1, 1), role.along(1, -1), role.partner()]

    def say_free(self, which):
        for device in self.peers:
            pl.semaphore_signal(self.free.at[which], inc=1, device_id=device, device_id_type=MESH)

    def wait_free(self, which):
        pl.semaphore_wait(self.free.at[which], len(self.peers))

    def cols(self, step):
        which, start, wide = self.chunks[step]
        return pl.ds(start, wide)

    def core_copy(self, step):
        which = self.chunks[step][0]
        at = step % RING * 2 * N_SCATTER
        to = step * 2 * N_SCATTER
        return remote(
            self.grads[which].at[:, :, 1 - self.role.c, :, :, self.cols(step)],
            self.works[which].at[:, :, 0, :, :, self.cols(step)],
            (self.sem.send.at[at], self.sem.recv.at[to]),
            self.role.partner(),
        )

    def piece(self, step, half, first, second, part=None):
        index = (first, second) if half == 0 else (second, first)
        cols = self.cols(step) if part is None else near_far(self.chunks[step], part)
        return self.grads[self.chunks[step][0]].at[index[0], index[1], self.role.c, half, :, cols]

    def spot(self, step, half, first, second, part=None):
        cols = self.cols(step) if part is None else near_far(self.chunks[step], part)
        return self.works[self.chunks[step][0]].at[first, second, 1, half, :, cols]

    def hop(self, step, half, number):
        role = self.role
        place = (role.y, role.z)
        one, two = half, 1 - half
        p, s = place[one], place[two]
        nxt, prv, opp = (p + 1) % 4, (p + 3) % 4, (p + 2) % 4
        snx, spv, sop = (s + 1) % 4, (s + 3) % 4, (s + 2) % 4
        every, low, high = slice(None), pl.ds(0, 2), pl.ds(2, 2)
        src, dst = (
            ((opp, low, None), (2, low, None)),
            ((opp, high, None), (2, high, None)),
            ((nxt, every, None), (0, every, None)),
            ((prv, every, None), (1, every, None)),
            ((p, sop, 0), (3, 0, 0)),
            ((p, sop, 1), (3, 1, 1)),
            ((p, snx, None), (3, 2, None)),
            ((p, spv, None), (3, 3, None)),
        )[number]
        axis = one if number < 4 else two
        at = (step % RING * 2 + half) * N_SCATTER + 1 + number
        to = (step * 2 + half) * N_SCATTER + 1 + number
        return remote(
            self.piece(step, half, *src),
            self.spot(step, half, *dst),
            (self.sem.send.at[at], self.sem.recv.at[to]),
            role.along(axis, 1 if number % 2 == 0 else -1),
        )

    def swapped(self, step, half):
        which = self.chunks[step][0]
        at = step * 2 + half
        return remote(
            self.grads[which].at[self.role.y, self.role.z, self.role.c, half, :, self.cols(step)],
            self.swaps[which].at[half, :, self.cols(step)],
            (self.sem.swap_send.at[at], self.sem.swap_recv.at[at]),
            self.role.swap(),
        )

    def add_core(self, step):
        self.core_copy(step).wait_recv()
        which = self.chunks[step][0]
        cols, c = self.cols(step), self.role.c
        grad, work = self.grads[which], self.works[which]

        @pl.loop(0, 16)
        def _(at):
            y, z = at // 4, at % 4
            grad[y, z, c, :, :, cols] = grad[y, z, c, :, :, cols] + work[y, z, 0, :, :, cols]

    def level(self, step, half, number):
        role = self.role
        place = (role.y, role.z)
        one, two = half, 1 - half
        p, s = place[one], place[two]
        nxt, prv = (p + 1) % 4, (p + 3) % 4
        snx, spv = (s + 1) % 4, (s + 3) % 4
        which = self.chunks[step][0]
        if number > 0:
            self.hop(step, half, 2 * number - 2).wait_recv()
            self.hop(step, half, 2 * number - 1).wait_recv()

        def add(there, *spots):
            total = there[...].astype(F32)
            for spot in spots:
                total = total + spot[...].astype(F32)
            there[...] = total.astype(BF)

        if number == 1:
            for i in range(2):
                add(self.piece(step, half, nxt, i), self.spot(step, half, 2, i))
                add(self.piece(step, half, prv, 2 + i), self.spot(step, half, 2, 2 + i))
        elif number == 2:
            for i in range(4):
                add(self.piece(step, half, p, i), self.spot(step, half, 0, i), self.spot(step, half, 1, i))
        elif number == 3:
            add(self.piece(step, half, p, snx, 0), self.spot(step, half, 3, 0, 0))
            add(self.piece(step, half, p, spv, 1), self.spot(step, half, 3, 1, 1))
        elif number == 4:
            here = self.piece(step, half, p, s)
            total = here[...].astype(F32)
            for i in (2, 3):
                total = total + self.spot(step, half, 3, i)[...].astype(F32)

            @pl.when(role.native)
            def _():
                self.outs[which][half, :, self.cols(step)] = total

            @pl.when(jnp.logical_not(role.native))
            def _():
                here[...] = total.astype(BF)
                self.swapped(step, half).start()

        if number < 4:
            for hop in (2 * number, 2 * number + 1):
                if step >= RING:
                    self.hop(step - RING, half, hop).wait_send()
                self.hop(step, half, hop).start()

    def core(self, which):
        self.wait_free(which)
        for step, chunk in enumerate(self.chunks):
            if chunk[0] == which:
                if step >= RING:
                    self.core_copy(step - RING).wait_send()
                self.core_copy(step).start()

    def enter(self, step):
        self.add_core(step)
        for half in (0, 1):
            self.level(step, half, 0)

    def leave(self, step):
        which = self.chunks[step][0]

        @pl.when(jnp.logical_not(self.role.native))
        def _():
            for half in (0, 1):
                self.swapped(step, half).wait()
                self.outs[which][half, :, self.cols(step)] = self.swaps[which][half, :, self.cols(step)].astype(F32)

    def run(self, start):
        count = len(self.chunks)
        for tick in range(count + 5):
            for number in range(1, 6):
                step = tick - number + 1
                if number == 1 and start <= tick + 1 < count:
                    self.enter(tick + 1)
                if not 0 <= step < count:
                    continue
                if number == 5:
                    self.leave(step)
                else:
                    for half in (0, 1):
                        self.level(step, half, number)

    def finish(self):
        count = len(self.chunks)
        for step in range(count - RING, count):
            self.core_copy(step).wait_send()
            for half in (0, 1):
                for number in range(8):
                    self.hop(step, half, number).wait_send()


class Rows:
    def __init__(self, role, which, source, out, sem):
        self.role, self.which, self.source, self.out, self.sem = role, which, source, out, sem
        self.source_x = (3, 0)[which]
        self.holds = role.x == self.source_x

    def copies(self, m):
        role, rows = self.role, SEQ // LAYERS
        made = []
        for section in range(LAYERS):
            target_x, target_c = 2 * (section // 2) + role.c, section % 2
            src = self.source.at[m, pl.ds(section * rows, rows)]
            at = (self.which * MICRO + m) * LAYERS + section
            arrival = self.which * MICRO + m
            here = jnp.logical_and(target_x == self.source_x, target_c == role.c)
            far = remote(
                src, self.out.at[m], (self.sem.row_send.at[at], self.sem.row_recv.at[arrival]), role.dev(target_x, role.y, role.z, target_c)
            )
            near = pltpu.make_async_copy(src, self.out.at[m], self.sem.row_local.at[arrival])
            made.append((here, far, near))
        return made

    def start(self, m):
        @pl.when(self.holds)
        def _():
            for here, far, near in self.copies(m):
                pl.when(here)(near.start)
                pl.when(jnp.logical_not(here))(far.start)

    def sent(self, m):
        @pl.when(self.holds)
        def _():
            for here, far, near in self.copies(m):
                pl.when(here)(near.wait)
                pl.when(jnp.logical_not(here))(far.wait_send)

    def arrived(self, m):
        kept = jnp.logical_and(self.holds, (self.role.x // 2) * 2 + self.role.c == self.role.x)
        kept = jnp.logical_and(kept, self.role.x_lo == self.role.c)

        @pl.when(jnp.logical_not(kept))
        def _():
            self.copies(m)[0][1].wait_recv()


def load_shards(role, weights, lengths, stages, b, sem):
    w_query, w_key, w_value, w_out, attn_gain, ffn_gain, w_up, w_down = weights
    rows = D // 32
    pairs = [
        (w_query, b.dx.at[0:rows]),
        (w_out, b.dx.at[rows : 2 * rows]),
        (w_key, b.probs.at[0, 0:rows]),
        (w_value, b.probs.at[0, rows : 2 * rows]),
    ]
    pairs += [(w_up.at[:, pl.ds(n * D, D)], b.after.at[1, n * rows : (n + 1) * rows]) for n in range(4)]
    pairs += [(w_down, b.after.at[0])]
    copies = [pltpu.make_async_copy(src, dst, sem.local.at[at]) for at, (src, dst) in enumerate(pairs)]
    for copy in copies:
        copy.start()

    for copy in copies:
        copy.wait()
    first, second, third = stages
    down = lax.broadcasted_iota(jnp.int32, (rows, rows), 0)
    across = lax.broadcasted_iota(jnp.int32, (rows, rows), 1)

    def column(gain):
        line = jnp.broadcast_to(gain[...].reshape(1, rows), (rows, rows))
        return jnp.sum(jnp.where(down == across, line, 0.0), axis=1, keepdims=True)

    lane = lax.broadcasted_iota(jnp.int32, (rows, HD), 1)
    gains = jnp.where(lane == 0, column(attn_gain), jnp.where(lane == 1, column(ffn_gain), 0.0))
    first[:, :, 0:D] = b.dx[0:rows].astype(BF).reshape(2, 16, D)
    first[:, :, D : D + HD] = b.probs[0, 0:rows].astype(BF).reshape(2, 16, HD)
    first[:, :, D + HD : D + 2 * HD] = b.probs[0, rows : 2 * rows].astype(BF).reshape(2, 16, HD)
    first[:, :, D + 2 * HD : D + 3 * HD] = gains.astype(BF).reshape(2, 16, HD)
    first[:, :, W1 - D :] = b.dx[rows : 2 * rows].astype(BF).reshape(2, 16, D)
    for n in range(4):
        second[:, :, n * D : (n + 1) * D] = b.after[1, n * rows : (n + 1) * rows].astype(BF).reshape(2, 16, D)
    third[...] = b.after[0].astype(BF).reshape(2, 64, D)
    for m in range(MICRO):
        b.lens_own[m] = jnp.broadcast_to(lengths[m : m + 1, 0:1].astype(F32), (16, HD)).astype(BF)


def decoder_kernel(*refs):
    inputs, cotangent, lengths = refs[:3]
    weights = refs[3:11]
    o1, o2, o3, final_out, start_out = refs[11:16]
    b, sem = Bufs(), Bufs()
    rest = list(refs[16:])
    for name, _, _ in SCRATCH:
        setattr(b, name, rest.pop(0))
    swaps = [rest.pop(0) for _ in range(3)]
    for name, _ in SEMAPHORES:
        setattr(sem, name, rest.pop(0))
    free = rest.pop(0)
    turn = rest.pop(0)

    role = Role()
    x, y, z, c = role.x, role.y, role.z, role.c
    first, last = x == 0, x == LAYERS - 1
    later, before_last = jnp.logical_not(first), jnp.logical_not(last)
    peers = [role.along(0, 1), role.along(0, -1), role.along(1, 1), role.along(1, -1)]
    for away in range(4):
        for other in range(2):
            if (away, other) != (0, 0):
                peers.append(role.dev((x + away) % 4, y, z, (c + other) % 2))
    greet(peers)
    load_shards(role, weights, lengths, swaps, b, sem)
    pl.semaphore_wait(pltpu.get_barrier_semaphore(), len(peers))

    gather = Gather(role, swaps, (b.w1, b.w2, b.w3), (inputs, cotangent), b.act, b.lens_own, b.lens, sem)

    def with_first():
        gather.close_extra()
        read_gains(b)

        @pl.when(last)
        def _():
            b.gb[...] = b.act[...]

        @pl.when(first)
        def _():
            b.hb[...] = b.act[...]

            @pl.loop(0, MICRO)
            def _(m):
                for phase in FORWARD[:3]:
                    phase(b, m)

    def with_up():
        @pl.when(first)
        def _():
            @pl.loop(0, MICRO)
            def _(m):
                forward_up(b, m)

    gather.open()
    ends = [max(step for step, chunk in enumerate(gather.chunks) if chunk[0] == which) for which in range(3)]
    gather.run({ends[0]: with_first, ends[1]: with_up})
    gather.finish()

    def relay(which, m):
        dst, there = ((b.hb, (x + 1) % 4), (b.gb, (x + 3) % 4))[which]
        at = which * MICRO + m
        return remote(b.ho.at[m], dst.at[m], (sem.relay_send.at[at], sem.relay_recv.at[at]), role.dev(there, y, z, c))

    final_rows = Rows(role, 0, b.ho, final_out, sem)
    start_rows = Rows(role, 1, b.ho, start_out, sem)

    @pl.when(jnp.logical_or(later, c == 1))
    def _():
        transpose_down(b)

    pl.when(later)(lambda: transpose_up(b))

    @pl.loop(0, MICRO)
    def _(m):
        @pl.when(later)
        def _():
            relay(0, m).wait_recv()
            for phase in FORWARD[:4]:
                phase(b, m)

        forward_down(b, m)

        @pl.when(jnp.logical_and(first, jnp.logical_and(m == MICRO - 1, c == 1)))
        def _():
            pl.semaphore_wait(turn, 1)

        pl.when(before_last)(lambda: relay(0, m).start())
        final_rows.start(m)

        @pl.when(jnp.logical_and(first, m == 0))
        def _():
            pl.when(c == 0)(lambda: transpose_down(b))
            transpose_up(b)

    @pl.when(jnp.logical_and(first, c == 0))
    def _():
        relay(0, MICRO - 1).wait_send()
        pl.semaphore_signal(turn, inc=1, device_id=role.partner(), device_id_type=MESH)

    scatter = Scatter(role, (b.g1, b.g2, b.g3), (b.w1, b.w2, b.w3), swaps, (o1, o2, o3), sem, free)
    scatter.say_free(1)
    scatter.say_free(2)

    def up_made():
        grads_up(b)
        scatter.core(1)

    def down_made():
        grads_down(b)
        scatter.core(2)

    @pl.loop(0, MICRO)
    def _(m):
        ahead = jnp.logical_and(first, m == MICRO - 1)
        pl.when(before_last)(lambda: relay(1, m).wait_recv())
        backward_act(b, m)
        pl.when(ahead)(up_made)
        backward_up(b, m)
        pl.when(ahead)(down_made)
        backward_ffn_norm(b, m)
        backward_out(b, m)
        backward_attention(b, m)
        backward_qkv(b, m)
        held = jnp.logical_and(before_last, jnp.logical_or(later, jnp.logical_or(c == 1, m < MICRO - 1)))
        pl.when(held)(lambda: relay(0, m).wait_send())
        final_rows.sent(m)
        backward_in(b, m)
        pl.when(later)(lambda: relay(1, m).start())
        start_rows.start(m)

    scatter.say_free(0)

    @pl.when(later)
    def _():
        up_made()
        down_made()

    scatter.enter(0)
    scatter.enter(1)
    grads_first(b)
    scatter.core(0)
    scatter.run(2)
    scatter.finish()
    for m in range(MICRO):
        pl.when(later)(lambda: relay(1, m).wait_send())
        start_rows.sent(m)
        final_rows.arrived(m)
        start_rows.arrived(m)


HBM = pl.BlockSpec(memory_space=pl.ANY)
IN_VMEM = pl.BlockSpec(memory_space=pltpu.VMEM)


def decoder(inputs, cotangent, lengths, weights):
    shapes = [(2, 16, W1), (2, 16, FF), (2, 64, D)]
    rows = SEQ // LAYERS
    return pl.pallas_call(
        decoder_kernel,
        out_shape=[jax.ShapeDtypeStruct(shape, F32) for shape in shapes]
        + [jax.ShapeDtypeStruct((MICRO, rows, D), BF)] * 2,
        in_specs=[HBM, HBM, IN_VMEM] + [HBM] * 4 + [IN_VMEM] * 2 + [HBM] * 2,
        out_specs=[IN_VMEM] * 3 + [HBM] * 2,
        scratch_shapes=[pltpu.VMEM(shape, dtype) for _, shape, dtype in SCRATCH]
        + [pltpu.VMEM(shape, BF) for shape in shapes]
        + [pltpu.SemaphoreType.DMA((count,)) for _, count in SEMAPHORES]
        + [pltpu.SemaphoreType.REGULAR((3,)), pltpu.SemaphoreType.REGULAR],
        compiler_params=pltpu.CompilerParams(collective_id=0, has_side_effects=True, vmem_limit_bytes=63 << 20),
        name="decoder_step",
    )(inputs, cotangent, lengths, *weights)


def deliver_kernel(o1, o2, o3, final_in, start_in, *rest):
    final_out, start_out, attn_gain, w_query, w_key, w_value, w_out, ffn_gain, w_up, w_down = rest
    final_out[...] = final_in[...]
    start_out[...] = start_in[...]
    w_query[...] = o1[:, :, 0:D]
    w_key[...] = o1[:, :, D : D + HD]
    w_value[...] = o1[:, :, D + HD : D + 2 * HD]
    w_out[...] = o1[:, :, W1 - D :]
    w_up[...] = o2[...]
    w_down[...] = o3[...]
    rows = D // 32
    down = lax.broadcasted_iota(jnp.int32, (rows, rows), 0)
    across = lax.broadcasted_iota(jnp.int32, (rows, rows), 1)
    columns = o1[:, :, D + 2 * HD : D + 3 * HD].reshape(rows, HD)
    for at, gain in ((0, attn_gain), (1, ffn_gain)):
        wide = jnp.broadcast_to(columns[:, at : at + 1], (rows, rows))
        gain[...] = jnp.sum(jnp.where(down == across, wide, 0.0), axis=0)


def deliver(o1, o2, o3, final_rows, start_rows):
    shapes = [
        (final_rows.shape, BF),
        (start_rows.shape, BF),
        ((32,), F32),
        ((2, 16, D), F32),
        ((2, 16, HD), F32),
        ((2, 16, HD), F32),
        ((2, 16, D), F32),
        ((32,), F32),
        ((2, 16, FF), F32),
        ((2, 64, D), F32),
    ]
    return pl.pallas_call(
        deliver_kernel,
        out_shape=[jax.ShapeDtypeStruct(shape, dtype) for shape, dtype in shapes],
        in_specs=[IN_VMEM] * 5,
        out_specs=[IN_VMEM] * len(shapes),
        name="deliver",
    )(o1, o2, o3, final_rows, start_rows)


def body(
    inputs, cotangent, lengths, attn_gain, w_query, w_key, w_value, w_out, ffn_gain, w_up, w_down
):
    weights = (w_query, w_key, w_value, w_out, attn_gain, ffn_gain, w_up, w_down)
    made = deliver(*decoder(inputs[:, 0], cotangent[:, 0], lengths, weights))
    final_rows, start_rows, g_attn, g_query, g_key, g_value, g_out, g_ffn, g_up, g_down = made
    return (
        final_rows[:, None],
        start_rows[:, None],
        g_attn,
        g_query.reshape(32, D),
        g_key.reshape(32, HD),
        g_value.reshape(32, HD),
        g_out.reshape(32, D),
        g_ffn,
        g_up.reshape(32, FF),
        g_down.reshape(128, D),
    )


def solution(mesh):
    both_axes = P(("section", "dp"))
    both_rows = P(("section", "dp"), None)
    acts = P(None, "dp", None, None)
    outs = P(None, "dp", "section", None)
    weights = (both_axes, both_rows, both_rows, both_rows, both_rows, both_axes, both_rows, both_rows)
    return jax.shard_map(
        body,
        mesh=mesh,
        in_specs=(acts, acts, P(None, "dp")) + weights,
        out_specs=(outs, outs) + weights,
        check_vma=False,
    )
```

```python
import functools

import jax
import jax.numpy as jnp
from jax import lax
from jax.experimental import pallas as pl
from jax.experimental.pallas import tpu as pltpu
from jax.sharding import PartitionSpec as P

D = 1024
HEADS = 8
HD = 128
FF = 4096
LAYERS = 4
SEQ = 128
MICRO = 2
NORM_EPS = 1e-06
NEG_FILL = -1000000000.0
W1 = D + 2 * HD + HD + D
BF = jnp.bfloat16
F32 = jnp.float32
MESH = pl.DeviceIdType.MESH


class Role:
    def __init__(self):
        section = lax.axis_index("section")
        dp = lax.axis_index("dp")
        self.c = section % 2
        self.x_lo = dp % 2
        self.x = (section // 2) * 2 + self.x_lo
        self.z = (dp // 2) % 4
        self.y = dp // 8
        self.native = self.c == self.x_lo

    def dev(self, x, y, z, c):
        return ((x // 2) * 2 + c, (y * 4 + z) * 2 + x % 2)

    def along(self, axis, step):
        if axis == 0:
            return self.dev(self.x, (self.y + step + 4) % 4, self.z, self.c)
        return self.dev(self.x, self.y, (self.z + step + 4) % 4, self.c)

    def partner(self):
        return self.dev(self.x, self.y, self.z, 1 - self.c)

    def swap(self):
        return self.dev(self.x + 1 - 2 * self.x_lo, self.y, self.z, 1 - self.c)


def remote(src, dst, sems, device):
    return pltpu.make_async_remote_copy(
        src_ref=src, dst_ref=dst, send_sem=sems[0], recv_sem=sems[1], device_id=device, device_id_type=MESH
    )


def greet(devices):
    for device in devices:
        pl.semaphore_signal(pltpu.get_barrier_semaphore(), inc=1, device_id=device, device_id_type=MESH)


class Bufs:
    pass


SCRATCH = (
    ("w1", (4, 4, 2, 2, 16, W1), BF),
    ("w2", (4, 4, 2, 2, 16, FF), BF),
    ("w3", (4, 4, 2, 2, 64, D), BF),
    ("g1", (4, 4, 2, 2, 16, W1), BF),
    ("g2", (4, 4, 2, 2, 16, FF), BF),
    ("g3", (4, 4, 2, 2, 64, D), BF),
    ("act", (MICRO, SEQ, D), BF),
    ("lens", (MICRO, 16, HD), BF),
    ("lens_own", (MICRO, 16, HD), BF),
    ("hb", (MICRO, SEQ, D), BF),
    ("gb", (MICRO, SEQ, D), BF),
    ("ho", (MICRO, SEQ, D), BF),
    ("xa", (MICRO, SEQ, D), BF),
    ("qkv", (MICRO, SEQ, D + 2 * HD), BF),
    ("probs", (MICRO, HEADS * SEQ, SEQ), F32),
    ("mixed", (MICRO, SEQ, D), BF),
    ("after", (MICRO, SEQ, D), F32),
    ("xf", (MICRO, SEQ, D), BF),
    ("u", (MICRO, SEQ, FF), BF),
    ("dp", (MICRO, SEQ, FF), BF),
    ("gf", (MICRO, SEQ, D), BF),
    ("dx", (SEQ, D), F32),
    ("dr", (SEQ, D), F32),
    ("ga", (MICRO, SEQ, D), BF),
    ("do", (SEQ, D), BF),
    ("dqkv", (MICRO, SEQ, D + 2 * HD), BF),
    ("gains", (8, D), F32),
    ("gain_sums", (2, MICRO, 8, D), F32),
)


def dot(left, right):
    return jnp.dot(left, right, preferred_element_type=F32)


def dot_nt(left, right):
    return lax.dot_general(left, right, (((1,), (1,)), ((), ())), preferred_element_type=F32)


def dot_tn(left, right):
    return lax.dot_general(left, right, (((0,), (0,)), ((), ())), preferred_element_type=F32)


def dot_w(weight, value):
    return jnp.transpose(dot(weight, jnp.transpose(value)))


def rms_factor(values):
    return lax.rsqrt(jnp.mean(values * values, axis=-1, keepdims=True) + NORM_EPS)


def norm_back(grad_normed, normed, factor):
    return factor * (grad_normed - normed * jnp.mean(grad_normed * normed, axis=-1, keepdims=True))


def tile(at, wide):
    return pl.ds(pl.multiple_of(at * wide, wide), wide)


def heads_down(value):
    return jnp.concatenate([value[:, h * HD : (h + 1) * HD] for h in range(HEADS)], axis=0)


def heads_across(value):
    return jnp.concatenate([value[h * SEQ : (h + 1) * SEQ] for h in range(HEADS)], axis=1)


def pad_column(lens, m):
    length = lens[m, 0:1, 0:1].astype(F32)
    positions = lax.broadcasted_iota(jnp.int32, (SEQ, 1), 0).astype(F32)
    return jnp.where(positions < length, 1.0, 0.0)


def read_gains(b):
    for start in range(4):
        block = b.w1[start, :, :, :, :, D + 2 * HD : D + 3 * HD].reshape(D // 4, HD).astype(F32)
        b.gains[:, start * 256 : (start + 1) * 256] = jnp.transpose(block)[0:8]


def transpose_down(b):
    @pl.loop(0, 4)
    def _(n):
        b.g2[:, :, :, :, :, tile(n, D)] = jnp.transpose(b.w3[n].reshape(D, D)).reshape(4, 4, 2, 2, 16, D)


def transpose_up(b):
    @pl.loop(0, 4)
    def _(n):
        b.g3[n] = jnp.transpose(b.w2[:, :, :, :, :, tile(n, D)].reshape(D, D)).reshape(4, 2, 2, 64, D)


def forward_qkv(b, m):
    hidden = b.hb[m].astype(F32)
    b.xa[m] = (hidden * rms_factor(hidden) * b.gains[0:1, :]).astype(BF)

    wide = D + 2 * HD
    b.qkv[m] = dot(b.xa[m], b.w1[:, :, :, :, :, 0:wide].reshape(D, wide)).astype(BF)


def forward_attention(b, m):
    length = b.lens[m, 0:1, 0:1].astype(F32)
    rows = lax.broadcasted_iota(jnp.int32, (SEQ, SEQ), 0)
    columns = lax.broadcasted_iota(jnp.int32, (SEQ, SEQ), 1)
    allowed = jnp.logical_and(columns <= rows, columns.astype(F32) < length)
    keys_all = b.qkv[m, :, D : D + HD]
    values_all = b.qkv[m, :, D + HD : D + 2 * HD]
    scores = dot_nt(heads_down(b.qkv[m, :, 0:D]), keys_all) * HD ** (-0.5)
    scores = jnp.where(allowed[None], scores.reshape(HEADS, SEQ, SEQ), NEG_FILL)
    raised = jnp.exp(scores - jnp.max(scores, axis=-1, keepdims=True))
    probs = (raised / jnp.sum(raised, axis=-1, keepdims=True)).reshape(HEADS * SEQ, SEQ)
    b.probs[m] = probs
    b.mixed[m] = heads_across(dot(probs.astype(BF), values_all)).astype(BF)


def forward_out(b, m):
    pad = pad_column(b.lens, m)

    w = b.w1[:, :, :, :, :, W1 - D :].reshape(D, D)
    b.after[m] = b.hb[m].astype(F32) + pad * dot(b.mixed[m], w)

    after = b.after[m]
    b.xf[m] = (after * rms_factor(after) * b.gains[1:2, :]).astype(BF)


def forward_up(b, m):
    a = dot(b.xf[m], b.w2[...].reshape(D, FF))
    sigmoid = 0.5 + 0.5 * jnp.tanh(0.5 * a)
    u = a * sigmoid
    b.u[m] = u.astype(BF)
    b.dp[m] = (sigmoid + u * (1.0 - sigmoid)).astype(BF)


def forward_down(b, m):
    pad = pad_column(b.lens, m)

    b.ho[m] = (b.after[m] + pad * dot(b.u[m], b.w3[...].reshape(FF, D))).astype(BF)


def backward_act(b, m):
    pad = pad_column(b.lens, m)
    b.gf[m] = (b.gb[m].astype(F32) * pad).astype(BF)

    b.dp[m] = (dot(b.gf[m], b.g2[...].reshape(D, FF)) * b.dp[m].astype(F32)).astype(BF)


def backward_up(b, m):
    b.dx[...] = dot(b.dp[m], b.g3[...].reshape(FF, D))


def backward_ffn_norm(b, m):
    pad = pad_column(b.lens, m)
    after = b.after[m]
    factor = rms_factor(after)
    normed = after * factor
    d_xf = b.dx[...]
    b.gain_sums[1, m] = jnp.sum((d_xf * normed).reshape(SEQ // 8, 8, D), axis=0)
    d_r = b.gb[m].astype(F32) + norm_back(d_xf * b.gains[1:2, :], normed, factor)
    b.dr[...] = d_r
    b.ga[m] = (d_r * pad).astype(BF)


def backward_out(b, m):
    b.do[...] = dot_w(b.w1[:, :, :, :, :, W1 - D :].reshape(D, D), b.ga[m]).astype(BF)


def backward_attention(b, m):
    scale = HD ** (-0.5)
    d_mixed = heads_down(b.do[...])
    keys_all = b.qkv[m, :, D : D + HD]
    values_all = b.qkv[m, :, D + HD : D + 2 * HD]
    probs = b.probs[m]
    d_p = dot_nt(d_mixed, values_all)
    b.dqkv[m, :, D + HD : D + 2 * HD] = dot_tn(probs.astype(BF), d_mixed).astype(BF)
    d_s = (probs * (d_p - jnp.sum(probs * d_p, axis=-1, keepdims=True))).astype(BF)
    b.dqkv[m, :, 0:D] = heads_across(dot(d_s, keys_all) * scale).astype(BF)
    b.dqkv[m, :, D : D + HD] = (dot_tn(d_s, heads_down(b.qkv[m, :, 0:D])) * scale).astype(BF)


def backward_qkv(b, m):
    wide = D + 2 * HD
    b.dx[...] = dot_w(b.w1[:, :, :, :, :, 0:wide].reshape(D, wide), b.dqkv[m])


def backward_in(b, m):
    hidden = b.hb[m].astype(F32)
    factor = rms_factor(hidden)
    normed = hidden * factor
    d_xa = b.dx[...]
    b.gain_sums[0, m] = jnp.sum((d_xa * normed).reshape(SEQ // 8, 8, D), axis=0)
    b.ho[m] = (b.dr[...] + norm_back(d_xa * b.gains[0:1, :], normed, factor)).astype(BF)


def both(ref, cols):
    return ref[:, :, cols].reshape(MICRO * SEQ, -1)


def grads_down(b):
    left = b.u[...].reshape(MICRO * SEQ, FF)
    b.g3[...] = dot_tn(left, b.gf[...].reshape(MICRO * SEQ, D)).astype(BF).reshape(4, 4, 2, 2, 64, D)


def grads_up(b, start, end):
    wide = end - start
    right = b.dp[:, :, start:end].reshape(MICRO * SEQ, wide)
    made = dot_tn(b.xf[...].reshape(MICRO * SEQ, D), right).astype(BF)
    b.g2[:, :, :, :, :, start:end] = made.reshape(4, 4, 2, 2, 16, wide)


def grads_first(b):
    wide = D + 2 * HD

    left = b.xa[...].reshape(MICRO * SEQ, D)
    b.g1[:, :, :, :, :, 0:wide] = dot_tn(left, b.dqkv[...].reshape(MICRO * SEQ, wide)).astype(BF).reshape(4, 4, 2, 2, 16, wide)
    left = b.mixed[...].reshape(MICRO * SEQ, D)
    b.g1[:, :, :, :, :, W1 - D :] = dot_tn(left, b.ga[...].reshape(MICRO * SEQ, D)).astype(BF).reshape(4, 4, 2, 2, 16, D)

    lines = [jnp.sum(b.gain_sums[k, 0] + b.gain_sums[k, 1], axis=0, keepdims=True) for k in range(2)]
    sums = jnp.concatenate(lines + [jnp.zeros((HD - 2, D), F32)], axis=0)
    for n in range(4):
        block = jnp.transpose(sums[:, n * 256 : (n + 1) * 256]).astype(BF)
        b.g1[n, :, :, :, :, D + 2 * HD : D + 3 * HD] = block.reshape(4, 2, 2, 16, HD)


FORWARD = (forward_qkv, forward_attention, forward_out, forward_up, forward_down)
BACKWARD = (
    backward_act,
    backward_up,
    backward_ffn_norm,
    backward_out,
    backward_attention,
    backward_qkv,
    backward_in,
)


N_GATHER = 12
N_SCATTER = 9
GATHER_CHUNKS = ((0, 0, 1280), (0, 1280, 1152), (1, 0, 2048), (1, 2048, 2048), (2, 0, 512), (2, 512, 512))
SCATTER_CHUNKS = (
    (1, 0, 1024),
    (1, 1024, 1536),
    (1, 2560, 1536),
    (2, 0, 512),
    (2, 512, 512),
    (0, 0, 1664),
    (0, 1664, 768),
)
RING = 3
SEMAPHORES = (
    ("send", RING * 2 * N_GATHER),
    ("recv", 6 * 2 * N_GATHER),
    ("swap_send", 14),
    ("swap_recv", 14),
    ("local", 9),
    ("relay_send", 2 * MICRO),
    ("relay_recv", 2 * MICRO),
    ("row_send", 2 * MICRO * LAYERS),
    ("row_recv", 2 * MICRO),
    ("row_local", 2 * MICRO),
)


def near_far(chunk, part):
    which, start, wide = chunk
    near = (wide // HD + 1) // 2 * HD
    return pl.ds(start, near) if part == 0 else pl.ds(start + near, wide - near)


class Gather:
    ARRIVE = ((), (0, 1), (2, 3), (4, 5), (6, 7), (8, 9, 10, 11))
    LEAVE = ((0, 1), (2, 3), (4, 5, 8), (6, 7, 9, 10), (11,), ())

    def __init__(self, role, shards, fulls, acts, act, lens_own, lens, sem):
        self.role, self.shards, self.fulls, self.sem = role, shards, fulls, sem
        self.acts, self.act, self.lens_own, self.lens = acts, act, lens_own, lens
        self.chunks = GATHER_CHUNKS

    def own_copies(self, step, owner):
        role = self.role
        which, start, wide = self.chunks[step]
        src = self.shards[which].at[:, :, pl.ds(start, wide)]
        dst = self.fulls[which].at[role.y, role.z, owner, :, :, pl.ds(start, wide)]
        return (
            remote(src, dst, (self.sem.swap_send.at[step], self.sem.swap_recv.at[step]), role.swap()),
            pltpu.make_async_copy(src, dst, self.sem.local.at[step]),
        )

    def extra_copies(self):
        made = []
        for at, (src, dst) in enumerate(((self.acts[0], self.act), (self.acts[1], self.act), (self.lens_own, self.lens))):
            at = len(self.chunks) + (0 if at < 2 else 1)
            made.append(
                (
                    remote(src, dst, (self.sem.swap_send.at[at], self.sem.swap_recv.at[at]), self.role.swap()),
                    pltpu.make_async_copy(src, dst, self.sem.local.at[at]),
                )
            )
        return made

    def open(self):
        role = self.role

        def each(kind, act):
            for step in range(len(self.chunks)):
                getattr(self.own_copies(step, role.c if kind else 1 - role.c)[kind], act)()
            extra = self.extra_copies()
            pl.when(role.x < 2)(lambda: getattr(extra[0][kind], act)())
            pl.when(role.x >= 2)(lambda: getattr(extra[1][kind], act)())
            getattr(extra[2][kind], act)()

        pl.when(role.native)(lambda: each(1, "start"))
        pl.when(jnp.logical_not(role.native))(lambda: each(0, "start"))

    def close_extra(self):
        role = self.role
        extra = self.extra_copies()
        for kind, native in ((1, role.native), (0, jnp.logical_not(role.native))):

            @pl.when(native)
            def _():
                extra[0][kind].wait()
                extra[2][kind].wait()

    def hop(self, step, half, number):
        role = self.role
        which, start, wide = self.chunks[step]
        place = (role.y, role.z)
        one, two = half, 1 - half
        p, s = place[one], place[two]
        nxt, prv = (p + 1) % 4, (p + 3) % 4
        snx, spv, sop = (s + 1) % 4, (s + 3) % 4, (s + 2) % 4
        every, low, high = slice(None), pl.ds(0, 2), pl.ds(2, 2)
        first, second, part, axis = (
            (p, s, None, one),
            (p, s, None, one),
            (prv, s, 0, one),
            (nxt, s, 1, one),
            (every, s, None, two),
            (every, s, None, two),
            (low, spv, None, two),
            (high, snx, None, two),
            (every, s, None, None),
            (every, spv, None, None),
            (every, snx, None, None),
            (every, sop, None, None),
        )[number]
        device = role.partner() if axis is None else role.along(axis, 1 if number % 2 == 0 else -1)
        cols = pl.ds(start, wide) if part is None else near_far(self.chunks[step], part)
        index = (first, second) if half == 0 else (second, first)
        view = self.fulls[which].at[index[0], index[1], role.c, half, :, cols]
        at = (step % RING * 2 + half) * N_GATHER + number
        to = (step * 2 + half) * N_GATHER + number
        return remote(view, view, (self.sem.send.at[at], self.sem.recv.at[to]), device)

    def level(self, step, number):
        role = self.role
        if number == 0:
            pl.when(role.native)(lambda: self.own_copies(step, role.c)[1].wait())
            pl.when(jnp.logical_not(role.native))(lambda: self.own_copies(step, 1 - role.c)[0].wait())
        for half in (0, 1):
            for hop in self.ARRIVE[number]:
                self.hop(step, half, hop).wait_recv()
            for hop in self.LEAVE[number]:
                if step >= RING:
                    self.hop(step - RING, half, hop).wait_send()
                self.hop(step, half, hop).start()

    def run(self, hooks):
        count = len(self.chunks)
        for tick in range(count + 5):
            for number in range(6):
                for step in (2 * tick, 2 * tick + 1) if number == 0 else (tick - number,):
                    if 0 <= step < count:
                        self.level(step, number)
            if tick - 5 in hooks:
                hooks[tick - 5]()

    def finish(self):
        for step in range(len(self.chunks) - RING, len(self.chunks)):
            for half in (0, 1):
                for number in range(N_GATHER):
                    self.hop(step, half, number).wait_send()


class Scatter:
    def __init__(self, role, grads, works, swaps, outs, sem, free):
        self.role, self.grads, self.works, self.swaps, self.outs = role, grads, works, swaps, outs
        self.sem, self.free = sem, free
        self.chunks = SCATTER_CHUNKS
        self.peers = [role.along(0, 1), role.along(0, -1), role.along(1, 1), role.along(1, -1), role.partner()]

    def say_free(self, which):
        for device in self.peers:
            pl.semaphore_signal(self.free.at[which], inc=1, device_id=device, device_id_type=MESH)

    def wait_free(self, which):
        pl.semaphore_wait(self.free.at[which], len(self.peers))

    def cols(self, step):
        which, start, wide = self.chunks[step]
        return pl.ds(start, wide)

    def core_copy(self, step):
        which = self.chunks[step][0]
        at = step % RING * 2 * N_SCATTER
        to = step * 2 * N_SCATTER
        return remote(
            self.grads[which].at[:, :, 1 - self.role.c, :, :, self.cols(step)],
            self.works[which].at[:, :, 0, :, :, self.cols(step)],
            (self.sem.send.at[at], self.sem.recv.at[to]),
            self.role.partner(),
        )

    def piece(self, step, half, first, second, part=None):
        index = (first, second) if half == 0 else (second, first)
        cols = self.cols(step) if part is None else near_far(self.chunks[step], part)
        return self.grads[self.chunks[step][0]].at[index[0], index[1], self.role.c, half, :, cols]

    def spot(self, step, half, first, second, part=None):
        cols = self.cols(step) if part is None else near_far(self.chunks[step], part)
        return self.works[self.chunks[step][0]].at[first, second, 1, half, :, cols]

    def hop(self, step, half, number):
        role = self.role
        place = (role.y, role.z)
        one, two = half, 1 - half
        p, s = place[one], place[two]
        nxt, prv, opp = (p + 1) % 4, (p + 3) % 4, (p + 2) % 4
        snx, spv, sop = (s + 1) % 4, (s + 3) % 4, (s + 2) % 4
        every, low, high = slice(None), pl.ds(0, 2), pl.ds(2, 2)
        src, dst = (
            ((opp, low, None), (2, low, None)),
            ((opp, high, None), (2, high, None)),
            ((nxt, every, None), (0, every, None)),
            ((prv, every, None), (1, every, None)),
            ((p, sop, 0), (3, 0, 0)),
            ((p, sop, 1), (3, 1, 1)),
            ((p, snx, None), (3, 2, None)),
            ((p, spv, None), (3, 3, None)),
        )[number]
        axis = one if number < 4 else two
        at = (step % RING * 2 + half) * N_SCATTER + 1 + number
        to = (step * 2 + half) * N_SCATTER + 1 + number
        return remote(
            self.piece(step, half, *src),
            self.spot(step, half, *dst),
            (self.sem.send.at[at], self.sem.recv.at[to]),
            role.along(axis, 1 if number % 2 == 0 else -1),
        )

    def swapped(self, step, half):
        which = self.chunks[step][0]
        at = step * 2 + half
        return remote(
            self.grads[which].at[self.role.y, self.role.z, self.role.c, half, :, self.cols(step)],
            self.swaps[which].at[half, :, self.cols(step)],
            (self.sem.swap_send.at[at], self.sem.swap_recv.at[at]),
            self.role.swap(),
        )

    def add_core(self, step):
        self.core_copy(step).wait_recv()
        which = self.chunks[step][0]
        cols, c = self.cols(step), self.role.c
        grad, work = self.grads[which], self.works[which]

        @pl.loop(0, 16)
        def _(at):
            y, z = at // 4, at % 4
            grad[y, z, c, :, :, cols] = grad[y, z, c, :, :, cols] + work[y, z, 0, :, :, cols]

    def level(self, step, half, number):
        role = self.role
        place = (role.y, role.z)
        one, two = half, 1 - half
        p, s = place[one], place[two]
        nxt, prv = (p + 1) % 4, (p + 3) % 4
        snx, spv = (s + 1) % 4, (s + 3) % 4
        which = self.chunks[step][0]
        if number > 0:
            self.hop(step, half, 2 * number - 2).wait_recv()
            self.hop(step, half, 2 * number - 1).wait_recv()

        def add(there, *spots):
            total = there[...].astype(F32)
            for spot in spots:
                total = total + spot[...].astype(F32)
            there[...] = total.astype(BF)

        if number == 1:
            for i in range(2):
                add(self.piece(step, half, nxt, i), self.spot(step, half, 2, i))
                add(self.piece(step, half, prv, 2 + i), self.spot(step, half, 2, 2 + i))
        elif number == 2:
            for i in range(4):
                add(self.piece(step, half, p, i), self.spot(step, half, 0, i), self.spot(step, half, 1, i))
        elif number == 3:
            add(self.piece(step, half, p, snx, 0), self.spot(step, half, 3, 0, 0))
            add(self.piece(step, half, p, spv, 1), self.spot(step, half, 3, 1, 1))
        elif number == 4:
            here = self.piece(step, half, p, s)
            total = here[...].astype(F32)
            for i in (2, 3):
                total = total + self.spot(step, half, 3, i)[...].astype(F32)

            @pl.when(role.native)
            def _():
                self.outs[which][half, :, self.cols(step)] = total

            @pl.when(jnp.logical_not(role.native))
            def _():
                here[...] = total.astype(BF)
                self.swapped(step, half).start()

        if number < 4:
            for hop in (2 * number, 2 * number + 1):
                if step >= RING:
                    self.hop(step - RING, half, hop).wait_send()
                self.hop(step, half, hop).start()

    def core(self, *steps):
        for step in steps:
            which = self.chunks[step][0]
            if step == 0 or self.chunks[step - 1][0] != which:
                self.wait_free(which)
            if step >= RING:
                self.core_copy(step - RING).wait_send()
            self.core_copy(step).start()

    def enter(self, step):
        self.add_core(step)
        for half in (0, 1):
            self.level(step, half, 0)

    def pair(self, step, number):
        for half in (0, 1):
            self.level(step, half, number)

    def leave(self, step):
        which = self.chunks[step][0]

        @pl.when(jnp.logical_not(self.role.native))
        def _():
            for half in (0, 1):
                self.swapped(step, half).wait()
                self.outs[which][half, :, self.cols(step)] = self.swaps[which][half, :, self.cols(step)].astype(F32)

    def run(self):
        count = len(self.chunks)
        for tick in range(2, count + 5):
            for number in range(1, 6):
                step = tick - number + 1
                if number == 1 and tick + 1 < count:
                    self.enter(tick + 1)
                if not 0 <= step < count:
                    continue
                if number == 5:
                    self.leave(step)
                else:
                    self.pair(step, number)

    def finish(self):
        count = len(self.chunks)
        for step in range(count - RING, count):
            self.core_copy(step).wait_send()
            for half in (0, 1):
                for number in range(8):
                    self.hop(step, half, number).wait_send()


class Rows:
    def __init__(self, role, which, source, out, sem):
        self.role, self.which, self.source, self.out, self.sem = role, which, source, out, sem
        self.source_x = (3, 0)[which]
        self.holds = role.x == self.source_x

    def copies(self, m):
        role, rows = self.role, SEQ // LAYERS
        made = []
        for section in range(LAYERS):
            target_x, target_c = 2 * (section // 2) + role.c, section % 2
            src = self.source.at[m, pl.ds(section * rows, rows)]
            at = (self.which * MICRO + m) * LAYERS + section
            arrival = self.which * MICRO + m
            here = jnp.logical_and(target_x == self.source_x, target_c == role.c)
            far = remote(
                src, self.out.at[m], (self.sem.row_send.at[at], self.sem.row_recv.at[arrival]), role.dev(target_x, role.y, role.z, target_c)
            )
            near = pltpu.make_async_copy(src, self.out.at[m], self.sem.row_local.at[arrival])
            made.append((here, far, near))
        return made

    def start(self, m):
        @pl.when(self.holds)
        def _():
            for here, far, near in self.copies(m):
                pl.when(here)(near.start)
                pl.when(jnp.logical_not(here))(far.start)

    def sent(self, m):
        @pl.when(self.holds)
        def _():
            for here, far, near in self.copies(m):
                pl.when(here)(near.wait)
                pl.when(jnp.logical_not(here))(far.wait_send)

    def arrived(self, m):
        kept = jnp.logical_and(self.holds, (self.role.x // 2) * 2 + self.role.c == self.role.x)
        kept = jnp.logical_and(kept, self.role.x_lo == self.role.c)

        @pl.when(jnp.logical_not(kept))
        def _():
            self.copies(m)[0][1].wait_recv()


def load_shards(role, weights, lengths, stages, b, sem):
    w_query, w_key, w_value, w_out, attn_gain, ffn_gain, w_up, w_down = weights
    rows = D // 32
    pairs = [
        (w_query, b.dx.at[0:rows]),
        (w_out, b.dx.at[rows : 2 * rows]),
        (w_key, b.probs.at[0, 0:rows]),
        (w_value, b.probs.at[0, rows : 2 * rows]),
    ]
    pairs += [(w_up.at[:, pl.ds(n * D, D)], b.after.at[1, n * rows : (n + 1) * rows]) for n in range(4)]
    pairs += [(w_down, b.after.at[0])]
    copies = [pltpu.make_async_copy(src, dst, sem.local.at[at]) for at, (src, dst) in enumerate(pairs)]
    for copy in copies:
        copy.start()

    for copy in copies:
        copy.wait()
    first, second, third = stages
    down = lax.broadcasted_iota(jnp.int32, (rows, rows), 0)
    across = lax.broadcasted_iota(jnp.int32, (rows, rows), 1)

    def column(gain):
        line = jnp.broadcast_to(gain[...].reshape(1, rows), (rows, rows))
        return jnp.sum(jnp.where(down == across, line, 0.0), axis=1, keepdims=True)

    lane = lax.broadcasted_iota(jnp.int32, (rows, HD), 1)
    gains = jnp.where(lane == 0, column(attn_gain), jnp.where(lane == 1, column(ffn_gain), 0.0))
    first[:, :, 0:D] = b.dx[0:rows].astype(BF).reshape(2, 16, D)
    first[:, :, D : D + HD] = b.probs[0, 0:rows].astype(BF).reshape(2, 16, HD)
    first[:, :, D + HD : D + 2 * HD] = b.probs[0, rows : 2 * rows].astype(BF).reshape(2, 16, HD)
    first[:, :, D + 2 * HD : D + 3 * HD] = gains.astype(BF).reshape(2, 16, HD)
    first[:, :, W1 - D :] = b.dx[rows : 2 * rows].astype(BF).reshape(2, 16, D)
    for n in range(4):
        second[:, :, n * D : (n + 1) * D] = b.after[1, n * rows : (n + 1) * rows].astype(BF).reshape(2, 16, D)
    third[...] = b.after[0].astype(BF).reshape(2, 64, D)
    for m in range(MICRO):
        b.lens_own[m] = jnp.broadcast_to(lengths[m : m + 1, 0:1].astype(F32), (16, HD)).astype(BF)


def decoder_kernel(*refs):
    inputs, cotangent, lengths = refs[:3]
    weights = refs[3:11]
    o1, o2, o3, final_out, start_out = refs[11:16]
    b, sem = Bufs(), Bufs()
    rest = list(refs[16:])
    for name, _, _ in SCRATCH:
        setattr(b, name, rest.pop(0))
    swaps = [rest.pop(0) for _ in range(3)]
    for name, _ in SEMAPHORES:
        setattr(sem, name, rest.pop(0))
    free = rest.pop(0)

    role = Role()
    x, y, z, c = role.x, role.y, role.z, role.c
    first, last = x == 0, x == LAYERS - 1
    later, before_last = jnp.logical_not(first), jnp.logical_not(last)
    peers = [role.along(0, 1), role.along(0, -1), role.along(1, 1), role.along(1, -1)]
    for away in range(4):
        for other in range(2):
            if (away, other) != (0, 0):
                peers.append(role.dev((x + away) % 4, y, z, (c + other) % 2))
    greet(peers)
    load_shards(role, weights, lengths, swaps, b, sem)
    pl.semaphore_wait(pltpu.get_barrier_semaphore(), len(peers))

    gather = Gather(role, swaps, (b.w1, b.w2, b.w3), (inputs, cotangent), b.act, b.lens_own, b.lens, sem)

    def with_first():
        gather.close_extra()
        read_gains(b)

        @pl.when(last)
        def _():
            b.gb[...] = b.act[...]

        @pl.when(first)
        def _():
            b.hb[...] = b.act[...]

            @pl.loop(0, MICRO)
            def _(m):
                for phase in FORWARD[:3]:
                    phase(b, m)

    def with_up():
        @pl.when(first)
        def _():
            @pl.loop(0, MICRO)
            def _(m):
                forward_up(b, m)

    gather.open()
    ends = [max(step for step, chunk in enumerate(gather.chunks) if chunk[0] == which) for which in range(3)]
    gather.run({ends[0]: with_first, ends[1]: with_up})
    gather.finish()

    def relay(which, m):
        dst, there = ((b.hb, (x + 1) % 4), (b.gb, (x + 3) % 4))[which]
        at = which * MICRO + m
        return remote(b.ho.at[m], dst.at[m], (sem.relay_send.at[at], sem.relay_recv.at[at]), role.dev(there, y, z, c))

    final_rows = Rows(role, 0, b.ho, final_out, sem)
    start_rows = Rows(role, 1, b.ho, start_out, sem)

    @pl.when(later)
    def _():
        transpose_down(b)
        transpose_up(b)

    @pl.loop(0, MICRO)
    def _(m):
        @pl.when(later)
        def _():
            relay(0, m).wait_recv()
            for phase in FORWARD[:4]:
                phase(b, m)

        forward_down(b, m)

        pl.when(before_last)(lambda: relay(0, m).start())
        final_rows.start(m)

    @pl.when(first)
    def _():
        transpose_down(b)
        transpose_up(b)

    scatter = Scatter(role, (b.g1, b.g2, b.g3), (b.w1, b.w2, b.w3), swaps, (o1, o2, o3), sem, free)
    scatter.say_free(1)
    scatter.say_free(2)

    def up_made():
        grads_up(b, 0, D)
        scatter.core(0)
        grads_up(b, D, FF)
        scatter.core(1, 2)

    def down_made():
        grads_down(b)
        scatter.core(3, 4)

    @pl.loop(0, MICRO)
    def _(m):
        ahead = jnp.logical_and(first, m == MICRO - 1)
        pl.when(before_last)(lambda: relay(1, m).wait_recv())
        backward_act(b, m)
        pl.when(ahead)(up_made)
        backward_up(b, m)

        @pl.when(ahead)
        def _():
            scatter.enter(0)
            down_made()
            scatter.enter(1)
            scatter.pair(0, 1)

        backward_ffn_norm(b, m)
        backward_out(b, m)
        backward_attention(b, m)
        backward_qkv(b, m)
        pl.when(before_last)(lambda: relay(0, m).wait_send())
        final_rows.sent(m)
        backward_in(b, m)
        pl.when(later)(lambda: relay(1, m).start())
        start_rows.start(m)

    scatter.say_free(0)

    @pl.when(later)
    def _():
        up_made()
        scatter.enter(0)
        down_made()
        scatter.enter(1)
        scatter.pair(0, 1)

    scatter.enter(2)
    scatter.pair(1, 1)
    grads_first(b)
    scatter.core(5, 6)
    scatter.pair(0, 2)
    scatter.run()
    scatter.finish()
    for m in range(MICRO):
        pl.when(later)(lambda: relay(1, m).wait_send())
        start_rows.sent(m)
        final_rows.arrived(m)
        start_rows.arrived(m)


HBM = pl.BlockSpec(memory_space=pl.ANY)
IN_VMEM = pl.BlockSpec(memory_space=pltpu.VMEM)


def decoder(inputs, cotangent, lengths, weights):
    shapes = [(2, 16, W1), (2, 16, FF), (2, 64, D)]
    rows = SEQ // LAYERS
    return pl.pallas_call(
        decoder_kernel,
        out_shape=[jax.ShapeDtypeStruct(shape, F32) for shape in shapes]
        + [jax.ShapeDtypeStruct((MICRO, rows, D), BF)] * 2,
        in_specs=[HBM, HBM, IN_VMEM] + [HBM] * 4 + [IN_VMEM] * 2 + [HBM] * 2,
        out_specs=[IN_VMEM] * 3 + [HBM] * 2,
        scratch_shapes=[pltpu.VMEM(shape, dtype) for _, shape, dtype in SCRATCH]
        + [pltpu.VMEM(shape, BF) for shape in shapes]
        + [pltpu.SemaphoreType.DMA((count,)) for _, count in SEMAPHORES]
        + [pltpu.SemaphoreType.REGULAR((3,))],
        compiler_params=pltpu.CompilerParams(collective_id=0, has_side_effects=True, vmem_limit_bytes=63 << 20),
        name="decoder_step",
    )(inputs, cotangent, lengths, *weights)


def deliver_kernel(o1, o2, o3, final_in, start_in, *rest):
    final_out, start_out, attn_gain, w_query, w_key, w_value, w_out, ffn_gain, w_up, w_down = rest
    final_out[...] = final_in[...]
    start_out[...] = start_in[...]
    w_query[...] = o1[:, :, 0:D]
    w_key[...] = o1[:, :, D : D + HD]
    w_value[...] = o1[:, :, D + HD : D + 2 * HD]
    w_out[...] = o1[:, :, W1 - D :]
    w_up[...] = o2[...]
    w_down[...] = o3[...]
    rows = D // 32
    down = lax.broadcasted_iota(jnp.int32, (rows, rows), 0)
    across = lax.broadcasted_iota(jnp.int32, (rows, rows), 1)
    columns = o1[:, :, D + 2 * HD : D + 3 * HD].reshape(rows, HD)
    for at, gain in ((0, attn_gain), (1, ffn_gain)):
        wide = jnp.broadcast_to(columns[:, at : at + 1], (rows, rows))
        gain[...] = jnp.sum(jnp.where(down == across, wide, 0.0), axis=0)


def deliver(o1, o2, o3, final_rows, start_rows):
    shapes = [
        (final_rows.shape, BF),
        (start_rows.shape, BF),
        ((32,), F32),
        ((2, 16, D), F32),
        ((2, 16, HD), F32),
        ((2, 16, HD), F32),
        ((2, 16, D), F32),
        ((32,), F32),
        ((2, 16, FF), F32),
        ((2, 64, D), F32),
    ]
    return pl.pallas_call(
        deliver_kernel,
        out_shape=[jax.ShapeDtypeStruct(shape, dtype) for shape, dtype in shapes],
        in_specs=[IN_VMEM] * 5,
        out_specs=[IN_VMEM] * len(shapes),
        name="deliver",
    )(o1, o2, o3, final_rows, start_rows)


def body(
    inputs, cotangent, lengths, attn_gain, w_query, w_key, w_value, w_out, ffn_gain, w_up, w_down
):
    weights = (w_query, w_key, w_value, w_out, attn_gain, ffn_gain, w_up, w_down)
    made = deliver(*decoder(inputs[:, 0], cotangent[:, 0], lengths, weights))
    final_rows, start_rows, g_attn, g_query, g_key, g_value, g_out, g_ffn, g_up, g_down = made
    return (
        final_rows[:, None],
        start_rows[:, None],
        g_attn,
        g_query.reshape(32, D),
        g_key.reshape(32, HD),
        g_value.reshape(32, HD),
        g_out.reshape(32, D),
        g_ffn,
        g_up.reshape(32, FF),
        g_down.reshape(128, D),
    )


def solution(mesh):
    both_axes = P(("section", "dp"))
    both_rows = P(("section", "dp"), None)
    acts = P(None, "dp", None, None)
    outs = P(None, "dp", "section", None)
    weights = (both_axes, both_rows, both_rows, both_rows, both_rows, both_axes, both_rows, both_rows)
    return jax.shard_map(
        body,
        mesh=mesh,
        in_specs=(acts, acts, P(None, "dp")) + weights,
        out_specs=(outs, outs) + weights,
        check_vma=False,
    )
```

```python
import functools

import jax
import jax.numpy as jnp
from jax import lax
from jax.experimental import pallas as pl
from jax.experimental.pallas import tpu as pltpu
from jax.sharding import PartitionSpec as P

D = 1024
HEADS = 8
HD = 128
FF = 4096
LAYERS = 4
SEQ = 128
MICRO = 2
NORM_EPS = 1e-06
NEG_FILL = -1000000000.0
W1 = D + 2 * HD + HD + D
BF = jnp.bfloat16
F32 = jnp.float32
MESH = pl.DeviceIdType.MESH


class Role:
    def __init__(self):
        section = lax.axis_index("section")
        dp = lax.axis_index("dp")
        self.c = section % 2
        self.x_lo = dp % 2
        self.x = (section // 2) * 2 + self.x_lo
        self.z = (dp // 2) % 4
        self.y = dp // 8
        self.native = self.c == self.x_lo

    def dev(self, x, y, z, c):
        return ((x // 2) * 2 + c, (y * 4 + z) * 2 + x % 2)

    def along(self, axis, step):
        if axis == 0:
            return self.dev(self.x, (self.y + step + 4) % 4, self.z, self.c)
        return self.dev(self.x, self.y, (self.z + step + 4) % 4, self.c)

    def partner(self):
        return self.dev(self.x, self.y, self.z, 1 - self.c)

    def swap(self):
        return self.dev(self.x + 1 - 2 * self.x_lo, self.y, self.z, 1 - self.c)


def remote(src, dst, sems, device):
    return pltpu.make_async_remote_copy(
        src_ref=src, dst_ref=dst, send_sem=sems[0], recv_sem=sems[1], device_id=device, device_id_type=MESH
    )


def greet(devices):
    for device in devices:
        pl.semaphore_signal(pltpu.get_barrier_semaphore(), inc=1, device_id=device, device_id_type=MESH)


class Bufs:
    pass


SCRATCH = (
    ("w1", (4, 4, 2, 2, 16, W1), BF),
    ("w2", (4, 4, 2, 2, 16, FF), BF),
    ("w3", (4, 4, 2, 2, 64, D), BF),
    ("g1", (4, 4, 2, 2, 16, W1), BF),
    ("g2", (4, 4, 2, 2, 16, FF), BF),
    ("g3", (4, 4, 2, 2, 64, D), BF),
    ("act", (MICRO, SEQ, D), BF),
    ("lens", (MICRO, 16, HD), BF),
    ("lens_own", (MICRO, 16, HD), BF),
    ("hb", (MICRO, SEQ, D), BF),
    ("gb", (MICRO, SEQ, D), BF),
    ("ho", (MICRO, SEQ, D), BF),
    ("xa", (MICRO, SEQ, D), BF),
    ("qkv", (MICRO, SEQ, D + 2 * HD), BF),
    ("probs", (MICRO, HEADS * SEQ, SEQ), F32),
    ("mixed", (MICRO, SEQ, D), BF),
    ("after", (MICRO, SEQ, D), F32),
    ("xf", (MICRO, SEQ, D), BF),
    ("u", (MICRO, SEQ, FF), BF),
    ("dp", (MICRO, SEQ, FF), BF),
    ("gf", (MICRO, SEQ, D), BF),
    ("dx", (SEQ, D), F32),
    ("dr", (SEQ, D), F32),
    ("ga", (MICRO, SEQ, D), BF),
    ("do", (SEQ, D), BF),
    ("dqkv", (MICRO, SEQ, D + 2 * HD), BF),
    ("gains", (8, D), F32),
    ("gain_sums", (2, MICRO, 8, D), F32),
)


def dot(left, right):
    return jnp.dot(left, right, preferred_element_type=F32)


def dot_nt(left, right):
    return lax.dot_general(left, right, (((1,), (1,)), ((), ())), preferred_element_type=F32)


def dot_tn(left, right):
    return lax.dot_general(left, right, (((0,), (0,)), ((), ())), preferred_element_type=F32)


def dot_w(weight, value):
    return jnp.transpose(dot(weight, jnp.transpose(value)))


def rms_factor(values):
    return lax.rsqrt(jnp.mean(values * values, axis=-1, keepdims=True) + NORM_EPS)


def norm_back(grad_normed, normed, factor):
    return factor * (grad_normed - normed * jnp.mean(grad_normed * normed, axis=-1, keepdims=True))


def tile(at, wide):
    return pl.ds(pl.multiple_of(at * wide, wide), wide)


def heads_down(value):
    return jnp.concatenate([value[:, h * HD : (h + 1) * HD] for h in range(HEADS)], axis=0)


def heads_across(value):
    return jnp.concatenate([value[h * SEQ : (h + 1) * SEQ] for h in range(HEADS)], axis=1)


def pad_column(lens, m):
    length = lens[m, 0:1, 0:1].astype(F32)
    positions = lax.broadcasted_iota(jnp.int32, (SEQ, 1), 0).astype(F32)
    return jnp.where(positions < length, 1.0, 0.0)


def read_gains(b):
    for start in range(4):
        block = b.w1[start, :, :, :, :, D + 2 * HD : D + 3 * HD].reshape(D // 4, HD).astype(F32)
        b.gains[:, start * 256 : (start + 1) * 256] = jnp.transpose(block)[0:8]


def transpose_down(b):
    @pl.loop(0, 4)
    def _(n):
        b.g2[:, :, :, :, :, tile(n, D)] = jnp.transpose(b.w3[n].reshape(D, D)).reshape(4, 4, 2, 2, 16, D)


def transpose_up(b):
    @pl.loop(0, 4)
    def _(n):
        b.g3[n] = jnp.transpose(b.w2[:, :, :, :, :, tile(n, D)].reshape(D, D)).reshape(4, 2, 2, 64, D)


def forward_qkv(b, m):
    hidden = b.hb[m].astype(F32)
    b.xa[m] = (hidden * rms_factor(hidden) * b.gains[0:1, :]).astype(BF)

    wide = D + 2 * HD
    b.qkv[m] = dot(b.xa[m], b.w1[:, :, :, :, :, 0:wide].reshape(D, wide)).astype(BF)


def forward_attention(b, m):
    length = b.lens[m, 0:1, 0:1].astype(F32)
    rows = lax.broadcasted_iota(jnp.int32, (SEQ, SEQ), 0)
    columns = lax.broadcasted_iota(jnp.int32, (SEQ, SEQ), 1)
    allowed = jnp.logical_and(columns <= rows, columns.astype(F32) < length)
    keys_all = b.qkv[m, :, D : D + HD]
    values_all = b.qkv[m, :, D + HD : D + 2 * HD]
    scores = dot_nt(heads_down(b.qkv[m, :, 0:D]), keys_all) * HD ** (-0.5)
    scores = jnp.where(allowed[None], scores.reshape(HEADS, SEQ, SEQ), NEG_FILL)
    raised = jnp.exp(scores - jnp.max(scores, axis=-1, keepdims=True))
    probs = (raised / jnp.sum(raised, axis=-1, keepdims=True)).reshape(HEADS * SEQ, SEQ)
    b.probs[m] = probs
    b.mixed[m] = heads_across(dot(probs.astype(BF), values_all)).astype(BF)


def forward_out(b, m):
    pad = pad_column(b.lens, m)

    w = b.w1[:, :, :, :, :, W1 - D :].reshape(D, D)
    b.after[m] = b.hb[m].astype(F32) + pad * dot(b.mixed[m], w)

    after = b.after[m]
    b.xf[m] = (after * rms_factor(after) * b.gains[1:2, :]).astype(BF)


def forward_up(b, m):
    a = dot(b.xf[m], b.w2[...].reshape(D, FF))
    sigmoid = 0.5 + 0.5 * jnp.tanh(0.5 * a)
    u = a * sigmoid
    b.u[m] = u.astype(BF)
    b.dp[m] = (sigmoid + u * (1.0 - sigmoid)).astype(BF)


def forward_down(b, m):
    pad = pad_column(b.lens, m)

    b.ho[m] = (b.after[m] + pad * dot(b.u[m], b.w3[...].reshape(FF, D))).astype(BF)


def backward_act(b, m):
    pad = pad_column(b.lens, m)
    b.gf[m] = (b.gb[m].astype(F32) * pad).astype(BF)

    b.dp[m] = (dot(b.gf[m], b.g2[...].reshape(D, FF)) * b.dp[m].astype(F32)).astype(BF)


def backward_up(b, m):
    b.dx[...] = dot(b.dp[m], b.g3[...].reshape(FF, D))


def backward_ffn_norm(b, m):
    pad = pad_column(b.lens, m)
    after = b.after[m]
    factor = rms_factor(after)
    normed = after * factor
    d_xf = b.dx[...]
    b.gain_sums[1, m] = jnp.sum((d_xf * normed).reshape(SEQ // 8, 8, D), axis=0)
    d_r = b.gb[m].astype(F32) + norm_back(d_xf * b.gains[1:2, :], normed, factor)
    b.dr[...] = d_r
    b.ga[m] = (d_r * pad).astype(BF)


def backward_out(b, m):
    b.do[...] = dot_w(b.w1[:, :, :, :, :, W1 - D :].reshape(D, D), b.ga[m]).astype(BF)


def backward_attention(b, m):
    scale = HD ** (-0.5)
    d_mixed = heads_down(b.do[...])
    keys_all = b.qkv[m, :, D : D + HD]
    values_all = b.qkv[m, :, D + HD : D + 2 * HD]
    probs = b.probs[m]
    d_p = dot_nt(d_mixed, values_all)
    b.dqkv[m, :, D + HD : D + 2 * HD] = dot_tn(probs.astype(BF), d_mixed).astype(BF)
    d_s = (probs * (d_p - jnp.sum(probs * d_p, axis=-1, keepdims=True))).astype(BF)
    b.dqkv[m, :, 0:D] = heads_across(dot(d_s, keys_all) * scale).astype(BF)
    b.dqkv[m, :, D : D + HD] = (dot_tn(d_s, heads_down(b.qkv[m, :, 0:D])) * scale).astype(BF)


def backward_qkv(b, m):
    wide = D + 2 * HD
    b.dx[...] = dot_w(b.w1[:, :, :, :, :, 0:wide].reshape(D, wide), b.dqkv[m])


def backward_in(b, m):
    hidden = b.hb[m].astype(F32)
    factor = rms_factor(hidden)
    normed = hidden * factor
    d_xa = b.dx[...]
    b.gain_sums[0, m] = jnp.sum((d_xa * normed).reshape(SEQ // 8, 8, D), axis=0)
    b.ho[m] = (b.dr[...] + norm_back(d_xa * b.gains[0:1, :], normed, factor)).astype(BF)


def both(ref, cols):
    return ref[:, :, cols].reshape(MICRO * SEQ, -1)


def grads_down(b):
    left = b.u[...].reshape(MICRO * SEQ, FF)
    b.g3[...] = dot_tn(left, b.gf[...].reshape(MICRO * SEQ, D)).astype(BF).reshape(4, 4, 2, 2, 64, D)


def grads_up(b, start, end):
    wide = end - start
    right = b.dp[:, :, start:end].reshape(MICRO * SEQ, wide)
    made = dot_tn(b.xf[...].reshape(MICRO * SEQ, D), right).astype(BF)
    b.g2[:, :, :, :, :, start:end] = made.reshape(4, 4, 2, 2, 16, wide)


def grads_first(b):
    wide = D + 2 * HD

    left = b.xa[...].reshape(MICRO * SEQ, D)
    b.g1[:, :, :, :, :, 0:wide] = dot_tn(left, b.dqkv[...].reshape(MICRO * SEQ, wide)).astype(BF).reshape(4, 4, 2, 2, 16, wide)
    left = b.mixed[...].reshape(MICRO * SEQ, D)
    b.g1[:, :, :, :, :, W1 - D :] = dot_tn(left, b.ga[...].reshape(MICRO * SEQ, D)).astype(BF).reshape(4, 4, 2, 2, 16, D)

    lines = [jnp.sum(b.gain_sums[k, 0] + b.gain_sums[k, 1], axis=0, keepdims=True) for k in range(2)]
    sums = jnp.concatenate(lines + [jnp.zeros((HD - 2, D), F32)], axis=0)
    for n in range(4):
        block = jnp.transpose(sums[:, n * 256 : (n + 1) * 256]).astype(BF)
        b.g1[n, :, :, :, :, D + 2 * HD : D + 3 * HD] = block.reshape(4, 2, 2, 16, HD)


FORWARD = (forward_qkv, forward_attention, forward_out, forward_up, forward_down)
BACKWARD = (
    backward_act,
    backward_up,
    backward_ffn_norm,
    backward_out,
    backward_attention,
    backward_qkv,
    backward_in,
)


N_GATHER = 12
N_SCATTER = 9
GATHER_CHUNKS = ((0, 0, 1280), (0, 1280, 1152), (1, 0, 2048), (1, 2048, 2048), (2, 0, 512), (2, 512, 512))
SCATTER_CHUNKS = (
    (1, 0, 1024),
    (1, 1024, 1536),
    (1, 2560, 1536),
    (2, 0, 512),
    (2, 512, 512),
    (0, 0, 1664),
    (0, 1664, 768),
)
RING = 3
SEMAPHORES = (
    ("send", RING * 2 * N_GATHER),
    ("recv", 6 * 2 * N_GATHER),
    ("swap_send", 14),
    ("swap_recv", 14),
    ("local", 9),
    ("relay_send", 2 * MICRO),
    ("relay_recv", 2 * MICRO),
    ("row_send", 2 * MICRO * LAYERS),
    ("row_recv", 2 * MICRO),
    ("row_local", 2 * MICRO),
)


def near_far(chunk, part):
    which, start, wide = chunk
    near = (wide // HD + 1) // 2 * HD
    return pl.ds(start, near) if part == 0 else pl.ds(start + near, wide - near)


class Gather:
    ARRIVE = ((), (0, 1), (2, 3), (4, 5), (6, 7), (8, 9, 10, 11))
    LEAVE = ((0, 1), (2, 3), (4, 5, 8), (6, 7, 9, 10), (11,), ())

    def __init__(self, role, shards, fulls, acts, act, lens_own, lens, sem):
        self.role, self.shards, self.fulls, self.sem = role, shards, fulls, sem
        self.acts, self.act, self.lens_own, self.lens = acts, act, lens_own, lens
        self.chunks = GATHER_CHUNKS

    def own_copies(self, step, owner):
        role = self.role
        which, start, wide = self.chunks[step]
        src = self.shards[which].at[:, :, pl.ds(start, wide)]
        dst = self.fulls[which].at[role.y, role.z, owner, :, :, pl.ds(start, wide)]
        return (
            remote(src, dst, (self.sem.swap_send.at[step], self.sem.swap_recv.at[step]), role.swap()),
            pltpu.make_async_copy(src, dst, self.sem.local.at[step]),
        )

    def extra_copies(self):
        made = []
        for at, (src, dst) in enumerate(((self.acts[0], self.act), (self.acts[1], self.act), (self.lens_own, self.lens))):
            at = len(self.chunks) + (0 if at < 2 else 1)
            made.append(
                (
                    remote(src, dst, (self.sem.swap_send.at[at], self.sem.swap_recv.at[at]), self.role.swap()),
                    pltpu.make_async_copy(src, dst, self.sem.local.at[at]),
                )
            )
        return made

    def open(self):
        role = self.role

        def each(kind, act):
            for step in range(len(self.chunks)):
                getattr(self.own_copies(step, role.c if kind else 1 - role.c)[kind], act)()
            extra = self.extra_copies()
            pl.when(role.x < 2)(lambda: getattr(extra[0][kind], act)())
            pl.when(role.x >= 2)(lambda: getattr(extra[1][kind], act)())
            getattr(extra[2][kind], act)()

        pl.when(role.native)(lambda: each(1, "start"))
        pl.when(jnp.logical_not(role.native))(lambda: each(0, "start"))

    def close_extra(self):
        role = self.role
        extra = self.extra_copies()
        for kind, native in ((1, role.native), (0, jnp.logical_not(role.native))):

            @pl.when(native)
            def _():
                extra[0][kind].wait()
                extra[2][kind].wait()

    def hop(self, step, half, number):
        role = self.role
        which, start, wide = self.chunks[step]
        place = (role.y, role.z)
        one, two = half, 1 - half
        p, s = place[one], place[two]
        nxt, prv = (p + 1) % 4, (p + 3) % 4
        snx, spv, sop = (s + 1) % 4, (s + 3) % 4, (s + 2) % 4
        every, low, high = slice(None), pl.ds(0, 2), pl.ds(2, 2)
        first, second, part, axis = (
            (p, s, None, one),
            (p, s, None, one),
            (prv, s, 0, one),
            (nxt, s, 1, one),
            (every, s, None, two),
            (every, s, None, two),
            (low, spv, None, two),
            (high, snx, None, two),
            (every, s, None, None),
            (every, spv, None, None),
            (every, snx, None, None),
            (every, sop, None, None),
        )[number]
        device = role.partner() if axis is None else role.along(axis, 1 if number % 2 == 0 else -1)
        cols = pl.ds(start, wide) if part is None else near_far(self.chunks[step], part)
        index = (first, second) if half == 0 else (second, first)
        view = self.fulls[which].at[index[0], index[1], role.c, half, :, cols]
        at = (step % RING * 2 + half) * N_GATHER + number
        to = (step * 2 + half) * N_GATHER + number
        return remote(view, view, (self.sem.send.at[at], self.sem.recv.at[to]), device)

    def level(self, step, number):
        role = self.role
        if number == 0:
            pl.when(role.native)(lambda: self.own_copies(step, role.c)[1].wait())
            pl.when(jnp.logical_not(role.native))(lambda: self.own_copies(step, 1 - role.c)[0].wait())
        for half in (0, 1):
            for hop in self.ARRIVE[number]:
                self.hop(step, half, hop).wait_recv()
            for hop in self.LEAVE[number]:
                if step >= RING:
                    self.hop(step - RING, half, hop).wait_send()
                self.hop(step, half, hop).start()

    def run(self, hooks):
        count = len(self.chunks)
        for tick in range(count + 5):
            for number in range(6):
                for step in (2 * tick, 2 * tick + 1) if number == 0 else (tick - number,):
                    if 0 <= step < count:
                        self.level(step, number)
            if tick - 5 in hooks:
                hooks[tick - 5]()

    def finish(self):
        for step in range(len(self.chunks) - RING, len(self.chunks)):
            for half in (0, 1):
                for number in range(N_GATHER):
                    self.hop(step, half, number).wait_send()


class Scatter:
    def __init__(self, role, grads, works, swaps, outs, sem, free):
        self.role, self.grads, self.works, self.swaps, self.outs = role, grads, works, swaps, outs
        self.sem, self.free = sem, free
        self.chunks = SCATTER_CHUNKS
        self.peers = [role.along(0, 1), role.along(0, -1), role.along(1, 1), role.along(1, -1), role.partner()]

    def say_free(self, which):
        for device in self.peers:
            pl.semaphore_signal(self.free.at[which], inc=1, device_id=device, device_id_type=MESH)

    def wait_free(self, which):
        pl.semaphore_wait(self.free.at[which], len(self.peers))

    def cols(self, step):
        which, start, wide = self.chunks[step]
        return pl.ds(start, wide)

    def core_copy(self, step):
        which = self.chunks[step][0]
        at = step % RING * 2 * N_SCATTER
        to = step * 2 * N_SCATTER
        return remote(
            self.grads[which].at[:, :, 1 - self.role.c, :, :, self.cols(step)],
            self.works[which].at[:, :, 0, :, :, self.cols(step)],
            (self.sem.send.at[at], self.sem.recv.at[to]),
            self.role.partner(),
        )

    def piece(self, step, half, first, second, part=None):
        index = (first, second) if half == 0 else (second, first)
        cols = self.cols(step) if part is None else near_far(self.chunks[step], part)
        return self.grads[self.chunks[step][0]].at[index[0], index[1], self.role.c, half, :, cols]

    def spot(self, step, half, first, second, part=None):
        cols = self.cols(step) if part is None else near_far(self.chunks[step], part)
        return self.works[self.chunks[step][0]].at[first, second, 1, half, :, cols]

    def hop(self, step, half, number):
        role = self.role
        place = (role.y, role.z)
        one, two = half, 1 - half
        p, s = place[one], place[two]
        nxt, prv, opp = (p + 1) % 4, (p + 3) % 4, (p + 2) % 4
        snx, spv, sop = (s + 1) % 4, (s + 3) % 4, (s + 2) % 4
        every, low, high = slice(None), pl.ds(0, 2), pl.ds(2, 2)
        src, dst = (
            ((opp, low, None), (2, low, None)),
            ((opp, high, None), (2, high, None)),
            ((nxt, every, None), (0, every, None)),
            ((prv, every, None), (1, every, None)),
            ((p, sop, 0), (3, 0, 0)),
            ((p, sop, 1), (3, 1, 1)),
            ((p, snx, None), (3, 2, None)),
            ((p, spv, None), (3, 3, None)),
        )[number]
        axis = one if number < 4 else two
        at = (step % RING * 2 + half) * N_SCATTER + 1 + number
        to = (step * 2 + half) * N_SCATTER + 1 + number
        return remote(
            self.piece(step, half, *src),
            self.spot(step, half, *dst),
            (self.sem.send.at[at], self.sem.recv.at[to]),
            role.along(axis, 1 if number % 2 == 0 else -1),
        )

    def swapped(self, step, half):
        which = self.chunks[step][0]
        at = step * 2 + half
        return remote(
            self.grads[which].at[self.role.y, self.role.z, self.role.c, half, :, self.cols(step)],
            self.swaps[which].at[half, :, self.cols(step)],
            (self.sem.swap_send.at[at], self.sem.swap_recv.at[at]),
            self.role.swap(),
        )

    def add_core(self, step):
        self.core_copy(step).wait_recv()
        which = self.chunks[step][0]
        cols, c = self.cols(step), self.role.c
        grad, work = self.grads[which], self.works[which]

        @pl.loop(0, 16)
        def _(at):
            y, z = at // 4, at % 4
            grad[y, z, c, :, :, cols] = grad[y, z, c, :, :, cols] + work[y, z, 0, :, :, cols]

    def level(self, step, half, number):
        role = self.role
        place = (role.y, role.z)
        one, two = half, 1 - half
        p, s = place[one], place[two]
        nxt, prv = (p + 1) % 4, (p + 3) % 4
        snx, spv = (s + 1) % 4, (s + 3) % 4
        which = self.chunks[step][0]
        if number > 0:
            self.hop(step, half, 2 * number - 2).wait_recv()
            self.hop(step, half, 2 * number - 1).wait_recv()

        def add(there, *spots):
            total = there[...].astype(F32)
            for spot in spots:
                total = total + spot[...].astype(F32)
            there[...] = total.astype(BF)

        if number == 1:
            for i in range(2):
                add(self.piece(step, half, nxt, i), self.spot(step, half, 2, i))
                add(self.piece(step, half, prv, 2 + i), self.spot(step, half, 2, 2 + i))
        elif number == 2:
            for i in range(4):
                add(self.piece(step, half, p, i), self.spot(step, half, 0, i), self.spot(step, half, 1, i))
        elif number == 3:
            add(self.piece(step, half, p, snx, 0), self.spot(step, half, 3, 0, 0))
            add(self.piece(step, half, p, spv, 1), self.spot(step, half, 3, 1, 1))
        elif number == 4:
            here = self.piece(step, half, p, s)
            total = here[...].astype(F32)
            for i in (2, 3):
                total = total + self.spot(step, half, 3, i)[...].astype(F32)

            @pl.when(role.native)
            def _():
                self.outs[which][half, :, self.cols(step)] = total

            @pl.when(jnp.logical_not(role.native))
            def _():
                here[...] = total.astype(BF)
                self.swapped(step, half).start()

        if number < 4:
            for hop in (2 * number, 2 * number + 1):
                if step >= RING:
                    self.hop(step - RING, half, hop).wait_send()
                self.hop(step, half, hop).start()

    def core(self, *steps):
        for step in steps:
            which = self.chunks[step][0]
            if step == 0 or self.chunks[step - 1][0] != which:
                self.wait_free(which)
            if step >= RING:
                self.core_copy(step - RING).wait_send()
            self.core_copy(step).start()

    def enter(self, step):
        self.add_core(step)
        for half in (0, 1):
            self.level(step, half, 0)

    def pair(self, step, number):
        for half in (0, 1):
            self.level(step, half, number)

    def leave(self, step):
        which = self.chunks[step][0]

        @pl.when(jnp.logical_not(self.role.native))
        def _():
            for half in (0, 1):
                self.swapped(step, half).wait()
                self.outs[which][half, :, self.cols(step)] = self.swaps[which][half, :, self.cols(step)].astype(F32)

    def run(self):
        count = len(self.chunks)
        for tick in range(2, count + 5):
            for number in range(1, 6):
                step = tick - number + 1
                if number == 1 and tick + 1 < count:
                    self.enter(tick + 1)
                if not 0 <= step < count:
                    continue
                if number == 5:
                    self.leave(step)
                else:
                    self.pair(step, number)

    def finish(self):
        count = len(self.chunks)
        for step in range(count - RING, count):
            self.core_copy(step).wait_send()
            for half in (0, 1):
                for number in range(8):
                    self.hop(step, half, number).wait_send()


class Rows:
    def __init__(self, role, which, source, out, sem):
        self.role, self.which, self.source, self.out, self.sem = role, which, source, out, sem
        self.source_x = (3, 0)[which]
        self.holds = role.x == self.source_x

    def copies(self, m):
        role, rows = self.role, SEQ // LAYERS
        made = []
        for section in range(LAYERS):
            target_x, target_c = 2 * (section // 2) + role.c, section % 2
            src = self.source.at[m, pl.ds(section * rows, rows)]
            at = (self.which * MICRO + m) * LAYERS + section
            arrival = self.which * MICRO + m
            here = jnp.logical_and(target_x == self.source_x, target_c == role.c)
            far = remote(
                src, self.out.at[m], (self.sem.row_send.at[at], self.sem.row_recv.at[arrival]), role.dev(target_x, role.y, role.z, target_c)
            )
            near = pltpu.make_async_copy(src, self.out.at[m], self.sem.row_local.at[arrival])
            made.append((here, far, near))
        return made

    def start(self, m):
        @pl.when(self.holds)
        def _():
            for here, far, near in self.copies(m):
                pl.when(here)(near.start)
                pl.when(jnp.logical_not(here))(far.start)

    def sent(self, m):
        @pl.when(self.holds)
        def _():
            for here, far, near in self.copies(m):
                pl.when(here)(near.wait)
                pl.when(jnp.logical_not(here))(far.wait_send)

    def arrived(self, m):
        kept = jnp.logical_and(self.holds, (self.role.x // 2) * 2 + self.role.c == self.role.x)
        kept = jnp.logical_and(kept, self.role.x_lo == self.role.c)

        @pl.when(jnp.logical_not(kept))
        def _():
            self.copies(m)[0][1].wait_recv()


def load_shards(role, weights, lengths, stages, b, sem):
    w_query, w_key, w_value, w_out, attn_gain, ffn_gain, w_up, w_down = weights
    rows = D // 32
    pairs = [
        (w_query, b.dx.at[0:rows]),
        (w_out, b.dx.at[rows : 2 * rows]),
        (w_key, b.probs.at[0, 0:rows]),
        (w_value, b.probs.at[0, rows : 2 * rows]),
    ]
    pairs += [(w_up.at[:, pl.ds(n * D, D)], b.after.at[1, n * rows : (n + 1) * rows]) for n in range(4)]
    pairs += [(w_down, b.after.at[0])]
    copies = [pltpu.make_async_copy(src, dst, sem.local.at[at]) for at, (src, dst) in enumerate(pairs)]
    for copy in copies:
        copy.start()

    for copy in copies:
        copy.wait()
    first, second, third = stages
    down = lax.broadcasted_iota(jnp.int32, (rows, rows), 0)
    across = lax.broadcasted_iota(jnp.int32, (rows, rows), 1)

    def column(gain):
        line = jnp.broadcast_to(gain[...].reshape(1, rows), (rows, rows))
        return jnp.sum(jnp.where(down == across, line, 0.0), axis=1, keepdims=True)

    lane = lax.broadcasted_iota(jnp.int32, (rows, HD), 1)
    gains = jnp.where(lane == 0, column(attn_gain), jnp.where(lane == 1, column(ffn_gain), 0.0))
    first[:, :, 0:D] = b.dx[0:rows].astype(BF).reshape(2, 16, D)
    first[:, :, D : D + HD] = b.probs[0, 0:rows].astype(BF).reshape(2, 16, HD)
    first[:, :, D + HD : D + 2 * HD] = b.probs[0, rows : 2 * rows].astype(BF).reshape(2, 16, HD)
    first[:, :, D + 2 * HD : D + 3 * HD] = gains.astype(BF).reshape(2, 16, HD)
    first[:, :, W1 - D :] = b.dx[rows : 2 * rows].astype(BF).reshape(2, 16, D)
    for n in range(4):
        second[:, :, n * D : (n + 1) * D] = b.after[1, n * rows : (n + 1) * rows].astype(BF).reshape(2, 16, D)
    third[...] = b.after[0].astype(BF).reshape(2, 64, D)
    for m in range(MICRO):
        b.lens_own[m] = jnp.broadcast_to(lengths[m : m + 1, 0:1].astype(F32), (16, HD)).astype(BF)


def decoder_kernel(*refs):
    inputs, cotangent, lengths = refs[:3]
    weights = refs[3:11]
    o1, o2, o3, final_out, start_out = refs[11:16]
    b, sem = Bufs(), Bufs()
    rest = list(refs[16:])
    for name, _, _ in SCRATCH:
        setattr(b, name, rest.pop(0))
    swaps = [rest.pop(0) for _ in range(3)]
    for name, _ in SEMAPHORES:
        setattr(sem, name, rest.pop(0))
    free = rest.pop(0)

    role = Role()
    x, y, z, c = role.x, role.y, role.z, role.c
    first, last = x == 0, x == LAYERS - 1
    later, before_last = jnp.logical_not(first), jnp.logical_not(last)
    peers = [role.along(0, 1), role.along(0, -1), role.along(1, 1), role.along(1, -1)]
    for away in range(4):
        for other in range(2):
            if (away, other) != (0, 0):
                peers.append(role.dev((x + away) % 4, y, z, (c + other) % 2))
    greet(peers)
    load_shards(role, weights, lengths, swaps, b, sem)
    pl.semaphore_wait(pltpu.get_barrier_semaphore(), len(peers))

    gather = Gather(role, swaps, (b.w1, b.w2, b.w3), (inputs, cotangent), b.act, b.lens_own, b.lens, sem)

    def with_first():
        gather.close_extra()
        read_gains(b)

        @pl.when(last)
        def _():
            b.gb[...] = b.act[...]

        @pl.when(first)
        def _():
            b.hb[...] = b.act[...]

            @pl.loop(0, MICRO)
            def _(m):
                for phase in FORWARD[:3]:
                    phase(b, m)

    def with_up():
        @pl.when(first)
        def _():
            @pl.loop(0, MICRO)
            def _(m):
                forward_up(b, m)

    gather.open()
    ends = [max(step for step, chunk in enumerate(gather.chunks) if chunk[0] == which) for which in range(3)]
    gather.run({ends[0]: with_first, ends[1]: with_up})
    gather.finish()

    def relay(which, m):
        dst, there = ((b.hb, (x + 1) % 4), (b.gb, (x + 3) % 4))[which]
        at = which * MICRO + m
        return remote(b.ho.at[m], dst.at[m], (sem.relay_send.at[at], sem.relay_recv.at[at]), role.dev(there, y, z, c))

    final_rows = Rows(role, 0, b.ho, final_out, sem)
    start_rows = Rows(role, 1, b.ho, start_out, sem)

    @pl.when(later)
    def _():
        transpose_down(b)
        transpose_up(b)

    scatter = Scatter(role, (b.g1, b.g2, b.g3), (b.w1, b.w2, b.w3), swaps, (o1, o2, o3), sem, free)

    def up_made():
        grads_up(b, 0, D)
        scatter.core(0)
        grads_up(b, D, FF)
        scatter.core(1, 2)

    def down_made():
        grads_down(b)
        scatter.core(3, 4)

    def forward(m):
        @pl.when(later)
        def _():
            relay(0, m).wait_recv()
            for phase in FORWARD[:4]:
                phase(b, m)

        forward_down(b, m)
        pl.when(before_last)(lambda: relay(0, m).start())
        final_rows.start(m)

    def backward(m, ahead):
        pl.when(before_last)(lambda: relay(1, m).wait_recv())
        backward_act(b, m)
        pl.when(ahead)(up_made)
        backward_up(b, m)

        @pl.when(ahead)
        def _():
            scatter.enter(0)
            down_made()
            scatter.enter(1)
            scatter.pair(0, 1)

        backward_ffn_norm(b, m)
        backward_out(b, m)
        backward_attention(b, m)
        backward_qkv(b, m)
        pl.when(before_last)(lambda: relay(0, m).wait_send())
        final_rows.sent(m)
        backward_in(b, m)
        pl.when(later)(lambda: relay(1, m).start())
        start_rows.start(m)

    @pl.loop(0, 2 * MICRO)
    def _(turn):
        m = jnp.where(last, turn // 2, turn % 2)
        onward = jnp.where(last, turn % 2, turn // 2) == 0

        @pl.when(jnp.logical_and(first, turn == MICRO))
        def _():
            transpose_down(b)
            transpose_up(b)

        @pl.when(turn == 2 * MICRO - 1)
        def _():
            scatter.say_free(1)
            scatter.say_free(2)

        pl.when(onward)(lambda: forward(m))
        pl.when(jnp.logical_not(onward))(lambda: backward(m, jnp.logical_and(first, turn == 2 * MICRO - 1)))

    scatter.say_free(0)

    @pl.when(later)
    def _():
        up_made()
        scatter.enter(0)
        down_made()
        scatter.enter(1)
        scatter.pair(0, 1)

    scatter.enter(2)
    scatter.pair(1, 1)
    grads_first(b)
    scatter.core(5, 6)
    scatter.pair(0, 2)
    scatter.run()
    scatter.finish()
    for m in range(MICRO):
        pl.when(later)(lambda: relay(1, m).wait_send())
        start_rows.sent(m)
        final_rows.arrived(m)
        start_rows.arrived(m)


HBM = pl.BlockSpec(memory_space=pl.ANY)
IN_VMEM = pl.BlockSpec(memory_space=pltpu.VMEM)


def decoder(inputs, cotangent, lengths, weights):
    shapes = [(2, 16, W1), (2, 16, FF), (2, 64, D)]
    rows = SEQ // LAYERS
    return pl.pallas_call(
        decoder_kernel,
        out_shape=[jax.ShapeDtypeStruct(shape, F32) for shape in shapes]
        + [jax.ShapeDtypeStruct((MICRO, rows, D), BF)] * 2,
        in_specs=[HBM, HBM, IN_VMEM] + [HBM] * 4 + [IN_VMEM] * 2 + [HBM] * 2,
        out_specs=[IN_VMEM] * 3 + [HBM] * 2,
        scratch_shapes=[pltpu.VMEM(shape, dtype) for _, shape, dtype in SCRATCH]
        + [pltpu.VMEM(shape, BF) for shape in shapes]
        + [pltpu.SemaphoreType.DMA((count,)) for _, count in SEMAPHORES]
        + [pltpu.SemaphoreType.REGULAR((3,))],
        compiler_params=pltpu.CompilerParams(collective_id=0, has_side_effects=True, vmem_limit_bytes=63 << 20),
        name="decoder_step",
    )(inputs, cotangent, lengths, *weights)


def deliver_kernel(o1, o2, o3, final_in, start_in, *rest):
    final_out, start_out, attn_gain, w_query, w_key, w_value, w_out, ffn_gain, w_up, w_down = rest
    final_out[...] = final_in[...]
    start_out[...] = start_in[...]
    w_query[...] = o1[:, :, 0:D]
    w_key[...] = o1[:, :, D : D + HD]
    w_value[...] = o1[:, :, D + HD : D + 2 * HD]
    w_out[...] = o1[:, :, W1 - D :]
    w_up[...] = o2[...]
    w_down[...] = o3[...]
    rows = D // 32
    down = lax.broadcasted_iota(jnp.int32, (rows, rows), 0)
    across = lax.broadcasted_iota(jnp.int32, (rows, rows), 1)
    columns = o1[:, :, D + 2 * HD : D + 3 * HD].reshape(rows, HD)
    for at, gain in ((0, attn_gain), (1, ffn_gain)):
        wide = jnp.broadcast_to(columns[:, at : at + 1], (rows, rows))
        gain[...] = jnp.sum(jnp.where(down == across, wide, 0.0), axis=0)


def deliver(o1, o2, o3, final_rows, start_rows):
    shapes = [
        (final_rows.shape, BF),
        (start_rows.shape, BF),
        ((32,), F32),
        ((2, 16, D), F32),
        ((2, 16, HD), F32),
        ((2, 16, HD), F32),
        ((2, 16, D), F32),
        ((32,), F32),
        ((2, 16, FF), F32),
        ((2, 64, D), F32),
    ]
    return pl.pallas_call(
        deliver_kernel,
        out_shape=[jax.ShapeDtypeStruct(shape, dtype) for shape, dtype in shapes],
        in_specs=[IN_VMEM] * 5,
        out_specs=[IN_VMEM] * len(shapes),
        name="deliver",
    )(o1, o2, o3, final_rows, start_rows)


def body(
    inputs, cotangent, lengths, attn_gain, w_query, w_key, w_value, w_out, ffn_gain, w_up, w_down
):
    weights = (w_query, w_key, w_value, w_out, attn_gain, ffn_gain, w_up, w_down)
    made = deliver(*decoder(inputs[:, 0], cotangent[:, 0], lengths, weights))
    final_rows, start_rows, g_attn, g_query, g_key, g_value, g_out, g_ffn, g_up, g_down = made
    return (
        final_rows[:, None],
        start_rows[:, None],
        g_attn,
        g_query.reshape(32, D),
        g_key.reshape(32, HD),
        g_value.reshape(32, HD),
        g_out.reshape(32, D),
        g_ffn,
        g_up.reshape(32, FF),
        g_down.reshape(128, D),
    )


def solution(mesh):
    both_axes = P(("section", "dp"))
    both_rows = P(("section", "dp"), None)
    acts = P(None, "dp", None, None)
    outs = P(None, "dp", "section", None)
    weights = (both_axes, both_rows, both_rows, both_rows, both_rows, both_axes, both_rows, both_rows)
    return jax.shard_map(
        body,
        mesh=mesh,
        in_specs=(acts, acts, P(None, "dp")) + weights,
        out_specs=(outs, outs) + weights,
        check_vma=False,
    )
```
